1024 devices in a mesh: ctx: 64 (over y_hi, x, core), head: 16 (over z, y_lo).
Axes of the slice: x: 8, y: 8 (y_hi: 4, y_lo: 2; y = y_hi * 2 + y_lo), z: 8, core: 2. Of those that a mesh axis runs over, the one named last changes fastest.
Arguments:
- query_rows: bfloat16 [32768, 16, 128], P('ctx', 'head'), may hold values from -45 to 45
- key_rows: bfloat16 [32768, 16, 128], P('ctx', 'head'), may hold values from -7 to 7
- value_rows: bfloat16 [32768, 16, 128], P('ctx', 'head'), may hold values from -6 to 6
- out_grad: bfloat16 [32768, 16, 128], P('ctx', 'head'), may hold values from -6 to 6
- global_pos: int32 [256], replicated, may hold values from 0 to 32767, as said below
Outputs:
- attn_out: bfloat16 [32768, 16, 128], P('ctx', 'head')
- query_grad: float32 [32768, 16, 128], P('ctx', 'head')
- key_grad: float32 [32768, 16, 128], P('ctx', 'head')
- value_grad: float32 [32768, 16, 128], P('ctx', 'head')
The draws below stay inside these ranges and needn't reach their ends.
Inputs may be any that keep to these rules, and one draw needn't show every extreme that they name: `global_pos`: distinct positions; the aligned block of 512 positions that holds the most of them holds exactly 8, and the other blocks hold counts that differ by at most one.
All inputs are finite; a program needn't handle non-finite values.
Results may differ from the reference program's by a relative error of at most 0.03.
Values may be sent and summed in bfloat16 or wider, within the bound.
A program may use at most 64 MiB of HBM per device.

```python
import jax
import jax.numpy as jnp
from jax import lax

TOK_DEV = 512
H = 16
DH = 128
HALF = 512
G = 256
SEQ = 32768
GMAX = 8


def place_globals(key):
    base_key = jax.random.fold_in(key, 11)
    blocks = SEQ // TOK_DEV
    busiest = jax.random.randint(jax.random.fold_in(base_key, 1), (), 0, blocks)
    block_order = jax.random.permutation(jax.random.fold_in(base_key, 2), blocks - 1)
    serial = jnp.arange(G)
    beyond = jnp.maximum(serial - GMAX, 0)
    others = (busiest + 1 + block_order[beyond % (blocks - 1)]) % blocks
    owner_block = jnp.where(serial < GMAX, busiest, others)
    within = jnp.where(serial < GMAX, serial, beyond // (blocks - 1))

    def shuffle(number):
        return jax.random.permutation(jax.random.fold_in(base_key, 100 + number), TOK_DEV)
    shuffled = jax.vmap(shuffle)(jnp.arange(blocks))
    positions = owner_block * TOK_DEV + shuffled[owner_block, within]
    mixing = jax.random.permutation(jax.random.fold_in(base_key, 3), G)
    return positions[mixing].astype(jnp.int32)


def query_key_pair(key):
    base_key = jax.random.fold_in(key, 23)
    shape_all = (SEQ, H, DH)
    key_part = 1.6 * jnp.clip(jax.random.normal(jax.random.fold_in(base_key, 1), shape_all), -4.0, 4.0)
    query_part = 1.6 * jnp.clip(jax.random.normal(jax.random.fold_in(base_key, 2), shape_all), -4.0, 4.0)
    return (query_part, key_part)


def draw_query_rows(key, part):
    return query_key_pair(key)[0].astype(jnp.bfloat16)


def draw_key_rows(key, part):
    return query_key_pair(key)[1].astype(jnp.bfloat16)


def draw_global_pos(key, part):
    return place_globals(key)


def shard_levels(key, dims, shards, least, high):
    def one(position, blocks):
        steps = jax.random.uniform(jax.random.fold_in(jax.random.fold_in(key, 6), position), (blocks,), jnp.float32, least / len(shards), high / len(shards))
        return jnp.repeat(jnp.exp(steps), dims[position] // blocks).reshape((-1,) + (1,) * (len(dims) - position - 1))

    gain = one(*shards[0])
    for cut in shards[1:]:
        gain = gain * one(*cut)
    return gain


def gaussian(stream_key, shape, width, limit, shards=(), held_as=jnp.bfloat16):
    values = width * jax.random.normal(stream_key, shape, jnp.float32)
    if shards:
        values = values * shard_levels(stream_key, shape, shards, -0.22, 0.18)
    return jnp.clip(values, -limit, limit).astype(held_as)


def setup_inputs(seed: int = 0) -> dict:
    keys = jax.random.split(jax.random.key(seed), 6)
    return {
        "query_rows": draw_query_rows(jax.random.fold_in(keys[5], 71), 0),
        "key_rows": draw_key_rows(jax.random.fold_in(keys[5], 71), 0),
        "value_rows": gaussian(keys[2], (SEQ, H, DH), 1.0, 6.0, ((0, 64), (1, 16))),
        "out_grad": gaussian(keys[3], (SEQ, H, DH), 1.0, 6.0, ((0, 64), (1, 16))),
        "global_pos": draw_global_pos(jax.random.fold_in(keys[5], 71), 0),
    }


big_negative = -1e30


def head_scores(row_block, col_block, score_scale):
    return jnp.einsum("qhd,khd->hqk", row_block.astype(jnp.float32), col_block.astype(jnp.float32)) * score_scale


def heads_first(array):
    return jnp.transpose(array, (1, 0, 2))


def reference(query_rows, key_rows, value_rows, out_grad, global_pos):
    seq_rows = query_rows.shape[0]
    score_scale = DH ** -0.5
    block_rows = min(512, TOK_DEV)
    span_count = 1 + 2 * HALF // block_rows
    block_count = seq_rows // block_rows
    is_global = jnp.zeros((seq_rows,), dtype=bool).at[global_pos].set(True)
    excluded = jnp.pad(is_global, (HALF, HALF), constant_values=True)
    local_grad = jnp.where(is_global[:, None, None], jnp.zeros_like(out_grad), out_grad)
    pad_rows = ((HALF, HALF), (0, 0), (0, 0))
    key_pad = jnp.pad(key_rows, pad_rows)
    value_pad = jnp.pad(value_rows, pad_rows)
    global_keys = key_rows[global_pos]
    global_values = value_rows[global_pos]
    offsets = jnp.arange(block_rows)

    def one_block(running, number):
        grad_pad, key_grad_g, value_grad_g = running
        start_row = number * block_rows
        row_block = lax.dynamic_slice_in_dim(query_rows, start_row, block_rows, 0)
        grad_block = lax.dynamic_slice_in_dim(local_grad, start_row, block_rows, 0)
        key_sets = [(global_keys, global_values, None, 0)]
        for stretch in range(span_count):
            key_start = start_row + stretch * block_rows
            in_reach = jnp.abs(offsets[None, :] + stretch * block_rows - offsets[:, None] - HALF) <= HALF
            allowed = in_reach & jnp.logical_not(lax.dynamic_slice_in_dim(excluded, key_start, block_rows, 0))[None, :]
            key_sets.append((lax.dynamic_slice_in_dim(key_pad, key_start, block_rows, 0),
                             lax.dynamic_slice_in_dim(value_pad, key_start, block_rows, 0), allowed, key_start))
        logit_sets = []
        for key_block, value_block, allowed, key_start in key_sets:
            logits = head_scores(row_block, key_block, score_scale)
            if allowed is not None:
                logits = jnp.where(allowed[None], logits, big_negative)
            logit_sets.append(logits)
        row_max = logit_sets[0].max(axis=-1)
        for logits in logit_sets[1:]:
            row_max = jnp.maximum(row_max, logits.max(axis=-1))
        row_sum = jnp.zeros_like(row_max)
        for logits in logit_sets:
            row_sum = row_sum + jnp.sum(jnp.exp(logits - row_max[..., None]), axis=-1)
        log_sum = row_max + jnp.log(row_sum)
        local_out = jnp.zeros((block_rows, H, DH), jnp.float32)
        for (key_block, value_block, allowed, key_start), logits in zip(key_sets, logit_sets):
            weights = jnp.exp(logits - log_sum[..., None])
            rounded = lax.optimization_barrier(weights.astype(jnp.bfloat16)).astype(jnp.float32)
            local_out = local_out + jnp.einsum("hqk,khd->qhd", rounded, value_block.astype(jnp.float32))
        row_dot = jnp.sum(grad_block.astype(jnp.float32) * local_out, axis=-1).T
        query_part = jnp.zeros((block_rows, H, DH), jnp.float32)
        for (key_block, value_block, allowed, key_start), logits in zip(key_sets, logit_sets):
            weights = jnp.exp(logits - log_sum[..., None])
            rounded = lax.optimization_barrier(weights.astype(jnp.bfloat16)).astype(jnp.float32)
            grad_weights = jnp.einsum("qhd,khd->hqk", grad_block.astype(jnp.float32), value_block.astype(jnp.float32))
            grad_scores = weights * (grad_weights - row_dot[..., None])
            grad_scores = lax.optimization_barrier(grad_scores.astype(jnp.bfloat16)).astype(jnp.float32)
            query_part = query_part + score_scale * jnp.einsum("hqk,khd->qhd", grad_scores, key_block.astype(jnp.float32))
            key_part = score_scale * jnp.einsum("hqk,qhd->khd", grad_scores, row_block.astype(jnp.float32))
            value_part = jnp.einsum("hqk,qhd->khd", rounded, grad_block.astype(jnp.float32))
            if allowed is None:
                key_grad_g = key_grad_g + key_part
                value_grad_g = value_grad_g + value_part
            else:
                current = lax.dynamic_slice_in_dim(grad_pad, key_start, block_rows, 0)
                grad_pad = lax.dynamic_update_slice_in_dim(
                    grad_pad, current + jnp.stack([key_part, value_part], axis=1), key_start, 0)
        return (grad_pad, key_grad_g, value_grad_g), (local_out, query_part)

    start_state = (jnp.zeros((seq_rows + 2 * HALF, 2, H, DH), jnp.float32),
                   jnp.zeros((G, H, DH), jnp.float32), jnp.zeros((G, H, DH), jnp.float32))
    (grad_pad, key_grad_g, value_grad_g), (local_out, query_local) = lax.scan(
        one_block, start_state, jnp.arange(block_count))
    local_out = local_out.reshape(seq_rows, H, DH)
    query_local = query_local.reshape(seq_rows, H, DH)

    def global_head(operands):
        query_h, grad_h, key_h, value_h = operands
        logits = jnp.dot(query_h, key_h.T, preferred_element_type=jnp.float32) * score_scale
        row_max = jnp.max(logits, axis=-1)
        log_sum = row_max + jnp.log(jnp.sum(jnp.exp(logits - row_max[:, None]), axis=-1))
        weights = jnp.exp(logits - log_sum[:, None])
        out_h = jnp.dot(weights, value_h.astype(jnp.float32), precision=lax.Precision.HIGHEST)
        row_dot = jnp.sum(grad_h.astype(jnp.float32) * out_h, axis=-1)
        rounded = weights.astype(jnp.bfloat16)
        value_grad_h = jnp.dot(rounded.T, grad_h, preferred_element_type=jnp.float32)
        grad_weights = jnp.dot(grad_h, value_h.T, preferred_element_type=jnp.float32)
        grad_scores = (weights * (grad_weights - row_dot[:, None])).astype(jnp.bfloat16)
        query_grad_h = score_scale * jnp.dot(grad_scores, key_h, preferred_element_type=jnp.float32)
        key_grad_h = score_scale * jnp.dot(grad_scores.T, query_h, preferred_element_type=jnp.float32)
        return out_h, query_grad_h, key_grad_h, value_grad_h

    global_out, global_qgrad, key_from_global, value_from_global = lax.map(
        global_head, (heads_first(query_rows[global_pos]), heads_first(out_grad[global_pos]),
                      heads_first(key_rows), heads_first(value_rows)))
    attn_out = local_out.at[global_pos].set(heads_first(global_out)).astype(jnp.bfloat16)
    query_grad = query_local.at[global_pos].add(heads_first(global_qgrad))
    window = grad_pad[HALF:HALF + seq_rows]
    key_grad = (window[:, 0] + heads_first(key_from_global)).at[global_pos].add(key_grad_g)
    value_grad = (window[:, 1] + heads_first(value_from_global)).at[global_pos].add(value_grad_g)
    return attn_out, query_grad, key_grad, value_grad
```

```python
import functools

import jax
import jax.numpy as jnp
from jax import lax
from jax.experimental import pallas as pl
from jax.experimental.pallas import tpu as pltpu
from jax.sharding import PartitionSpec as P

MESH = pl.DeviceIdType.MESH
HALF = 512
TILE = 128
SLOTS = 4
ROWS = 16
NEG = -1e30
F32 = jnp.float32
BF16 = jnp.bfloat16
I32 = jnp.int32


def dot_nn(a, b):
    return lax.dot_general(a, b, (((1,), (0,)), ((), ())), preferred_element_type=F32)


def dot_nt(a, b):
    return lax.dot_general(a, b, (((1,), (1,)), ((), ())), preferred_element_type=F32)


def dot_tn(a, b):
    return lax.dot_general(a, b, (((0,), (0,)), ((), ())), preferred_element_type=F32)


def iota(shape, dim):
    return lax.broadcasted_iota(I32, shape, dim)


def one_hot(cond):
    return jnp.where(cond, 1.0, 0.0).astype(BF16)


def kernel(
    sizes,
    pos_col,
    pos_row,
    q_ref,
    k_ref,
    v_ref,
    do_ref,
    out_ref,
    dq_ref,
    dk_ref,
    dv_ref,
    kpad,
    vpad,
    lgrad,
    colbias,
    rowflag,
    pack,
    gx,
    gath,
    glob,
    p_scr,
    d_scr,
    m_scr,
    l_scr,
    o_scr,
    dkpad,
    dvpad,
    dkg,
    dvg,
    sg_scr,
    gw_scr,
    st_own,
    st_sib,
    st_x,
    st_xin,
    st_y,
    st_yin,
    dkown,
    dvown,
    z_own,
    z_sib,
    t_own,
    t_in,
    u_own,
    u_in,
    r_scr,
    rim_out,
    rim_in,
    send_sem,
    recv_sem,
):
    n, yn, xn, tok, count, width = sizes
    seq = n * tok
    scale = width**-0.5
    x_shift = xn.bit_length() - 1
    tok_shift = tok.bit_length() - 1
    window = tok + 2 * HALF
    span = TILE + 2 * HALF
    tiles = tok // TILE

    me = lax.axis_index("ctx")
    core = lax.rem(me, 2)
    xx = lax.rem(lax.div(me, 2), xn)
    yy = lax.div(me, 2 * xn)

    def ctx_id(y, x, c):
        return (y * xn + x) * 2 + c

    x_peers = [ctx_id(yy, lax.rem(xx + d, xn), core) for d in range(1, xn)]
    y_peers = [ctx_id(lax.rem(yy + e, yn), xx, core) for e in range(1, yn)]
    sibling = me + 1 - 2 * core
    right = lax.rem(me + 1, n)
    left = lax.rem(me + n - 1, n)
    greeted = x_peers + y_peers + [left, right]

    barrier = pltpu.get_barrier_semaphore()
    for peer in greeted:
        pl.semaphore_signal(barrier, inc=1, device_id={"ctx": peer}, device_id_type=MESH)

    copies = []

    def send(src, dst, peer):
        number = len(copies)
        copy = pltpu.make_async_remote_copy(
            src_ref=src,
            dst_ref=dst,
            send_sem=send_sem.at[number],
            recv_sem=recv_sem.at[number],
            device_id={"ctx": peer},
            device_id_type=MESH,
        )
        copy.start()
        copies.append(copy)
        return copy

    pos_c, pos_r = pos_col[...], pos_row[...]
    owner_c, owner_r = pos_c >> tok_shift, pos_r >> tok_shift
    local_c, local_r = pos_c & (tok - 1), pos_r & (tok - 1)
    same = owner_c == owner_r
    first, second = iota((count, count), 0), iota((count, count), 1)
    rank_c = jnp.sum(jnp.where(same & (second < first), 1.0, 0.0), axis=1, keepdims=True).astype(I32)
    rank_r = jnp.sum(jnp.where(same & (first < second), 1.0, 0.0), axis=0, keepdims=True).astype(I32)

    rho = iota((2 * ROWS, count), 0)
    slot_rank = ((rho >> 4) << 2) + (rho & 3)
    chosen = (owner_r == me) & (rank_r == slot_rank)
    slot_col = jnp.sum(jnp.where(chosen, (local_r + 1).astype(F32), 0.0), axis=1, keepdims=True).astype(I32) - 1
    array_of = (iota((2 * ROWS, tok), 0) >> 2) & 3
    at_slot = iota((2 * ROWS, tok), 1) == slot_col
    picked = jnp.zeros((2 * ROWS, width), F32)
    for a, rows_ref in enumerate((q_ref, k_ref, v_ref, do_ref)):
        picked = picked + dot_nn(one_hot(at_slot & (array_of == a)), rows_ref[...])
    pack[...] = picked.astype(BF16).reshape(2, ROWS, width)
    gx[0] = pack[...]

    pl.semaphore_wait(barrier, len(greeted))

    from_x = [send(pack, gx.at[d], x_peers[d - 1]) for d in range(1, xn)]
    halos = [
        send(k_ref, kpad.at[pl.ds(0, HALF)], right),
        send(k_ref, kpad.at[pl.ds(HALF + tok, HALF)], left),
        send(v_ref, vpad.at[pl.ds(0, HALF)], right),
        send(v_ref, vpad.at[pl.ds(HALF + tok, HALF)], left),
    ]

    kpad[pl.ds(HALF, tok)] = k_ref[...]
    vpad[pl.ds(HALF, tok)] = v_ref[...]
    dkpad[...] = jnp.zeros((window, width), F32)
    dvpad[...] = jnp.zeros((window, width), F32)
    for part in range(window // 512):
        reach = me * tok - HALF + part * 512 + iota((1, 512), 1)
        bias = jnp.min(jnp.where(pos_c == reach, NEG, 0.0), axis=0, keepdims=True)
        inside = (reach >= 0) & (reach < seq)
        colbias[:, pl.ds(part * 512, 512)] = jnp.where(inside, bias, NEG)
    row_pos = me * tok + iota((tok, 1), 0)
    flag = jnp.max(jnp.where(row_pos == pos_r, 1.0, 0.0), axis=1, keepdims=True)
    rowflag[...] = jnp.broadcast_to(flag, (tok, width))
    lgrad[...] = jnp.where(rowflag[...] > 0.5, 0.0, do_ref[...].astype(F32)).astype(BF16)

    for copy in from_x:
        copy.wait_recv()
    over = gx[0, 1].astype(F32)
    gath[0, 0, 0] = gx[0, 0]
    for d in range(1, xn):
        gath[0, 0, d] = gx[d, 0]
        over = over + gx[d, 1].astype(F32)
    gath[0, 0, xn] = over.astype(BF16)
    from_y = [send(gath.at[0, 0], gath.at[0, e], y_peers[e - 1]) for e in range(1, yn)]
    from_sib = [send(gath.at[0, 0], gath.at[1, 0], sibling)]

    for copy in halos:
        copy.wait_recv()

    lane = iota((TILE, TILE), 1)
    sub = iota((TILE, TILE), 0)
    low_bias = jnp.where(lane >= sub, 0.0, NEG)
    high_bias = jnp.where(lane <= sub, 0.0, NEG)

    def before(t, carry):
        start = pl.multiple_of(t * TILE, TILE)
        rows, keys = pl.ds(start, TILE), pl.ds(start, span)
        s = dot_nt(q_ref[rows, :], kpad[keys, :]) * scale + colbias[:, keys]
        s = jnp.concatenate(
            [s[:, :TILE] + low_bias, s[:, TILE : 2 * HALF], s[:, 2 * HALF :] + high_bias], axis=1
        )
        top = jnp.max(s, axis=1, keepdims=True)
        p = jnp.exp(s - top)
        p_scr[rows, :] = p
        m_scr[rows, :] = jnp.broadcast_to(top, (TILE, width))
        l_scr[rows, :] = jnp.broadcast_to(jnp.sum(p, axis=1, keepdims=True), (TILE, width))
        d_scr[rows, :] = dot_nt(lgrad[rows, :], vpad[keys, :])
        return carry

    lax.fori_loop(0, tiles, before, 0)

    for e in range(1, yn):
        from_y[e - 1].wait_recv()
        from_sib.append(send(gath.at[0, e], gath.at[1, e], sibling))

    core_c, xo_c, yo_c = owner_c & 1, (owner_c >> 1) & (xn - 1), owner_c >> (1 + x_shift)
    half_c = (core_c ^ core) * yn + ((yy - yo_c) & (yn - 1))
    src_c = jnp.where(
        rank_c < SLOTS,
        (half_c * (xn + 1) + ((xx - xo_c) & (xn - 1))) * ROWS + rank_c,
        (half_c * (xn + 1) + xn) * ROWS + rank_c - SLOTS,
    )
    total = 2 * yn * (xn + 1) * ROWS
    for copy in from_sib:
        copy.wait_recv()
    everything = gath[...].reshape(total, width)
    for a in range(4):
        hot = one_hot(iota((count, total), 1) == src_c + SLOTS * a)
        glob[a] = dot_nn(hot, everything).astype(BF16)

    sg = dot_nt(k_ref[...], glob[0]) * scale
    gw = dot_nt(v_ref[...], glob[3])
    sg_scr[...] = sg
    gw_scr[...] = gw
    top = jnp.max(sg, axis=0, keepdims=True)
    p = jnp.exp(sg - top)
    stat_rows = [top, jnp.sum(p, axis=0, keepdims=True), jnp.sum(p * gw, axis=0, keepdims=True)]
    for r, row in enumerate(stat_rows):
        st_own[2 * r : 2 * r + 1, :] = row[:, :TILE]
        st_own[2 * r + 1 : 2 * r + 2, :] = row[:, TILE:]
    st_own[6:8, :] = jnp.zeros((2, TILE), F32)

    def join(parts):
        joined = functools.reduce(jnp.maximum, [part[0:2, :] for part in parts])
        weigh = [jnp.exp(part[0:2, :] - joined) for part in parts]
        return (
            joined,
            sum(part[2:4, :] * w for part, w in zip(parts, weigh)),
            sum(part[4:6, :] * w for part, w in zip(parts, weigh)),
        )

    def store(ref, stats):
        for r, part in enumerate(stats):
            ref[2 * r : 2 * r + 2, :] = part
        ref[6:8, :] = jnp.zeros((2, TILE), F32)

    stat_sib = send(st_own, st_sib, sibling)

    dkg[...] = jnp.zeros((count, width), F32)
    dvg[...] = jnp.zeros((count, width), F32)

    def after(t, carry):
        start = pl.multiple_of(t * TILE, TILE)
        rows, keys = pl.ds(start, TILE), pl.ds(start, span)
        q, lg = q_ref[rows, :], lgrad[rows, :]
        kw, vw = kpad[keys, :], vpad[keys, :]
        s = dot_nt(q, glob[1]) * scale
        top_w = m_scr[rows, 0:1]
        top = jnp.maximum(top_w, jnp.max(s, axis=1, keepdims=True))
        pg = jnp.exp(s - top)
        down = jnp.exp(top_w - top)
        inv = 1.0 / (l_scr[rows, 0:1] * down + jnp.sum(pg, axis=1, keepdims=True))
        pw = p_scr[rows, :] * (down * inv)
        pg = pg * inv
        pw16, pg16 = pw.astype(BF16), pg.astype(BF16)
        o = dot_nn(pw16, vw) + dot_nn(pg16, glob[2])
        o_scr[rows, :] = o
        row_dot = jnp.sum(lg.astype(F32) * o, axis=1, keepdims=True)
        dsw = (pw * (d_scr[rows, :] - row_dot)).astype(BF16)
        dsg = (pg * (dot_nt(lg, glob[2]) - row_dot)).astype(BF16)
        dq_ref[rows, :] = (dot_nn(dsw, kw) + dot_nn(dsg, glob[1])) * scale
        dkpad[keys, :] += dot_tn(dsw, q)
        dvpad[keys, :] += dot_tn(pw16, lg)
        dkg[...] += dot_tn(dsg, q)
        dvg[...] += dot_tn(pg16, lg)
        return carry

    first_stop, second_stop = tiles // 4, 3 * tiles // 4
    lax.fori_loop(0, first_stop, after, 0)
    stat_sib.wait_recv()
    store(st_x, join([st_own[...], st_sib[...]]))
    stat_x = [send(st_x, st_xin.at[d - 1], x_peers[d - 1]) for d in range(1, xn)]
    lax.fori_loop(first_stop, second_stop, after, 0)
    for copy in stat_x:
        copy.wait_recv()
    store(st_y, join([st_x[...]] + [st_xin[d - 1] for d in range(1, xn)]))
    stat_y = [send(st_y, st_yin.at[e - 1], y_peers[e - 1]) for e in range(1, yn)]
    lax.fori_loop(second_stop, tiles, after, 0)

    rim_out[0, 0] = dkpad[pl.ds(0, HALF), :].astype(BF16)
    rim_out[0, 1] = dvpad[pl.ds(0, HALF), :].astype(BF16)
    rim_out[1, 0] = dkpad[pl.ds(HALF + tok, HALF), :].astype(BF16)
    rim_out[1, 1] = dvpad[pl.ds(HALF + tok, HALF), :].astype(BF16)

    for copy in stat_y:
        copy.wait_recv()
    joined, summed, dotted = join([st_y[...]] + [st_yin[e - 1] for e in range(1, yn)])
    lse = joined + jnp.log(summed)
    ratio = dotted / summed
    lse = jnp.concatenate([lse[0:1], lse[1:2]], axis=1)
    ratio = jnp.concatenate([ratio[0:1], ratio[1:2]], axis=1)

    w = jnp.exp(sg_scr[...] - lse)
    w16 = w.astype(BF16)
    ds16 = (w * (gw_scr[...] - ratio)).astype(BF16)
    partial = (
        dot_tn(w16, v_ref[...]).astype(BF16),
        dot_tn(ds16, k_ref[...]).astype(BF16),
        dkg[...].astype(BF16),
        dvg[...].astype(BF16),
    )

    core_r, xo_r, yo_r = owner_r & 1, (owner_r >> 1) & (xn - 1), owner_r >> (1 + x_shift)
    regular = xn * yn * ROWS
    order = ((xo_r - xx) & (xn - 1)) * yn + ((yo_r - yy) & (yn - 1))
    extra = 4 * regular
    key_r = jnp.where(
        rank_r < SLOTS, (core_r ^ core) * regular + order * ROWS + rank_r, extra + rank_r - SLOTS
    )
    half_rows = regular + ROWS
    for half in range(2):
        row = iota((half_rows, count), 0)
        key = jnp.where(row < regular, row + half * regular, row - regular + extra)
        z = jnp.zeros((half_rows, width), F32)
        for a in range(4):
            z = z + dot_nn(one_hot(key == key_r + SLOTS * a), partial[a])
        z_own[half] = z.astype(BF16).reshape(xn * yn + 1, ROWS, width)
    z_copy = send(z_own.at[1], z_sib, sibling)
    rims = [send(rim_out.at[1], rim_in.at[0], right), send(rim_out.at[0], rim_in.at[1], left)]

    dvown[...] = dot_nn(w16, glob[3])
    dkown[...] = dot_nn(ds16, glob[0])

    z_copy.wait_recv()
    both = z_own[0].astype(F32) + z_sib[...].astype(F32)
    for d in range(xn):
        t_own[d, 0:yn] = both[d * yn : (d + 1) * yn].astype(BF16)
        t_own[d, yn] = both[xn * yn].astype(BF16)
    t_copies = [send(t_own.at[d], t_in.at[d - 1], x_peers[d - 1]) for d in range(1, xn)]
    for copy in t_copies:
        copy.wait_recv()
    column = t_own[0].astype(F32)
    for d in range(1, xn):
        column = column + t_in[d - 1].astype(F32)
    for e in range(yn):
        u_own[e, 0] = column[e].astype(BF16)
        u_own[e, 1] = column[yn].astype(BF16)
    u_copies = [send(u_own.at[e], u_in.at[e - 1], y_peers[e - 1]) for e in range(1, yn)]

    for copy in rims:
        copy.wait_recv()
    dk_sum = dkpad[pl.ds(HALF, tok), :] + dkown[...]
    dv_sum = dvpad[pl.ds(HALF, tok), :] + dvown[...]
    for side in range(2):
        dk_sum = dk_sum + rim_in[side, 0].astype(F32)
        dv_sum = dv_sum + rim_in[side, 1].astype(F32)
    dkown[...] = dk_sum
    dvown[...] = dv_sum

    rho_lane = iota((count, TILE), 1)
    lane_rank = ((rho_lane >> 4) << 2) + (rho_lane & 3)
    chosen_c = (owner_c == me) & (rank_c == lane_rank) & (rho_lane < 2 * ROWS)
    slot_row = jnp.sum(jnp.where(chosen_c, (local_c + 1).astype(F32), 0.0), axis=0, keepdims=True).astype(I32) - 1
    lane_array = (iota((tok, TILE), 1) >> 2) & 3
    row_here = iota((tok, TILE), 0) == slot_row

    for copy in u_copies:
        copy.wait_recv()
    own = u_own[0].astype(F32)
    for e in range(1, yn):
        own = own + u_in[e - 1].astype(F32)
    r_scr[...] = jnp.zeros((TILE, width), F32)
    r_scr[0 : 2 * ROWS, :] = own.reshape(2 * ROWS, width)
    upper = r_scr[...].astype(BF16)
    lower = (r_scr[...] - upper.astype(F32)).astype(BF16)

    def placed(a):
        hot = one_hot(row_here & (lane_array == a))
        return dot_nn(hot, upper) + dot_nn(hot, lower)

    out_ref[...] = jnp.where(rowflag[...] > 0.5, placed(0), o_scr[...]).astype(BF16)
    dq_ref[...] = dq_ref[...] + placed(1) * scale
    dk_ref[...] = (dkown[...] + placed(2)) * scale
    dv_ref[...] = dvown[...] + placed(3)

    for copy in copies:
        copy.wait_send()


def shards(n, query_rows, key_rows, value_rows, out_grad, global_pos):
    tok, _, width = query_rows.shape
    count = global_pos.shape[0]
    yn = 4
    xn = n // (2 * yn)
    window = tok + 2 * HALF
    span = TILE + 2 * HALF
    copies = 4 * (xn - 1) + 4 * (yn - 1) + 16
    vmem = pl.BlockSpec(memory_space=pltpu.VMEM)
    flat = [x.reshape(tok, width) for x in (query_rows, key_rows, value_rows, out_grad)]
    results = pl.pallas_call(
        functools.partial(kernel, (n, yn, xn, tok, count, width)),
        name="sparse_attention",
        out_shape=(
            jax.ShapeDtypeStruct((tok, width), BF16),
            jax.ShapeDtypeStruct((tok, width), F32),
            jax.ShapeDtypeStruct((tok, width), F32),
            jax.ShapeDtypeStruct((tok, width), F32),
        ),
        in_specs=[vmem] * 6,
        out_specs=(vmem,) * 4,
        scratch_shapes=[
            pltpu.VMEM((window, width), BF16),
            pltpu.VMEM((window, width), BF16),
            pltpu.VMEM((tok, width), BF16),
            pltpu.VMEM((1, window), F32),
            pltpu.VMEM((tok, width), F32),
            pltpu.VMEM((2, ROWS, width), BF16),
            pltpu.VMEM((xn, 2, ROWS, width), BF16),
            pltpu.VMEM((2, yn, xn + 1, ROWS, width), BF16),
            pltpu.VMEM((4, count, width), BF16),
            pltpu.VMEM((tok, span), F32),
            pltpu.VMEM((tok, span), F32),
            pltpu.VMEM((tok, width), F32),
            pltpu.VMEM((tok, width), F32),
            pltpu.VMEM((tok, width), F32),
            pltpu.VMEM((window, width), F32),
            pltpu.VMEM((window, width), F32),
            pltpu.VMEM((count, width), F32),
            pltpu.VMEM((count, width), F32),
            pltpu.VMEM((tok, count), F32),
            pltpu.VMEM((tok, count), F32),
            pltpu.VMEM((8, TILE), F32),
            pltpu.VMEM((8, TILE), F32),
            pltpu.VMEM((8, TILE), F32),
            pltpu.VMEM((xn - 1, 8, TILE), F32),
            pltpu.VMEM((8, TILE), F32),
            pltpu.VMEM((yn - 1, 8, TILE), F32),
            pltpu.VMEM((tok, width), F32),
            pltpu.VMEM((tok, width), F32),
            pltpu.VMEM((2, xn * yn + 1, ROWS, width), BF16),
            pltpu.VMEM((xn * yn + 1, ROWS, width), BF16),
            pltpu.VMEM((xn, yn + 1, ROWS, width), BF16),
            pltpu.VMEM((xn - 1, yn + 1, ROWS, width), BF16),
            pltpu.VMEM((yn, 2, ROWS, width), BF16),
            pltpu.VMEM((yn - 1, 2, ROWS, width), BF16),
            pltpu.VMEM((TILE, width), F32),
            pltpu.VMEM((2, 2, HALF, width), BF16),
            pltpu.VMEM((2, 2, HALF, width), BF16),
            pltpu.SemaphoreType.DMA((copies,)),
            pltpu.SemaphoreType.DMA((copies,)),
        ],
        compiler_params=pltpu.CompilerParams(collective_id=0, has_side_effects=True),
    )(global_pos.reshape(count, 1), global_pos.reshape(1, count), *flat)
    return tuple(x.reshape(tok, 1, width) for x in results)


def solution(mesh):
    rows = P("ctx", "head", None)
    return jax.shard_map(
        functools.partial(shards, mesh.shape["ctx"]),
        mesh=mesh,
        in_specs=(rows,) * 4 + (P(),),
        out_specs=(rows,) * 4,
        check_vma=False,
    )
```

```python
import functools

import jax
import jax.numpy as jnp
from jax import lax
from jax.experimental import pallas as pl
from jax.experimental.pallas import tpu as pltpu
from jax.sharding import PartitionSpec as P

MESH = pl.DeviceIdType.MESH
HALF = 512
TILE = 128
SLOTS = 4
ROWS = 16
NEG = -1e30
F32 = jnp.float32
BF16 = jnp.bfloat16
I32 = jnp.int32


def dot_nn(a, b):
    return lax.dot_general(a, b, (((1,), (0,)), ((), ())), preferred_element_type=F32)


def dot_nt(a, b):
    return lax.dot_general(a, b, (((1,), (1,)), ((), ())), preferred_element_type=F32)


def dot_tn(a, b):
    return lax.dot_general(a, b, (((0,), (0,)), ((), ())), preferred_element_type=F32)


def iota(shape, dim):
    return lax.broadcasted_iota(I32, shape, dim)


def one_hot(cond):
    return jnp.where(cond, 1.0, 0.0).astype(BF16)


def kernel(
    sizes,
    pos_hbm,
    q_hbm,
    k_hbm,
    v_hbm,
    do_hbm,
    o_out,
    dq_out,
    dk_out,
    dv_out,
    hot_out,
    flag_out,
    r_out,
    pos_scr,
    q_ref,
    do_ref,
    kpad,
    vpad,
    lgrad,
    colbias,
    rowflag,
    pack,
    gx,
    gath,
    pick,
    glob,
    p_scr,
    d_scr,
    m_scr,
    l_scr,
    o_scr,
    dq_scr,
    dkpad,
    dvpad,
    dkg,
    dvg,
    sg_scr,
    gw_scr,
    st_own,
    st_sib,
    st_x,
    st_xin,
    st_y,
    st_yin,
    dkown,
    dvown,
    spread,
    spread_over,
    hot_scr,
    z_own,
    z_sib,
    t_own,
    t_in,
    u_own,
    u_in,
    r_scr,
    rim_out,
    rim_in,
    send_sem,
    recv_sem,
    load_sem,
    store_sem,
):
    n, yn, xn, tok, count, width = sizes
    seq = n * tok
    scale = width**-0.5
    x_shift = xn.bit_length() - 1
    tok_shift = tok.bit_length() - 1
    window = tok + 2 * HALF
    span = TILE + 2 * HALF
    tiles = tok // TILE
    own = pl.ds(HALF, tok)

    me = lax.axis_index("ctx")
    core = lax.rem(me, 2)
    xx = lax.rem(lax.div(me, 2), xn)
    yy = lax.div(me, 2 * xn)

    def ctx_id(y, x, c):
        return (y * xn + x) * 2 + c

    x_peers = [ctx_id(yy, lax.rem(xx + d, xn), core) for d in range(1, xn)]
    y_peers = [ctx_id(lax.rem(yy + e, yn), xx, core) for e in range(1, yn)]
    sibling = me + 1 - 2 * core
    right = lax.rem(me + 1, n)
    left = lax.rem(me + n - 1, n)
    greeted = x_peers + y_peers + [left, right]

    barrier = pltpu.get_barrier_semaphore()
    for peer in greeted:
        pl.semaphore_signal(barrier, inc=1, device_id={"ctx": peer}, device_id_type=MESH)

    loads = [
        pltpu.make_async_copy(src, dst, load_sem.at[i])
        for i, (src, dst) in enumerate(
            (
                (pos_hbm, pos_scr),
                (q_hbm, q_ref),
                (k_hbm, kpad.at[own]),
                (v_hbm, vpad.at[own]),
                (do_hbm, do_ref),
            )
        )
    ]
    for load in loads:
        load.start()

    copies = []

    def send(src, dst, peer):
        number = len(copies)
        copy = pltpu.make_async_remote_copy(
            src_ref=src,
            dst_ref=dst,
            send_sem=send_sem.at[number],
            recv_sem=recv_sem.at[number],
            device_id={"ctx": peer},
            device_id_type=MESH,
        )
        copy.start()
        copies.append(copy)
        return copy

    stores = []

    def keep(src, dst):
        copy = pltpu.make_async_copy(src, dst, store_sem.at[len(stores)])
        copy.start()
        stores.append(copy)

    loads[0].wait()
    pos_r = pos_scr[...]
    first, second = iota((count, count), 0), iota((count, count), 1)
    pos_c = jnp.sum(jnp.where(first == second, pos_r.astype(F32), 0.0), axis=1, keepdims=True).astype(I32)
    owner_c, owner_r = pos_c >> tok_shift, pos_r >> tok_shift
    local_c, local_r = pos_c & (tok - 1), pos_r & (tok - 1)
    same = owner_c == owner_r
    rank_c = jnp.sum(jnp.where(same & (second < first), 1.0, 0.0), axis=1, keepdims=True).astype(I32)
    rank_r = jnp.sum(jnp.where(same & (first < second), 1.0, 0.0), axis=0, keepdims=True).astype(I32)

    rho = iota((2 * ROWS, count), 0)
    slot_rank = ((rho >> 4) << 2) + (rho & 3)
    chosen = (owner_r == me) & (rank_r == slot_rank)
    slot_col = jnp.sum(jnp.where(chosen, (local_r + 1).astype(F32), 0.0), axis=1, keepdims=True).astype(I32) - 1
    array_of = (iota((2 * ROWS, tok), 0) >> 2) & 3
    at_slot = iota((2 * ROWS, tok), 1) == slot_col
    picked = jnp.zeros((2 * ROWS, width), F32)
    for load in loads[1:]:
        load.wait()
    for a, rows in enumerate((q_ref[...], kpad[own, :], vpad[own, :], do_ref[...])):
        picked = picked + dot_nn(one_hot(at_slot & (array_of == a)), rows)
    pack[...] = picked.astype(BF16).reshape(2, ROWS, width)
    gx[0] = pack[...]

    pl.semaphore_wait(barrier, len(greeted))

    from_x = [send(pack, gx.at[d], x_peers[d - 1]) for d in range(1, xn)]
    halos = [
        send(kpad.at[own], kpad.at[pl.ds(0, HALF)], right),
        send(kpad.at[own], kpad.at[pl.ds(HALF + tok, HALF)], left),
        send(vpad.at[own], vpad.at[pl.ds(0, HALF)], right),
        send(vpad.at[own], vpad.at[pl.ds(HALF + tok, HALF)], left),
    ]

    dkpad[...] = jnp.zeros((window, width), F32)
    dvpad[...] = jnp.zeros((window, width), F32)
    for part in range(window // 512):
        reach = me * tok - HALF + part * 512 + iota((1, 512), 1)
        bias = jnp.min(jnp.where(pos_c == reach, NEG, 0.0), axis=0, keepdims=True)
        inside = (reach >= 0) & (reach < seq)
        colbias[:, pl.ds(part * 512, 512)] = jnp.where(inside, bias, NEG)
    row_pos = me * tok + iota((tok, 1), 0)
    flag = jnp.max(jnp.where(row_pos == pos_r, 1.0, 0.0), axis=1, keepdims=True)
    rowflag[...] = jnp.broadcast_to(flag, (tok, width))
    lgrad[...] = jnp.where(rowflag[...] > 0.5, 0.0, do_ref[...].astype(F32)).astype(BF16)

    for copy in from_x:
        copy.wait_recv()
    over = gx[0, 1].astype(F32)
    gath[0, 0, 0] = gx[0, 0]
    for d in range(1, xn):
        gath[0, 0, d] = gx[d, 0]
        over = over + gx[d, 1].astype(F32)
    gath[0, 0, xn] = over.astype(BF16)
    from_y = [send(gath.at[0, 0], gath.at[0, e], y_peers[e - 1]) for e in range(1, yn)]
    from_sib = [send(gath.at[0, 0], gath.at[1, 0], sibling)]

    core_c, xo_c, yo_c = owner_c & 1, (owner_c >> 1) & (xn - 1), owner_c >> (1 + x_shift)
    half_c = (core_c ^ core) * yn + ((yy - yo_c) & (yn - 1))
    src_c = jnp.where(
        rank_c < SLOTS,
        (half_c * (xn + 1) + ((xx - xo_c) & (xn - 1))) * ROWS + rank_c,
        (half_c * (xn + 1) + xn) * ROWS + rank_c - SLOTS,
    )
    total = 2 * yn * (xn + 1) * ROWS
    for a in range(4):
        pick[a] = one_hot(iota((count, total), 1) == src_c + SLOTS * a)

    core_r, xo_r, yo_r = owner_r & 1, (owner_r >> 1) & (xn - 1), owner_r >> (1 + x_shift)
    place = ((core_r ^ core) * xn + ((xo_r - xx) & (xn - 1))) * yn + ((yo_r - yy) & (yn - 1))
    beyond = 2 * xn * yn * SLOTS
    key_r = jnp.where(rank_r < SLOTS, place * SLOTS + rank_r, beyond + rank_r - SLOTS)
    spread[...] = one_hot(iota((beyond, count), 0) == key_r)
    over_row = iota((2 * ROWS, count), 0)
    spread_over[...] = jnp.where(beyond + (over_row & 3) == key_r, 1.0, 0.0)

    rho_lane = iota((count, TILE), 1)
    lane_rank = ((rho_lane >> 4) << 2) + (rho_lane & 3)
    chosen_c = (owner_c == me) & (rank_c == lane_rank) & (rho_lane < 2 * ROWS)
    slot_row = jnp.sum(jnp.where(chosen_c, (local_c + 1).astype(F32), 0.0), axis=0, keepdims=True).astype(I32) - 1
    hot_scr[...] = one_hot(iota((tok, TILE), 0) == slot_row)
    keep(hot_scr, hot_out)
    keep(rowflag, flag_out)

    for copy in halos:
        copy.wait_recv()

    lane = iota((TILE, TILE), 1)
    sub = iota((TILE, TILE), 0)
    low_bias = jnp.where(lane >= sub, 0.0, NEG)
    high_bias = jnp.where(lane <= sub, 0.0, NEG)

    def before(t, carry):
        start = pl.multiple_of(t * TILE, TILE)
        rows, keys = pl.ds(start, TILE), pl.ds(start, span)
        s = dot_nt(q_ref[rows, :], kpad[keys, :]) * scale + colbias[:, keys]
        s = jnp.concatenate(
            [s[:, :TILE] + low_bias, s[:, TILE : 2 * HALF], s[:, 2 * HALF :] + high_bias], axis=1
        )
        top = jnp.max(s, axis=1, keepdims=True)
        p = jnp.exp(s - top)
        p_scr[rows, :] = p
        m_scr[rows, :] = jnp.broadcast_to(top, (TILE, width))
        l_scr[rows, :] = jnp.broadcast_to(jnp.sum(p, axis=1, keepdims=True), (TILE, width))
        d_scr[rows, :] = dot_nt(lgrad[rows, :], vpad[keys, :])
        return carry

    lax.fori_loop(0, tiles, before, 0)

    for e in range(1, yn):
        from_y[e - 1].wait_recv()
        from_sib.append(send(gath.at[0, e], gath.at[1, e], sibling))
    for copy in from_sib:
        copy.wait_recv()
    everything = gath[...].reshape(total, width)
    for a in range(4):
        glob[a] = dot_nn(pick[a], everything).astype(BF16)

    middle = (jnp.sum(glob[2].astype(F32), axis=0, keepdims=True) * (1.0 / count)).astype(BF16)
    centre = dot_nt(jnp.broadcast_to(middle, (ROWS, width)), glob[3])[0:1, :]
    sg = dot_nt(kpad[own, :], glob[0]) * scale
    gw = dot_nt(vpad[own, :], glob[3]) - centre
    sg_scr[...] = sg
    gw_scr[...] = gw
    top = jnp.max(sg, axis=0, keepdims=True)
    p = jnp.exp(sg - top)
    stat_rows = [top, jnp.sum(p, axis=0, keepdims=True), jnp.sum(p * gw, axis=0, keepdims=True)]
    for r, row in enumerate(stat_rows):
        st_own[2 * r : 2 * r + 1, :] = row[:, :TILE]
        st_own[2 * r + 1 : 2 * r + 2, :] = row[:, TILE:]
    st_own[6:8, :] = jnp.zeros((2, TILE), F32)

    def join(parts):
        joined = functools.reduce(jnp.maximum, [part[0:2, :] for part in parts])
        weigh = [jnp.exp(part[0:2, :] - joined) for part in parts]
        return (
            joined,
            sum(part[2:4, :] * w for part, w in zip(parts, weigh)),
            sum(part[4:6, :] * w for part, w in zip(parts, weigh)),
        )

    def store(ref, stats):
        for r, part in enumerate(stats):
            ref[2 * r : 2 * r + 2, :] = part
        ref[6:8, :] = jnp.zeros((2, TILE), F32)

    def row_of(part):
        return jnp.concatenate([part[0:1], part[1:2]], axis=1)

    stat_sib = send(st_own, st_sib, sibling)

    dkg[...] = jnp.zeros((count, width), F32)
    dvg[...] = jnp.zeros((count, width), F32)

    def after(t, carry):
        start = pl.multiple_of(t * TILE, TILE)
        rows, keys = pl.ds(start, TILE), pl.ds(start, span)
        q, lg = q_ref[rows, :], lgrad[rows, :]
        kw, vw = kpad[keys, :], vpad[keys, :]
        s = dot_nt(q, glob[1]) * scale
        top_w = m_scr[rows, 0:1]
        top = jnp.maximum(top_w, jnp.max(s, axis=1, keepdims=True))
        pg = jnp.exp(s - top)
        down = jnp.exp(top_w - top)
        inv = 1.0 / (l_scr[rows, 0:1] * down + jnp.sum(pg, axis=1, keepdims=True))
        pw = p_scr[rows, :] * (down * inv)
        pg = pg * inv
        pw16, pg16 = pw.astype(BF16), pg.astype(BF16)
        o = dot_nn(pw16, vw) + dot_nn(pg16, glob[2])
        o_scr[rows, :] = o
        row_dot = jnp.sum(lg.astype(F32) * o, axis=1, keepdims=True)
        dsw = (pw * (d_scr[rows, :] - row_dot)).astype(BF16)
        dsg = (pg * (dot_nt(lg, glob[2]) - row_dot)).astype(BF16)
        dq_scr[rows, :] = (dot_nn(dsw, kw) + dot_nn(dsg, glob[1])) * scale
        dkpad[keys, :] += dot_tn(dsw, q)
        dvpad[keys, :] += dot_tn(pw16, lg)
        dkg[...] += dot_tn(dsg, q)
        dvg[...] += dot_tn(pg16, lg)
        return carry

    lax.fori_loop(0, 1, after, 0)
    stat_sib.wait_recv()
    store(st_x, join([st_own[...], st_sib[...]]))
    stat_x = [send(st_x, st_xin.at[d - 1], x_peers[d - 1]) for d in range(1, xn)]
    lax.fori_loop(1, tiles, after, 0)

    rim_out[0, 0] = dkpad[pl.ds(0, HALF), :].astype(BF16)
    rim_out[0, 1] = dvpad[pl.ds(0, HALF), :].astype(BF16)
    rim_out[1, 0] = dkpad[pl.ds(HALF + tok, HALF), :].astype(BF16)
    rim_out[1, 1] = dvpad[pl.ds(HALF + tok, HALF), :].astype(BF16)
    rims = [send(rim_out.at[1], rim_in.at[0], right), send(rim_out.at[0], rim_in.at[1], left)]
    keep(o_scr, o_out)
    keep(dq_scr, dq_out)

    pair_top = st_x[0:2, :]
    w = jnp.exp(sg_scr[...] - row_of(pair_top))
    w16 = w.astype(BF16)
    ds16 = (w * gw_scr[...]).astype(BF16)
    value_key = dot_tn(w16, jnp.concatenate([vpad[own, :], kpad[own, :]], axis=1))
    partial = jnp.concatenate(
        [
            value_key[:, :width],
            dot_tn(ds16, kpad[own, :]),
            value_key[:, width:],
            dkg[...],
            dvg[...],
        ],
        axis=1,
    ).astype(BF16)
    z = dot_nn(spread[...], partial).astype(BF16)
    z_over = jnp.zeros((2 * ROWS, width), F32)
    for a in range(5):
        mine = jnp.where((over_row >> 2) == a, spread_over[...], 0.0).astype(BF16)
        z_over = z_over + dot_nn(mine, partial[:, a * width : (a + 1) * width])
    z_over = z_over.astype(BF16).reshape(2, ROWS, width)
    for half in range(2):
        for d in range(xn):
            base = (half * xn + d) * ROWS
            for a in range(5):
                z_own[half, d * 5 + a] = z[base : base + ROWS, a * width : (a + 1) * width]
        z_own[half, 5 * xn : 5 * xn + 2] = z_over
    z_copy = send(z_own.at[1], z_sib, sibling)

    for copy in stat_x:
        copy.wait_recv()
    store(st_y, join([st_x[...]] + [st_xin[d - 1] for d in range(1, xn)]))
    stat_y = [send(st_y, st_yin.at[e - 1], y_peers[e - 1]) for e in range(1, yn)]
    row_top = st_y[0:2, :]
    fall = row_of(jnp.exp(pair_top - row_top))
    column_key = iota((xn * ROWS, count), 0)
    fall_c = jnp.sum(jnp.where(column_key == key_r, fall, 0.0), axis=1, keepdims=True)
    over_kind = iota((2 * ROWS, 1), 0) >> 2
    fall_o = jnp.sum(spread_over[...] * fall, axis=1, keepdims=True)
    fall_o = jnp.where(over_kind < 3, fall_o, 1.0)

    z_copy.wait_recv()
    over = z_own[0, 5 * xn : 5 * xn + 2].astype(F32) + z_sib[5 * xn : 5 * xn + 2].astype(F32)
    over = (over.reshape(2 * ROWS, width) * fall_o).astype(BF16).reshape(2, ROWS, width)
    for d in range(xn):
        both = z_own[0, d * 5 : d * 5 + 5].astype(F32) + z_sib[d * 5 : d * 5 + 5].astype(F32)
        down = fall_c[d * ROWS : (d + 1) * ROWS]
        for a in range(5):
            t_own[d, a] = (both[a] * down if a < 3 else both[a]).astype(BF16)
        t_own[d, 5:7] = over
    t_copies = [send(t_own.at[d], t_in.at[d - 1], x_peers[d - 1]) for d in range(1, xn)]

    for copy in stat_y:
        copy.wait_recv()
    joined, summed, dotted = join([st_y[...]] + [st_yin[e - 1] for e in range(1, yn)])
    lse = row_of(joined + jnp.log(summed))
    ratio = row_of(dotted / summed)
    fall = row_of(jnp.exp(row_top - joined) / summed)
    places = 7 * ROWS
    line = iota((places, count), 0)
    line_key = jnp.where(line < 5 * ROWS, line & (ROWS - 1), beyond + (line & 3))
    line_c = iota((places, 1), 0)
    kind = jnp.where(line_c < 5 * ROWS, line_c >> 4, (line_c - 5 * ROWS) >> 2)
    found = jnp.where(line_key == key_r, 1.0, 0.0)
    plain = jnp.sum(found * fall, axis=1, keepdims=True)
    moved = jnp.sum(found * (fall * ratio), axis=1, keepdims=True)
    factor = jnp.where(kind < 2, plain, jnp.where(kind == 2, -moved, 1.0))

    w = jnp.exp(sg_scr[...] - lse)
    dvown[...] = dot_nn(w.astype(BF16), glob[3])
    dkown[...] = dot_nn((w * (gw_scr[...] - ratio)).astype(BF16), glob[0])
    for copy in rims:
        copy.wait_recv()
    dk_sum = dkpad[own, :] + dkown[...]
    dv_sum = dvpad[own, :] + dvown[...]
    for side in range(2):
        dk_sum = dk_sum + rim_in[side, 0].astype(F32)
        dv_sum = dv_sum + rim_in[side, 1].astype(F32)
    dkown[...] = dk_sum * scale
    dvown[...] = dv_sum
    keep(dkown, dk_out)
    keep(dvown, dv_out)

    outs = (yn + 1) * ROWS
    goal, source = iota((outs, places), 0), iota((outs, places), 1)
    goal_row, goal_array, goal_slot = goal >> 4, (goal >> 2) & 3, goal & 3
    tile_of = jnp.where(goal_array < 2, goal_array, goal_array + 1)
    last = goal_row == yn
    main = jnp.where(last, 5 * ROWS + tile_of * SLOTS + goal_slot, tile_of * ROWS + goal_row * SLOTS + goal_slot)
    side_term = jnp.where(last, 5 * ROWS + 2 * SLOTS + goal_slot, 2 * ROWS + goal_row * SLOTS + goal_slot)
    arrange = one_hot((source == main) | ((source == side_term) & (goal_array == 1)))

    def split(x):
        upper = x.astype(BF16)
        return upper, (x - upper.astype(F32)).astype(BF16)

    for copy in t_copies:
        copy.wait_recv()
    column = t_own[0].astype(F32)
    for d in range(1, xn):
        column = column + t_in[d - 1].astype(F32)
    upper, lower = split(column.reshape(places, width) * factor)
    u = (dot_nn(arrange, upper) + dot_nn(arrange, lower)).astype(BF16).reshape(yn + 1, ROWS, width)
    for e in range(yn):
        u_own[e, 0] = u[e]
        u_own[e, 1] = u[yn]
    u_copies = [send(u_own.at[e], u_in.at[e - 1], y_peers[e - 1]) for e in range(1, yn)]

    for copy in u_copies:
        copy.wait_recv()
    mine = u_own[0].astype(F32)
    for e in range(1, yn):
        mine = mine + u_in[e - 1].astype(F32)
    r_scr[...] = mine.reshape(2 * ROWS, width)
    keep(r_scr, r_out)

    for copy in stores:
        copy.wait()
    for copy in copies:
        copy.wait_send()


def finish(scale, o_ref, dq_in, dk_in, dv_in, hot_ref, flag_ref, r_ref, out_ref, dq_ref, dk_ref, dv_ref, total):
    tok = o_ref.shape[0]
    total[...] = jnp.zeros_like(total)
    total[0 : 2 * ROWS, :] = r_ref[...]
    upper = total[...].astype(BF16)
    lower = (total[...] - upper.astype(F32)).astype(BF16)
    hot = hot_ref[...].astype(F32)
    lane_array = (iota((tok, TILE), 1) >> 2) & 3

    def placed(a):
        mine = jnp.where(lane_array == a, hot, 0.0).astype(BF16)
        return dot_nn(mine, upper) + dot_nn(mine, lower)

    out_ref[...] = jnp.where(flag_ref[...] > 0.5, placed(0), o_ref[...]).astype(BF16)
    dq_ref[...] = dq_in[...] + placed(1) * scale
    dk_ref[...] = dk_in[...] + placed(2) * scale
    dv_ref[...] = dv_in[...] + placed(3)


def shards(n, query_rows, key_rows, value_rows, out_grad, global_pos):
    tok, _, width = query_rows.shape
    count = global_pos.shape[0]
    yn = 4
    xn = n // (2 * yn)
    window = tok + 2 * HALF
    span = TILE + 2 * HALF
    copies = 4 * (xn - 1) + 4 * (yn - 1) + 16
    vmem = pl.BlockSpec(memory_space=pltpu.VMEM)
    anywhere = pl.BlockSpec(memory_space=pl.ANY)
    flat = [x.reshape(tok, width) for x in (query_rows, key_rows, value_rows, out_grad)]
    rows_f32 = jax.ShapeDtypeStruct((tok, width), F32)
    middle = pl.pallas_call(
        functools.partial(kernel, (n, yn, xn, tok, count, width)),
        name="sparse_attention",
        out_shape=(rows_f32,) * 4
        + (
            jax.ShapeDtypeStruct((tok, TILE), BF16),
            rows_f32,
            jax.ShapeDtypeStruct((2 * ROWS, width), F32),
        ),
        in_specs=[pl.BlockSpec(memory_space=pltpu.HBM)] * 5,
        out_specs=(anywhere,) * 7,
        scratch_shapes=[
            pltpu.VMEM((1, count), I32),
            pltpu.VMEM((tok, width), BF16),
            pltpu.VMEM((tok, width), BF16),
            pltpu.VMEM((window, width), BF16),
            pltpu.VMEM((window, width), BF16),
            pltpu.VMEM((tok, width), BF16),
            pltpu.VMEM((1, window), F32),
            pltpu.VMEM((tok, width), F32),
            pltpu.VMEM((2, ROWS, width), BF16),
            pltpu.VMEM((xn, 2, ROWS, width), BF16),
            pltpu.VMEM((2, yn, xn + 1, ROWS, width), BF16),
            pltpu.VMEM((4, count, 2 * yn * (xn + 1) * ROWS), BF16),
            pltpu.VMEM((4, count, width), BF16),
            pltpu.VMEM((tok, span), F32),
            pltpu.VMEM((tok, span), F32),
            pltpu.VMEM((tok, width), F32),
            pltpu.VMEM((tok, width), F32),
            pltpu.VMEM((tok, width), F32),
            pltpu.VMEM((tok, width), F32),
            pltpu.VMEM((window, width), F32),
            pltpu.VMEM((window, width), F32),
            pltpu.VMEM((count, width), F32),
            pltpu.VMEM((count, width), F32),
            pltpu.VMEM((tok, count), F32),
            pltpu.VMEM((tok, count), F32),
            pltpu.VMEM((8, TILE), F32),
            pltpu.VMEM((8, TILE), F32),
            pltpu.VMEM((8, TILE), F32),
            pltpu.VMEM((xn - 1, 8, TILE), F32),
            pltpu.VMEM((8, TILE), F32),
            pltpu.VMEM((yn - 1, 8, TILE), F32),
            pltpu.VMEM((tok, width), F32),
            pltpu.VMEM((tok, width), F32),
            pltpu.VMEM((2 * xn * yn * SLOTS, count), BF16),
            pltpu.VMEM((2 * ROWS, count), F32),
            pltpu.VMEM((tok, TILE), BF16),
            pltpu.VMEM((2, 5 * xn + 2, ROWS, width), BF16),
            pltpu.VMEM((5 * xn + 2, ROWS, width), BF16),
            pltpu.VMEM((xn, 7, ROWS, width), BF16),
            pltpu.VMEM((xn - 1, 7, ROWS, width), BF16),
            pltpu.VMEM((yn, 2, ROWS, width), BF16),
            pltpu.VMEM((yn - 1, 2, ROWS, width), BF16),
            pltpu.VMEM((2 * ROWS, width), F32),
            pltpu.VMEM((2, 2, HALF, width), BF16),
            pltpu.VMEM((2, 2, HALF, width), BF16),
            pltpu.SemaphoreType.DMA((copies,)),
            pltpu.SemaphoreType.DMA((copies,)),
            pltpu.SemaphoreType.DMA((5,)),
            pltpu.SemaphoreType.DMA((7,)),
        ],
        compiler_params=pltpu.CompilerParams(
            collective_id=0, has_side_effects=True, vmem_limit_bytes=24 << 20
        ),
    )(*[pltpu.with_memory_space_constraint(x, pltpu.HBM) for x in (global_pos.reshape(1, count), *flat)])
    results = pl.pallas_call(
        functools.partial(finish, width**-0.5),
        name="place_global_rows",
        out_shape=(jax.ShapeDtypeStruct((tok, width), BF16),) + (rows_f32,) * 3,
        in_specs=[vmem] * 7,
        out_specs=(vmem,) * 4,
        scratch_shapes=[pltpu.VMEM((TILE, width), F32)],
        compiler_params=pltpu.CompilerParams(vmem_limit_bytes=8 << 20),
    )(*middle)
    return tuple(x.reshape(tok, 1, width) for x in results)


def solution(mesh):
    rows = P("ctx", "head", None)
    return jax.shard_map(
        functools.partial(shards, mesh.shape["ctx"]),
        mesh=mesh,
        in_specs=(rows,) * 4 + (P(),),
        out_specs=(rows,) * 4,
        check_vma=False,
    )
```

```python
import functools

import jax
import jax.numpy as jnp
from jax import lax
from jax.experimental import pallas as pl
from jax.experimental.pallas import tpu as pltpu
from jax.sharding import PartitionSpec as P

MESH = pl.DeviceIdType.MESH
HALF = 512
TILE = 128
SLOTS = 4
ROWS = 16
NEG = -1e30
F32 = jnp.float32
BF16 = jnp.bfloat16
I32 = jnp.int32


def dot_nn(a, b):
    return lax.dot_general(a, b, (((1,), (0,)), ((), ())), preferred_element_type=F32)


def dot_nt(a, b):
    return lax.dot_general(a, b, (((1,), (1,)), ((), ())), preferred_element_type=F32)


def dot_tn(a, b):
    return lax.dot_general(a, b, (((0,), (0,)), ((), ())), preferred_element_type=F32)


def iota(shape, dim):
    return lax.broadcasted_iota(I32, shape, dim)


def one_hot(cond):
    return jnp.where(cond, 1.0, 0.0).astype(BF16)


def kernel(
    sizes,
    pos_hbm,
    q_hbm,
    k_hbm,
    v_hbm,
    do_hbm,
    o_out,
    dq_out,
    dk_out,
    dv_out,
    hot_out,
    flag_out,
    r_out,
    pos_scr,
    q_ref,
    do_ref,
    kpad,
    vpad,
    lgrad,
    colbias,
    rowflag,
    pack,
    gx,
    gath,
    pick,
    glob,
    p_scr,
    d_scr,
    m_scr,
    l_scr,
    o_scr,
    dq_scr,
    dkpad,
    dvpad,
    dkg,
    dvg,
    sg_scr,
    gw_scr,
    st_own,
    st_sib,
    st_x,
    st_xin,
    st_y,
    st_yin,
    dkown,
    dvown,
    spread,
    spread_over,
    hot_scr,
    z1_own,
    z1_sib,
    t1_own,
    t1_in,
    z2_own,
    z2_sib,
    t2_own,
    t2_in,
    f_scr,
    u_own,
    u_in,
    r_scr,
    rim_out,
    rim_in,
    send_sem,
    recv_sem,
    load_sem,
    store_sem,
):
    n, yn, xn, tok, count, width = sizes
    seq = n * tok
    scale = width**-0.5
    x_shift = xn.bit_length() - 1
    tok_shift = tok.bit_length() - 1
    window = tok + 2 * HALF
    span = TILE + 2 * HALF
    tiles = tok // TILE
    own = pl.ds(HALF, tok)

    me = lax.axis_index("ctx")
    core = lax.rem(me, 2)
    xx = lax.rem(lax.div(me, 2), xn)
    yy = lax.div(me, 2 * xn)

    def ctx_id(y, x, c):
        return (y * xn + x) * 2 + c

    x_peers = [ctx_id(yy, lax.rem(xx + d, xn), core) for d in range(1, xn)]
    y_peers = [ctx_id(lax.rem(yy + e, yn), xx, core) for e in range(1, yn)]
    sibling = me + 1 - 2 * core
    right = lax.rem(me + 1, n)
    left = lax.rem(me + n - 1, n)
    greeted = x_peers + y_peers + [left, right]
    x_order = sorted(range(1, xn), key=lambda d: -min(d, xn - d))
    y_order = sorted(range(1, yn), key=lambda e: -min(e, yn - e))

    barrier = pltpu.get_barrier_semaphore()
    for peer in greeted:
        pl.semaphore_signal(barrier, inc=1, device_id={"ctx": peer}, device_id_type=MESH)

    loads = [
        pltpu.make_async_copy(src, dst, load_sem.at[i])
        for i, (src, dst) in enumerate(
            (
                (pos_hbm, pos_scr),
                (q_hbm, q_ref),
                (k_hbm, kpad.at[own]),
                (v_hbm, vpad.at[own]),
                (do_hbm, do_ref),
            )
        )
    ]
    for load in loads:
        load.start()

    copies = []

    def send(src, dst, peer):
        number = len(copies)
        copy = pltpu.make_async_remote_copy(
            src_ref=src,
            dst_ref=dst,
            send_sem=send_sem.at[number],
            recv_sem=recv_sem.at[number],
            device_id={"ctx": peer},
            device_id_type=MESH,
        )
        copy.start()
        copies.append(copy)
        return copy

    stores = []

    def keep(src, dst):
        copy = pltpu.make_async_copy(src, dst, store_sem.at[len(stores)])
        copy.start()
        stores.append(copy)

    loads[0].wait()
    pos_r = pos_scr[...]
    first, second = iota((count, count), 0), iota((count, count), 1)
    pos_c = jnp.sum(jnp.where(first == second, pos_r.astype(F32), 0.0), axis=1, keepdims=True).astype(I32)
    owner_c, owner_r = pos_c >> tok_shift, pos_r >> tok_shift
    local_c, local_r = pos_c & (tok - 1), pos_r & (tok - 1)
    same = owner_c == owner_r
    rank_c = jnp.sum(jnp.where(same & (second < first), 1.0, 0.0), axis=1, keepdims=True).astype(I32)
    rank_r = jnp.sum(jnp.where(same & (first < second), 1.0, 0.0), axis=0, keepdims=True).astype(I32)

    rho = iota((2 * ROWS, count), 0)
    slot_rank = ((rho >> 4) << 2) + (rho & 3)
    chosen = (owner_r == me) & (rank_r == slot_rank)
    slot_col = jnp.sum(jnp.where(chosen, (local_r + 1).astype(F32), 0.0), axis=1, keepdims=True).astype(I32) - 1
    array_of = (iota((2 * ROWS, tok), 0) >> 2) & 3
    at_slot = iota((2 * ROWS, tok), 1) == slot_col
    picked = jnp.zeros((2 * ROWS, width), F32)
    for load in loads[1:]:
        load.wait()
    for a, rows in enumerate((q_ref[...], kpad[own, :], vpad[own, :], do_ref[...])):
        picked = picked + dot_nn(one_hot(at_slot & (array_of == a)), rows)
    pack[...] = picked.astype(BF16).reshape(2, ROWS, width)
    gx[0] = pack[...]

    pl.semaphore_wait(barrier, len(greeted))

    from_x = [send(pack, gx.at[d], x_peers[d - 1]) for d in x_order]
    halos = [
        send(kpad.at[own], kpad.at[pl.ds(0, HALF)], right),
        send(kpad.at[own], kpad.at[pl.ds(HALF + tok, HALF)], left),
        send(vpad.at[own], vpad.at[pl.ds(0, HALF)], right),
        send(vpad.at[own], vpad.at[pl.ds(HALF + tok, HALF)], left),
    ]

    dkpad[...] = jnp.zeros((window, width), F32)
    dvpad[...] = jnp.zeros((window, width), F32)
    for part in range(window // 512):
        reach = me * tok - HALF + part * 512 + iota((1, 512), 1)
        bias = jnp.min(jnp.where(pos_c == reach, NEG, 0.0), axis=0, keepdims=True)
        inside = (reach >= 0) & (reach < seq)
        colbias[:, pl.ds(part * 512, 512)] = jnp.where(inside, bias, NEG)
    row_pos = me * tok + iota((tok, 1), 0)
    flag = jnp.max(jnp.where(row_pos == pos_r, 1.0, 0.0), axis=1, keepdims=True)
    rowflag[...] = jnp.broadcast_to(flag, (tok, width))
    lgrad[...] = jnp.where(rowflag[...] > 0.5, 0.0, do_ref[...].astype(F32)).astype(BF16)

    for copy in from_x:
        copy.wait_recv()
    over = gx[0, 1].astype(F32)
    gath[0, 0, 0] = gx[0, 0]
    for d in range(1, xn):
        gath[0, 0, d] = gx[d, 0]
        over = over + gx[d, 1].astype(F32)
    gath[0, 0, xn] = over.astype(BF16)
    from_y = {e: send(gath.at[0, 0], gath.at[0, e], y_peers[e - 1]) for e in y_order}
    from_sib = [send(gath.at[0, 0], gath.at[1, 0], sibling)]

    core_c, xo_c, yo_c = owner_c & 1, (owner_c >> 1) & (xn - 1), owner_c >> (1 + x_shift)
    half_c = (core_c ^ core) * yn + ((yy - yo_c) & (yn - 1))
    src_c = jnp.where(
        rank_c < SLOTS,
        (half_c * (xn + 1) + ((xx - xo_c) & (xn - 1))) * ROWS + rank_c,
        (half_c * (xn + 1) + xn) * ROWS + rank_c - SLOTS,
    )
    total = 2 * yn * (xn + 1) * ROWS
    for a in range(4):
        pick[a] = one_hot(iota((count, total), 1) == src_c + SLOTS * a)

    core_r, xo_r, yo_r = owner_r & 1, (owner_r >> 1) & (xn - 1), owner_r >> (1 + x_shift)
    place = ((core_r ^ core) * xn + ((xo_r - xx) & (xn - 1))) * yn + ((yo_r - yy) & (yn - 1))
    beyond = 2 * xn * yn * SLOTS
    key_r = jnp.where(rank_r < SLOTS, place * SLOTS + rank_r, beyond + rank_r - SLOTS)
    spread[...] = one_hot(iota((beyond, count), 0) == key_r)
    spread_over[...] = jnp.where(beyond + (iota((ROWS, count), 0) & 3) == key_r, 1.0, 0.0)

    rho_lane = iota((count, TILE), 1)
    lane_rank = ((rho_lane >> 4) << 2) + (rho_lane & 3)
    chosen_c = (owner_c == me) & (rank_c == lane_rank) & (rho_lane < 2 * ROWS)
    slot_row = jnp.sum(jnp.where(chosen_c, (local_c + 1).astype(F32), 0.0), axis=0, keepdims=True).astype(I32) - 1
    hot_scr[...] = one_hot(iota((tok, TILE), 0) == slot_row)
    keep(hot_scr, hot_out)
    keep(rowflag, flag_out)

    for copy in halos:
        copy.wait_recv()

    lane = iota((TILE, TILE), 1)
    sub = iota((TILE, TILE), 0)
    low_bias = jnp.where(lane >= sub, 0.0, NEG)
    high_bias = jnp.where(lane <= sub, 0.0, NEG)

    def before(t, carry):
        start = pl.multiple_of(t * TILE, TILE)
        rows, keys = pl.ds(start, TILE), pl.ds(start, span)
        s = dot_nt(q_ref[rows, :], kpad[keys, :]) * scale + colbias[:, keys]
        s = jnp.concatenate(
            [s[:, :TILE] + low_bias, s[:, TILE : 2 * HALF], s[:, 2 * HALF :] + high_bias], axis=1
        )
        top = jnp.max(s, axis=1, keepdims=True)
        p = jnp.exp(s - top)
        p_scr[rows, :] = p
        m_scr[rows, :] = jnp.broadcast_to(top, (TILE, width))
        l_scr[rows, :] = jnp.broadcast_to(jnp.sum(p, axis=1, keepdims=True), (TILE, width))
        d_scr[rows, :] = dot_nt(lgrad[rows, :], vpad[keys, :])
        return carry

    lax.fori_loop(0, tiles, before, 0)

    for e in reversed(y_order):
        from_y[e].wait_recv()
        from_sib.append(send(gath.at[0, e], gath.at[1, e], sibling))
    for copy in from_sib:
        copy.wait_recv()
    everything = gath[...].reshape(total, width)
    for a in range(4):
        glob[a] = dot_nn(pick[a], everything).astype(BF16)

    middle = (jnp.sum(glob[2].astype(F32), axis=0, keepdims=True) * (1.0 / count)).astype(BF16)
    centre = dot_nt(jnp.broadcast_to(middle, (ROWS, width)), glob[3])[0:1, :]
    sg = dot_nt(kpad[own, :], glob[0]) * scale
    gw = dot_nt(vpad[own, :], glob[3]) - centre
    sg_scr[...] = sg
    gw_scr[...] = gw
    top = jnp.max(sg, axis=0, keepdims=True)
    p = jnp.exp(sg - top)
    stat_rows = [top, jnp.sum(p, axis=0, keepdims=True), jnp.sum(p * gw, axis=0, keepdims=True)]
    for r, row in enumerate(stat_rows):
        st_own[2 * r : 2 * r + 1, :] = row[:, :TILE]
        st_own[2 * r + 1 : 2 * r + 2, :] = row[:, TILE:]
    st_own[6:8, :] = jnp.zeros((2, TILE), F32)

    def join(parts):
        joined = functools.reduce(jnp.maximum, [part[0:2, :] for part in parts])
        weigh = [jnp.exp(part[0:2, :] - joined) for part in parts]
        return (
            joined,
            sum(part[2:4, :] * w for part, w in zip(parts, weigh)),
            sum(part[4:6, :] * w for part, w in zip(parts, weigh)),
        )

    def store(ref, stats):
        for r, part in enumerate(stats):
            ref[2 * r : 2 * r + 2, :] = part
        ref[6:8, :] = jnp.zeros((2, TILE), F32)

    def row_of(part):
        return jnp.concatenate([part[0:1], part[1:2]], axis=1)

    stat_sib = send(st_own, st_sib, sibling)

    dkg[...] = jnp.zeros((count, width), F32)
    dvg[...] = jnp.zeros((count, width), F32)

    def after(t, carry):
        start = pl.multiple_of(t * TILE, TILE)
        rows, keys = pl.ds(start, TILE), pl.ds(start, span)
        q, lg = q_ref[rows, :], lgrad[rows, :]
        kw, vw = kpad[keys, :], vpad[keys, :]
        s = dot_nt(q, glob[1]) * scale
        top_w = m_scr[rows, 0:1]
        top = jnp.maximum(top_w, jnp.max(s, axis=1, keepdims=True))
        pg = jnp.exp(s - top)
        down = jnp.exp(top_w - top)
        inv = 1.0 / (l_scr[rows, 0:1] * down + jnp.sum(pg, axis=1, keepdims=True))
        pw = p_scr[rows, :] * (down * inv)
        pg = pg * inv
        pw16, pg16 = pw.astype(BF16), pg.astype(BF16)
        o = dot_nn(pw16, vw) + dot_nn(pg16, glob[2])
        o_scr[rows, :] = o
        row_dot = jnp.sum(lg.astype(F32) * o, axis=1, keepdims=True)
        dsw = (pw * (d_scr[rows, :] - row_dot)).astype(BF16)
        dsg = (pg * (dot_nt(lg, glob[2]) - row_dot)).astype(BF16)
        dq_scr[rows, :] = (dot_nn(dsw, kw) + dot_nn(dsg, glob[1])) * scale
        dkpad[keys, :] += dot_tn(dsw, q)
        dvpad[keys, :] += dot_tn(pw16, lg)
        dkg[...] += dot_tn(dsg, q)
        dvg[...] += dot_tn(pg16, lg)
        return carry

    lax.fori_loop(0, 1, after, 0)
    stat_sib.wait_recv()
    store(st_x, join([st_own[...], st_sib[...]]))
    stat_x = [send(st_x, st_xin.at[d - 1], x_peers[d - 1]) for d in x_order]
    pair_top = st_x[0:2, :]
    over_row = iota((ROWS, count), 0)

    def ordered(partial, arrays, ref):
        z = dot_nn(spread[...], partial).astype(BF16)
        z_over = jnp.zeros((ROWS, width), F32)
        for a in range(arrays):
            mine = jnp.where((over_row >> 2) == a, spread_over[...], 0.0).astype(BF16)
            z_over = z_over + dot_nn(mine, partial[:, a * width : (a + 1) * width])
        z_over = z_over.astype(BF16)
        for half in range(2):
            for d in range(xn):
                base = (half * xn + d) * ROWS
                for a in range(arrays):
                    ref[half, d * arrays + a] = z[base : base + ROWS, a * width : (a + 1) * width]
            ref[half, arrays * xn] = z_over

    def paired(own_ref, sib_ref, arrays, ref):
        over = (own_ref[0, arrays * xn].astype(F32) + sib_ref[arrays * xn].astype(F32)).astype(BF16)
        for d in range(xn):
            tiles_of = pl.ds(d * arrays, arrays)
            ref[d, 0:arrays] = (own_ref[0, tiles_of].astype(F32) + sib_ref[tiles_of].astype(F32)).astype(BF16)
            ref[d, arrays] = over

    w = jnp.exp(sg_scr[...] - row_of(pair_top))
    w16 = w.astype(BF16)
    ds16 = (w * gw_scr[...]).astype(BF16)
    value_key = dot_tn(w16, jnp.concatenate([vpad[own, :], kpad[own, :]], axis=1))
    partial = [value_key[:, :width], dot_tn(ds16, kpad[own, :]), value_key[:, width:]]
    ordered(jnp.concatenate(partial, axis=1).astype(BF16), 3, z1_own)
    z1_copy = send(z1_own.at[1], z1_sib, sibling)

    lax.fori_loop(1, 2, after, 0)
    z1_copy.wait_recv()
    paired(z1_own, z1_sib, 3, t1_own)
    t1_copies = [send(t1_own.at[d], t1_in.at[d - 1], x_peers[d - 1]) for d in x_order]
    lax.fori_loop(2, tiles, after, 0)

    ordered(jnp.concatenate([dkg[...], dvg[...]], axis=1).astype(BF16), 2, z2_own)
    z2_copy = send(z2_own.at[1], z2_sib, sibling)

    rim_out[0, 0] = dkpad[pl.ds(0, HALF), :].astype(BF16)
    rim_out[0, 1] = dvpad[pl.ds(0, HALF), :].astype(BF16)
    rim_out[1, 0] = dkpad[pl.ds(HALF + tok, HALF), :].astype(BF16)
    rim_out[1, 1] = dvpad[pl.ds(HALF + tok, HALF), :].astype(BF16)
    keep(o_scr, o_out)
    keep(dq_scr, dq_out)

    z2_copy.wait_recv()
    paired(z2_own, z2_sib, 2, t2_own)
    t2_copies = [send(t2_own.at[d], t2_in.at[d - 1], x_peers[d - 1]) for d in x_order]
    rims = [send(rim_out.at[1], rim_in.at[0], right), send(rim_out.at[0], rim_in.at[1], left)]

    for copy in stat_x:
        copy.wait_recv()
    store(st_y, join([st_x[...]] + [st_xin[d - 1] for d in range(1, xn)]))
    stat_y = [send(st_y, st_yin.at[e - 1], y_peers[e - 1]) for e in y_order]

    outs = (yn + 1) * ROWS

    def arrange(arrays, wanted):
        goal, source = iota((outs, (arrays + 1) * ROWS), 0), iota((outs, (arrays + 1) * ROWS), 1)
        goal_row, goal_array, goal_slot = goal >> 4, (goal >> 2) & 3, goal & 3
        hit = jnp.zeros(goal.shape, F32)
        for array, tile in wanted:
            at = jnp.where(
                goal_row == yn,
                arrays * ROWS + tile * SLOTS + goal_slot,
                tile * ROWS + goal_row * SLOTS + goal_slot,
            )
            hit = hit + jnp.where((goal_array == array) & (source == at), 1.0, 0.0)
        return hit.astype(BF16)

    arrange_1 = arrange(3, ((0, 0), (1, 1), (1, 2)))
    arrange_2 = arrange(2, ((2, 0), (3, 1)))

    for copy in stat_y:
        copy.wait_recv()
    joined, summed, dotted = join([st_y[...]] + [st_yin[e - 1] for e in range(1, yn)])
    lse = row_of(joined + jnp.log(summed))
    ratio = row_of(dotted / summed)
    line = iota((4 * ROWS, count), 0)
    line_key = jnp.where(line < 3 * ROWS, line & (ROWS - 1), beyond + (line & 3))
    kind = jnp.where(line < 3 * ROWS, line >> 4, (line >> 2) & 3)
    found = jnp.where(line_key == key_r, 1.0, 0.0)
    found = found * jnp.where(kind == 2, -ratio, jnp.where(kind == 3, 0.0, 1.0))
    for d in range(xn):
        pair = st_x[0:2, :] if d == 0 else st_xin[d - 1, 0:2, :]
        fall = row_of(jnp.exp(pair - joined) / summed)
        factor = jnp.sum(found * fall, axis=1, keepdims=True)
        f_scr[d] = jnp.broadcast_to(factor, (4 * ROWS, width))

    w = jnp.exp(sg_scr[...] - lse)
    dvown[...] = dvpad[own, :] + dot_nn(w.astype(BF16), glob[3])
    dkown[...] = dkpad[own, :] + dot_nn((w * (gw_scr[...] - ratio)).astype(BF16), glob[0])

    def split(x):
        upper = x.astype(BF16)
        return upper, (x - upper.astype(F32)).astype(BF16)

    for copy in t1_copies:
        copy.wait_recv()
    column = t1_own[0].astype(F32).reshape(4 * ROWS, width) * f_scr[0]
    for d in range(1, xn):
        column = column + t1_in[d - 1].astype(F32).reshape(4 * ROWS, width) * f_scr[d]
    upper, lower = split(column)
    u = dot_nn(arrange_1, upper) + dot_nn(arrange_1, lower)
    for copy in t2_copies:
        copy.wait_recv()
    column = t2_own[0].astype(F32)
    for d in range(1, xn):
        column = column + t2_in[d - 1].astype(F32)
    upper, lower = split(column.reshape(3 * ROWS, width))
    u = u + dot_nn(arrange_2, upper) + dot_nn(arrange_2, lower)
    u = u.astype(BF16).reshape(yn + 1, ROWS, width)
    for e in range(yn):
        u_own[e, 0] = u[e]
        u_own[e, 1] = u[yn]
    u_copies = [send(u_own.at[e], u_in.at[e - 1], y_peers[e - 1]) for e in y_order]

    for copy in rims:
        copy.wait_recv()
    dk_sum, dv_sum = dkown[...], dvown[...]
    for side in range(2):
        dk_sum = dk_sum + rim_in[side, 0].astype(F32)
        dv_sum = dv_sum + rim_in[side, 1].astype(F32)
    dkown[...] = dk_sum * scale
    dvown[...] = dv_sum
    keep(dkown, dk_out)
    keep(dvown, dv_out)

    for copy in u_copies:
        copy.wait_recv()
    mine = u_own[0].astype(F32)
    for e in range(1, yn):
        mine = mine + u_in[e - 1].astype(F32)
    r_scr[...] = mine.reshape(2 * ROWS, width)
    keep(r_scr, r_out)

    for copy in stores:
        copy.wait()
    for copy in copies:
        copy.wait_send()


def finish(scale, o_ref, dq_in, dk_in, dv_in, hot_ref, flag_ref, r_ref, out_ref, dq_ref, dk_ref, dv_ref, total):
    tok = o_ref.shape[0]
    total[...] = jnp.zeros_like(total)
    total[0 : 2 * ROWS, :] = r_ref[...]
    upper = total[...].astype(BF16)
    lower = (total[...] - upper.astype(F32)).astype(BF16)
    hot = hot_ref[...].astype(F32)
    lane_array = (iota((tok, TILE), 1) >> 2) & 3

    def placed(a):
        mine = jnp.where(lane_array == a, hot, 0.0).astype(BF16)
        return dot_nn(mine, upper) + dot_nn(mine, lower)

    out_ref[...] = jnp.where(flag_ref[...] > 0.5, placed(0), o_ref[...]).astype(BF16)
    dq_ref[...] = dq_in[...] + placed(1) * scale
    dk_ref[...] = dk_in[...] + placed(2) * scale
    dv_ref[...] = dv_in[...] + placed(3)


def shards(n, query_rows, key_rows, value_rows, out_grad, global_pos):
    tok, _, width = query_rows.shape
    count = global_pos.shape[0]
    yn = 4
    xn = n // (2 * yn)
    window = tok + 2 * HALF
    span = TILE + 2 * HALF
    copies = 4 * (xn - 1) + 4 * (yn - 1) + 16
    vmem = pl.BlockSpec(memory_space=pltpu.VMEM)
    anywhere = pl.BlockSpec(memory_space=pl.ANY)
    flat = [x.reshape(tok, width) for x in (query_rows, key_rows, value_rows, out_grad)]
    rows_f32 = jax.ShapeDtypeStruct((tok, width), F32)
    middle = pl.pallas_call(
        functools.partial(kernel, (n, yn, xn, tok, count, width)),
        name="sparse_attention",
        out_shape=(rows_f32,) * 4
        + (
            jax.ShapeDtypeStruct((tok, TILE), BF16),
            rows_f32,
            jax.ShapeDtypeStruct((2 * ROWS, width), F32),
        ),
        in_specs=[pl.BlockSpec(memory_space=pltpu.HBM)] * 5,
        out_specs=(anywhere,) * 7,
        scratch_shapes=[
            pltpu.VMEM((1, count), I32),
            pltpu.VMEM((tok, width), BF16),
            pltpu.VMEM((tok, width), BF16),
            pltpu.VMEM((window, width), BF16),
            pltpu.VMEM((window, width), BF16),
            pltpu.VMEM((tok, width), BF16),
            pltpu.VMEM((1, window), F32),
            pltpu.VMEM((tok, width), F32),
            pltpu.VMEM((2, ROWS, width), BF16),
            pltpu.VMEM((xn, 2, ROWS, width), BF16),
            pltpu.VMEM((2, yn, xn + 1, ROWS, width), BF16),
            pltpu.VMEM((4, count, 2 * yn * (xn + 1) * ROWS), BF16),
            pltpu.VMEM((4, count, width), BF16),
            pltpu.VMEM((tok, span), F32),
            pltpu.VMEM((tok, span), F32),
            pltpu.VMEM((tok, width), F32),
            pltpu.VMEM((tok, width), F32),
            pltpu.VMEM((tok, width), F32),
            pltpu.VMEM((tok, width), F32),
            pltpu.VMEM((window, width), F32),
            pltpu.VMEM((window, width), F32),
            pltpu.VMEM((count, width), F32),
            pltpu.VMEM((count, width), F32),
            pltpu.VMEM((tok, count), F32),
            pltpu.VMEM((tok, count), F32),
            pltpu.VMEM((8, TILE), F32),
            pltpu.VMEM((8, TILE), F32),
            pltpu.VMEM((8, TILE), F32),
            pltpu.VMEM((xn - 1, 8, TILE), F32),
            pltpu.VMEM((8, TILE), F32),
            pltpu.VMEM((yn - 1, 8, TILE), F32),
            pltpu.VMEM((tok, width), F32),
            pltpu.VMEM((tok, width), F32),
            pltpu.VMEM((2 * xn * yn * SLOTS, count), BF16),
            pltpu.VMEM((ROWS, count), F32),
            pltpu.VMEM((tok, TILE), BF16),
            pltpu.VMEM((2, 3 * xn + 1, ROWS, width), BF16),
            pltpu.VMEM((3 * xn + 1, ROWS, width), BF16),
            pltpu.VMEM((xn, 4, ROWS, width), BF16),
            pltpu.VMEM((xn - 1, 4, ROWS, width), BF16),
            pltpu.VMEM((2, 2 * xn + 1, ROWS, width), BF16),
            pltpu.VMEM((2 * xn + 1, ROWS, width), BF16),
            pltpu.VMEM((xn, 3, ROWS, width), BF16),
            pltpu.VMEM((xn - 1, 3, ROWS, width), BF16),
            pltpu.VMEM((xn, 4 * ROWS, width), F32),
            pltpu.VMEM((yn, 2, ROWS, width), BF16),
            pltpu.VMEM((yn - 1, 2, ROWS, width), BF16),
            pltpu.VMEM((2 * ROWS, width), F32),
            pltpu.VMEM((2, 2, HALF, width), BF16),
            pltpu.VMEM((2, 2, HALF, width), BF16),
            pltpu.SemaphoreType.DMA((copies,)),
            pltpu.SemaphoreType.DMA((copies,)),
            pltpu.SemaphoreType.DMA((5,)),
            pltpu.SemaphoreType.DMA((7,)),
        ],
        compiler_params=pltpu.CompilerParams(
            collective_id=0, has_side_effects=True, vmem_limit_bytes=24 << 20
        ),
    )(*[pltpu.with_memory_space_constraint(x, pltpu.HBM) for x in (global_pos.reshape(1, count), *flat)])
    results = pl.pallas_call(
        functools.partial(finish, width**-0.5),
        name="place_global_rows",
        out_shape=(jax.ShapeDtypeStruct((tok, width), BF16),) + (rows_f32,) * 3,
        in_specs=[vmem] * 7,
        out_specs=(vmem,) * 4,
        scratch_shapes=[pltpu.VMEM((TILE, width), F32)],
        compiler_params=pltpu.CompilerParams(vmem_limit_bytes=8 << 20),
    )(*middle)
    return tuple(x.reshape(tok, 1, width) for x in results)


def solution(mesh):
    rows = P("ctx", "head", None)
    return jax.shard_map(
        functools.partial(shards, mesh.shape["ctx"]),
        mesh=mesh,
        in_specs=(rows,) * 4 + (P(),),
        out_specs=(rows,) * 4,
        check_vma=False,
    )
```

```python
import functools

import jax
import jax.numpy as jnp
from jax import lax
from jax.experimental import pallas as pl
from jax.experimental.pallas import tpu as pltpu
from jax.sharding import PartitionSpec as P

MESH = pl.DeviceIdType.MESH
HALF = 512
TILE = 128
SLOTS = 4
ROWS = 16
NEG = -1e30
F32 = jnp.float32
BF16 = jnp.bfloat16
I32 = jnp.int32


def dot_nn(a, b):
    return lax.dot_general(a, b, (((1,), (0,)), ((), ())), preferred_element_type=F32)


def dot_nt(a, b):
    return lax.dot_general(a, b, (((1,), (1,)), ((), ())), preferred_element_type=F32)


def dot_tn(a, b):
    return lax.dot_general(a, b, (((0,), (0,)), ((), ())), preferred_element_type=F32)


def iota(shape, dim):
    return lax.broadcasted_iota(I32, shape, dim)


def one_hot(cond):
    return jnp.where(cond, 1.0, 0.0).astype(BF16)


def kernel(
    sizes,
    pos_hbm,
    q_hbm,
    k_hbm,
    v_hbm,
    do_hbm,
    o_out,
    dq_out,
    dk_out,
    dv_out,
    hot_out,
    flag_out,
    r_out,
    pos_scr,
    q_ref,
    do_ref,
    kpad,
    vpad,
    lgrad,
    colbias,
    rowflag,
    pack,
    gx,
    gath,
    pick,
    glob,
    p_scr,
    ow_scr,
    d_scr,
    m_scr,
    l_scr,
    o_scr,
    dq_scr,
    dkpad,
    dvpad,
    sg_scr,
    gw_scr,
    st_own,
    st_sib,
    st_x,
    st_xin,
    st_y,
    st_yin,
    dkown,
    dvown,
    spread,
    spread_over,
    hot_scr,
    z1_own,
    z1_sib,
    t1_own,
    t1_in,
    z2_own,
    z2_sib,
    t2_own,
    t2_in,
    f_scr,
    u_own,
    u_in,
    v_own,
    v_in,
    r_scr,
    rim_out,
    rim_in,
    send_sem,
    recv_sem,
    load_sem,
    store_sem,
):
    n, yn, xn, tok, count, width = sizes
    seq = n * tok
    scale = width**-0.5
    x_shift = xn.bit_length() - 1
    tok_shift = tok.bit_length() - 1
    window = tok + 2 * HALF
    span = TILE + 2 * HALF
    tiles = tok // TILE
    own = pl.ds(HALF, tok)

    me = lax.axis_index("ctx")
    core = lax.rem(me, 2)
    xx = lax.rem(lax.div(me, 2), xn)
    yy = lax.div(me, 2 * xn)

    def ctx_id(y, x, c):
        return (y * xn + x) * 2 + c

    x_peers = [ctx_id(yy, lax.rem(xx + d, xn), core) for d in range(1, xn)]
    y_peers = [ctx_id(lax.rem(yy + e, yn), xx, core) for e in range(1, yn)]
    sibling = me + 1 - 2 * core
    right = lax.rem(me + 1, n)
    left = lax.rem(me + n - 1, n)
    greeted = x_peers + y_peers + [left, right]
    x_order = sorted(range(1, xn), key=lambda d: -min(d, xn - d))
    y_order = sorted(range(1, yn), key=lambda e: -min(e, yn - e))

    barrier = pltpu.get_barrier_semaphore()
    for peer in greeted:
        pl.semaphore_signal(barrier, inc=1, device_id={"ctx": peer}, device_id_type=MESH)

    loads = [
        pltpu.make_async_copy(src, dst, load_sem.at[i])
        for i, (src, dst) in enumerate(
            (
                (pos_hbm, pos_scr),
                (q_hbm, q_ref),
                (k_hbm, kpad.at[own]),
                (v_hbm, vpad.at[own]),
                (do_hbm, do_ref),
            )
        )
    ]
    for load in loads:
        load.start()

    copies = []

    def send(src, dst, peer):
        number = len(copies)
        copy = pltpu.make_async_remote_copy(
            src_ref=src,
            dst_ref=dst,
            send_sem=send_sem.at[number],
            recv_sem=recv_sem.at[number],
            device_id={"ctx": peer},
            device_id_type=MESH,
        )
        copy.start()
        copies.append(copy)
        return copy

    stores = []

    def keep(src, dst):
        copy = pltpu.make_async_copy(src, dst, store_sem.at[len(stores)])
        copy.start()
        stores.append(copy)

    loads[0].wait()
    pos_r = pos_scr[...]
    first, second = iota((count, count), 0), iota((count, count), 1)
    pos_c = jnp.sum(jnp.where(first == second, pos_r.astype(F32), 0.0), axis=1, keepdims=True).astype(I32)
    owner_c, owner_r = pos_c >> tok_shift, pos_r >> tok_shift
    local_c, local_r = pos_c & (tok - 1), pos_r & (tok - 1)
    same = owner_c == owner_r
    rank_c = jnp.sum(jnp.where(same & (second < first), 1.0, 0.0), axis=1, keepdims=True).astype(I32)
    rank_r = jnp.sum(jnp.where(same & (first < second), 1.0, 0.0), axis=0, keepdims=True).astype(I32)

    rho = iota((2 * ROWS, count), 0)
    slot_rank = ((rho >> 4) << 2) + (rho & 3)
    chosen = (owner_r == me) & (rank_r == slot_rank)
    slot_col = jnp.sum(jnp.where(chosen, (local_r + 1).astype(F32), 0.0), axis=1, keepdims=True).astype(I32) - 1
    array_of = (iota((2 * ROWS, tok), 0) >> 2) & 3
    at_slot = iota((2 * ROWS, tok), 1) == slot_col
    picked = jnp.zeros((2 * ROWS, width), F32)
    for load in loads[1:]:
        load.wait()
    for a, rows in enumerate((q_ref[...], kpad[own, :], vpad[own, :], do_ref[...])):
        picked = picked + dot_nn(one_hot(at_slot & (array_of == a)), rows)
    pack[...] = picked.astype(BF16).reshape(2, ROWS, width)
    gx[0] = pack[...]

    pl.semaphore_wait(barrier, len(greeted))

    from_x = [send(pack, gx.at[d], x_peers[d - 1]) for d in x_order]
    halos = [
        send(kpad.at[own], kpad.at[pl.ds(0, HALF)], right),
        send(kpad.at[own], kpad.at[pl.ds(HALF + tok, HALF)], left),
        send(vpad.at[own], vpad.at[pl.ds(0, HALF)], right),
        send(vpad.at[own], vpad.at[pl.ds(HALF + tok, HALF)], left),
    ]

    dkpad[...] = jnp.zeros((window, width), F32)
    dvpad[...] = jnp.zeros((window, width), F32)
    for part in range(window // 512):
        reach = me * tok - HALF + part * 512 + iota((1, 512), 1)
        bias = jnp.min(jnp.where(pos_c == reach, NEG, 0.0), axis=0, keepdims=True)
        inside = (reach >= 0) & (reach < seq)
        colbias[:, pl.ds(part * 512, 512)] = jnp.where(inside, bias, NEG)
    row_pos = me * tok + iota((tok, 1), 0)
    flag = jnp.max(jnp.where(row_pos == pos_r, 1.0, 0.0), axis=1, keepdims=True)
    rowflag[...] = jnp.broadcast_to(flag, (tok, width))
    lgrad[...] = jnp.where(rowflag[...] > 0.5, 0.0, do_ref[...].astype(F32)).astype(BF16)

    for copy in from_x:
        copy.wait_recv()
    over = gx[0, 1].astype(F32)
    gath[0, 0, 0] = gx[0, 0]
    for d in range(1, xn):
        gath[0, 0, d] = gx[d, 0]
        over = over + gx[d, 1].astype(F32)
    gath[0, 0, xn] = over.astype(BF16)
    from_y = {e: send(gath.at[0, 0], gath.at[0, e], y_peers[e - 1]) for e in y_order}
    from_sib = [send(gath.at[0, 0], gath.at[1, 0], sibling)]

    core_c, xo_c, yo_c = owner_c & 1, (owner_c >> 1) & (xn - 1), owner_c >> (1 + x_shift)
    half_c = (core_c ^ core) * yn + ((yy - yo_c) & (yn - 1))
    src_c = jnp.where(
        rank_c < SLOTS,
        (half_c * (xn + 1) + ((xx - xo_c) & (xn - 1))) * ROWS + rank_c,
        (half_c * (xn + 1) + xn) * ROWS + rank_c - SLOTS,
    )
    total = 2 * yn * (xn + 1) * ROWS
    for a in range(4):
        pick[a] = one_hot(iota((count, total), 1) == src_c + SLOTS * a)

    core_r, xo_r, yo_r = owner_r & 1, (owner_r >> 1) & (xn - 1), owner_r >> (1 + x_shift)
    place = ((core_r ^ core) * xn + ((xo_r - xx) & (xn - 1))) * yn + ((yo_r - yy) & (yn - 1))
    beyond = 2 * xn * yn * SLOTS
    key_r = jnp.where(rank_r < SLOTS, place * SLOTS + rank_r, beyond + rank_r - SLOTS)
    spread[0] = one_hot(iota((beyond, count), 0) == key_r)
    turned = ((core_r ^ core) * yn + ((yo_r - yy) & (yn - 1))) * xn + ((xo_r - xx) & (xn - 1))
    turned_r = jnp.where(rank_r < SLOTS, turned * SLOTS + rank_r, beyond + rank_r - SLOTS)
    spread[1] = one_hot(iota((beyond, count), 0) == turned_r)
    spread_over[...] = jnp.where(beyond + (iota((ROWS, count), 0) & 3) == key_r, 1.0, 0.0)

    rho_lane = iota((count, TILE), 1)
    lane_rank = ((rho_lane >> 4) << 2) + (rho_lane & 3)
    chosen_c = (owner_c == me) & (rank_c == lane_rank) & (rho_lane < 2 * ROWS)
    slot_row = jnp.sum(jnp.where(chosen_c, (local_c + 1).astype(F32), 0.0), axis=0, keepdims=True).astype(I32) - 1
    hot_scr[...] = one_hot(iota((tok, TILE), 0) == slot_row)
    keep(hot_scr, hot_out)
    keep(rowflag, flag_out)

    for copy in halos:
        copy.wait_recv()

    lane = iota((TILE, TILE), 1)
    sub = iota((TILE, TILE), 0)
    low_bias = jnp.where(lane >= sub, 0.0, NEG)
    high_bias = jnp.where(lane <= sub, 0.0, NEG)

    def before(t, carry):
        start = pl.multiple_of(t * TILE, TILE)
        rows, keys = pl.ds(start, TILE), pl.ds(start, span)
        s = dot_nt(q_ref[rows, :], kpad[keys, :]) * scale + colbias[:, keys]
        s = jnp.concatenate(
            [s[:, :TILE] + low_bias, s[:, TILE : 2 * HALF], s[:, 2 * HALF :] + high_bias], axis=1
        )
        top = jnp.max(s, axis=1, keepdims=True)
        p = jnp.exp(s - top)
        p_scr[rows, :] = p
        ow_scr[rows, :] = dot_nn(p.astype(BF16), vpad[keys, :])
        m_scr[rows, :] = jnp.broadcast_to(top, (TILE, width))
        l_scr[rows, :] = jnp.broadcast_to(jnp.sum(p, axis=1, keepdims=True), (TILE, width))
        d_scr[rows, :] = dot_nt(lgrad[rows, :], vpad[keys, :])
        return carry

    lax.fori_loop(0, tiles, before, 0)

    for e in reversed(y_order):
        from_y[e].wait_recv()
        from_sib.append(send(gath.at[0, e], gath.at[1, e], sibling))
    for copy in from_sib:
        copy.wait_recv()
    everything = gath[...].reshape(total, width)
    for a in range(4):
        glob[a] = dot_nn(pick[a], everything).astype(BF16)

    middle = (jnp.sum(glob[2].astype(F32), axis=0, keepdims=True) * (1.0 / count)).astype(BF16)
    centre = dot_nt(jnp.broadcast_to(middle, (ROWS, width)), glob[3])[0:1, :]
    sg = dot_nt(kpad[own, :], glob[0]) * scale
    gw = dot_nt(vpad[own, :], glob[3]) - centre
    sg_scr[...] = sg
    gw_scr[...] = gw
    top = jnp.max(sg, axis=0, keepdims=True)
    p = jnp.exp(sg - top)
    stat_rows = [top, jnp.sum(p, axis=0, keepdims=True), jnp.sum(p * gw, axis=0, keepdims=True)]
    for r, row in enumerate(stat_rows):
        st_own[2 * r : 2 * r + 1, :] = row[:, :TILE]
        st_own[2 * r + 1 : 2 * r + 2, :] = row[:, TILE:]
    st_own[6:8, :] = jnp.zeros((2, TILE), F32)

    def join(parts):
        joined = functools.reduce(jnp.maximum, [part[0:2, :] for part in parts])
        weigh = [jnp.exp(part[0:2, :] - joined) for part in parts]
        return (
            joined,
            sum(part[2:4, :] * w for part, w in zip(parts, weigh)),
            sum(part[4:6, :] * w for part, w in zip(parts, weigh)),
        )

    def store(ref, stats):
        for r, part in enumerate(stats):
            ref[2 * r : 2 * r + 2, :] = part
        ref[6:8, :] = jnp.zeros((2, TILE), F32)

    def row_of(part):
        return jnp.concatenate([part[0:1], part[1:2]], axis=1)

    stat_sib = send(st_own, st_sib, sibling)

    lg = lgrad[...]
    s = dot_nt(q_ref[...], glob[1]) * scale
    top_w = m_scr[:, 0:1]
    top = jnp.maximum(top_w, jnp.max(s, axis=1, keepdims=True))
    pg = jnp.exp(s - top)
    down = jnp.exp(top_w - top)
    inv = 1.0 / (l_scr[:, 0:1] * down + jnp.sum(pg, axis=1, keepdims=True))
    pg = pg * inv
    pg16 = pg.astype(BF16)
    o = ow_scr[...] * (down * inv) + dot_nn(pg16, glob[2])
    o_scr[...] = o
    row_dot = jnp.sum(lg.astype(F32) * o, axis=1, keepdims=True)
    dsg = (pg * (dot_nt(lg, glob[2]) - row_dot)).astype(BF16)
    m_scr[...] = jnp.broadcast_to(down * inv, (tok, width))
    l_scr[...] = jnp.broadcast_to(row_dot, (tok, width))
    dkg = dot_tn(dsg, q_ref[...])
    dvg = dot_tn(pg16, lg)
    dq_scr[...] = dot_nn(dsg, glob[1])

    def after(t, carry):
        start = pl.multiple_of(t * TILE, TILE)
        rows, keys = pl.ds(start, TILE), pl.ds(start, span)
        pw = p_scr[rows, :] * m_scr[rows, 0:1]
        dsw = (pw * (d_scr[rows, :] - l_scr[rows, 0:1])).astype(BF16)
        dq_scr[rows, :] = (dq_scr[rows, :] + dot_nn(dsw, kpad[keys, :])) * scale
        dkpad[keys, :] += dot_tn(dsw, q_ref[rows, :])
        dvpad[keys, :] += dot_tn(pw.astype(BF16), lgrad[rows, :])
        return carry

    over_row = iota((ROWS, count), 0)

    def overflow(partial, arrays):
        z_over = jnp.zeros((ROWS, width), F32)
        for a in range(arrays):
            mine = jnp.where((over_row >> 2) == a, spread_over[...], 0.0).astype(BF16)
            z_over = z_over + dot_nn(mine, partial[:, a * width : (a + 1) * width])
        return z_over.astype(BF16)

    def paired(own_ref, sib_ref, groups, arrays, ref):
        over = (own_ref[0, arrays * groups].astype(F32) + sib_ref[arrays * groups].astype(F32)).astype(BF16)
        for d in range(groups):
            tiles_of = pl.ds(d * arrays, arrays)
            ref[d, 0:arrays] = (own_ref[0, tiles_of].astype(F32) + sib_ref[tiles_of].astype(F32)).astype(BF16)
            ref[d, arrays] = over

    deep = xn * SLOTS // ROWS
    partial = jnp.concatenate([dkg, dvg], axis=1).astype(BF16)
    z = dot_nn(spread[1], partial).astype(BF16)
    z_over = overflow(partial, 2)
    for half in range(2):
        for e in range(yn):
            base = (half * yn + e) * deep * ROWS
            for a in range(2):
                mine = z[base : base + deep * ROWS, a * width : (a + 1) * width]
                z2_own[half, (e * 2 + a) * deep : (e * 2 + a + 1) * deep] = mine.reshape(deep, ROWS, width)
        z2_own[half, 2 * deep * yn] = z_over
    z2_copy = send(z2_own.at[1], z2_sib, sibling)

    stat_sib.wait_recv()
    store(st_x, join([st_own[...], st_sib[...]]))
    stat_x = [send(st_x, st_xin.at[d - 1], x_peers[d - 1]) for d in x_order]

    pair_top = st_x[0:2, :]
    w = jnp.exp(sg_scr[...] - row_of(pair_top))
    w16 = w.astype(BF16)
    ds16 = (w * gw_scr[...]).astype(BF16)
    value_key = dot_tn(w16, jnp.concatenate([vpad[own, :], kpad[own, :]], axis=1))
    partial = [value_key[:, :width], dot_tn(ds16, kpad[own, :]), value_key[:, width:]]
    partial = jnp.concatenate(partial, axis=1).astype(BF16)
    z = dot_nn(spread[0], partial).astype(BF16)
    z_over = overflow(partial, 3)
    for half in range(2):
        for d in range(xn):
            base = (half * xn + d) * ROWS
            for a in range(3):
                z1_own[half, d * 3 + a] = z[base : base + ROWS, a * width : (a + 1) * width]
        z1_own[half, 3 * xn] = z_over
    z1_copy = send(z1_own.at[1], z1_sib, sibling)

    z2_copy.wait_recv()
    paired(z2_own, z2_sib, yn, 2 * deep, t2_own)
    t2_copies = [send(t2_own.at[e], t2_in.at[e - 1], y_peers[e - 1]) for e in y_order]
    keep(o_scr, o_out)
    z1_copy.wait_recv()
    paired(z1_own, z1_sib, xn, 3, t1_own)
    t1_copies = [send(t1_own.at[d], t1_in.at[d - 1], x_peers[d - 1]) for d in x_order]

    lax.fori_loop(0, tiles, after, 0)

    rim_out[0, 0] = dkpad[pl.ds(0, HALF), :].astype(BF16)
    rim_out[0, 1] = dvpad[pl.ds(0, HALF), :].astype(BF16)
    rim_out[1, 0] = dkpad[pl.ds(HALF + tok, HALF), :].astype(BF16)
    rim_out[1, 1] = dvpad[pl.ds(HALF + tok, HALF), :].astype(BF16)
    rims = [send(rim_out.at[1], rim_in.at[0], right), send(rim_out.at[0], rim_in.at[1], left)]
    keep(dq_scr, dq_out)

    for copy in stat_x:
        copy.wait_recv()
    store(st_y, join([st_x[...]] + [st_xin[d - 1] for d in range(1, xn)]))
    stat_y = [send(st_y, st_yin.at[e - 1], y_peers[e - 1]) for e in y_order]

    def arrange(groups, depth, wanted, overflow_at, places):
        goal, source = iota((groups * ROWS, places), 0), iota((groups * ROWS, places), 1)
        goal_to, goal_array, goal_slot = goal >> 4, (goal >> 2) & 1, goal & 3
        hit = jnp.zeros(goal.shape, F32)
        for array, tile in wanted:
            at = jnp.where(
                (goal & 15) >= 8,
                overflow_at + tile * SLOTS + goal_slot,
                tile * depth * ROWS + goal_to * SLOTS + goal_slot,
            )
            hit = hit + jnp.where((goal_array == array) & (source == at), 1.0, 0.0)
        return hit.astype(BF16)

    arrange_1 = arrange(yn, 1, ((0, 0), (1, 1), (1, 2)), 3 * ROWS, 4 * ROWS)
    arrange_2 = arrange(xn, deep, ((0, 0), (1, 1)), 2 * deep * ROWS, (2 * deep + 1) * ROWS)

    for copy in t2_copies:
        copy.wait_recv()
    column = t2_own[0].astype(F32)
    for e in range(1, yn):
        column = column + t2_in[e - 1].astype(F32)
    v = dot_nn(arrange_2, column.reshape((2 * deep + 1) * ROWS, width).astype(BF16)).astype(BF16)
    v_own[...] = v.reshape(xn, ROWS, width)
    v_copies = [send(v_own.at[d], v_in.at[d - 1], x_peers[d - 1]) for d in x_order]

    for copy in stat_y:
        copy.wait_recv()
    joined, summed, dotted = join([st_y[...]] + [st_yin[e - 1] for e in range(1, yn)])
    lse = row_of(joined + jnp.log(summed))
    ratio = row_of(dotted / summed)
    line = iota((4 * ROWS, count), 0)
    line_key = jnp.where(line < 3 * ROWS, line & (ROWS - 1), beyond + (line & 3))
    kind = jnp.where(line < 3 * ROWS, line >> 4, (line >> 2) & 3)
    found = jnp.where(line_key == key_r, 1.0, 0.0)
    found = found * jnp.where(kind == 2, -ratio, jnp.where(kind == 3, 0.0, 1.0))
    column = jnp.zeros((4 * ROWS, width), F32)
    for d in range(xn):
        pair = st_x[0:2, :] if d == 0 else st_xin[d - 1, 0:2, :]
        fall = row_of(jnp.exp(pair - joined) / summed)
        factor = jnp.sum(found * fall, axis=1, keepdims=True)
        f_scr[d] = jnp.broadcast_to(factor, (4 * ROWS, width))

    for copy in t1_copies:
        copy.wait_recv()
    for d in range(xn):
        mine = t1_own[0] if d == 0 else t1_in[d - 1]
        column = column + mine.astype(F32).reshape(4 * ROWS, width) * f_scr[d]
    upper = column.astype(BF16)
    lower = (column - upper.astype(F32)).astype(BF16)
    u = (dot_nn(arrange_1, upper) + dot_nn(arrange_1, lower)).astype(BF16)
    u_own[...] = u.reshape(yn, ROWS, width)
    u_copies = [send(u_own.at[e], u_in.at[e - 1], y_peers[e - 1]) for e in y_order]

    w = jnp.exp(sg_scr[...] - lse)
    dv_sum = dvpad[own, :] + dot_nn(w.astype(BF16), glob[3])
    dk_sum = dkpad[own, :] + dot_nn((w * (gw_scr[...] - ratio)).astype(BF16), glob[0])
    for copy in rims:
        copy.wait_recv()
    for side in range(2):
        dk_sum = dk_sum + rim_in[side, 0].astype(F32)
        dv_sum = dv_sum + rim_in[side, 1].astype(F32)
    dkown[...] = dk_sum * scale
    dvown[...] = dv_sum
    keep(dkown, dk_out)
    keep(dvown, dv_out)

    for copy in v_copies:
        copy.wait_recv()
    late = v_own[0].astype(F32)
    for d in range(1, xn):
        late = late + v_in[d - 1].astype(F32)
    for copy in u_copies:
        copy.wait_recv()
    early = u_own[0].astype(F32)
    for e in range(1, yn):
        early = early + u_in[e - 1].astype(F32)
    for part in range(2):
        r_scr[part * ROWS : part * ROWS + 8, :] = early[part * 8 : part * 8 + 8]
        r_scr[part * ROWS + 8 : part * ROWS + 16, :] = late[part * 8 : part * 8 + 8]
    keep(r_scr, r_out)

    for copy in stores:
        copy.wait()
    for copy in copies:
        copy.wait_send()


def finish(scale, o_ref, dq_in, dk_in, dv_in, hot_ref, flag_ref, r_ref, out_ref, dq_ref, dk_ref, dv_ref, total):
    tok = o_ref.shape[0]
    total[...] = jnp.zeros_like(total)
    total[0 : 2 * ROWS, :] = r_ref[...]
    upper = total[...].astype(BF16)
    lower = (total[...] - upper.astype(F32)).astype(BF16)
    hot = hot_ref[...].astype(F32)
    lane_array = (iota((tok, TILE), 1) >> 2) & 3

    def placed(a):
        mine = jnp.where(lane_array == a, hot, 0.0).astype(BF16)
        return dot_nn(mine, upper) + dot_nn(mine, lower)

    out_ref[...] = jnp.where(flag_ref[...] > 0.5, placed(0), o_ref[...]).astype(BF16)
    dq_ref[...] = dq_in[...] + placed(1) * scale
    dk_ref[...] = dk_in[...] + placed(2) * scale
    dv_ref[...] = dv_in[...] + placed(3)


def shards(n, query_rows, key_rows, value_rows, out_grad, global_pos):
    tok, _, width = query_rows.shape
    count = global_pos.shape[0]
    yn = 4
    xn = n // (2 * yn)
    deep = xn * SLOTS // ROWS
    window = tok + 2 * HALF
    span = TILE + 2 * HALF
    copies = 4 * (xn - 1) + 4 * (yn - 1) + 16
    vmem = pl.BlockSpec(memory_space=pltpu.VMEM)
    anywhere = pl.BlockSpec(memory_space=pl.ANY)
    flat = [x.reshape(tok, width) for x in (query_rows, key_rows, value_rows, out_grad)]
    rows_f32 = jax.ShapeDtypeStruct((tok, width), F32)
    middle = pl.pallas_call(
        functools.partial(kernel, (n, yn, xn, tok, count, width)),
        name="sparse_attention",
        out_shape=(rows_f32,) * 4
        + (
            jax.ShapeDtypeStruct((tok, TILE), BF16),
            rows_f32,
            jax.ShapeDtypeStruct((2 * ROWS, width), F32),
        ),
        in_specs=[pl.BlockSpec(memory_space=pltpu.HBM)] * 5,
        out_specs=(anywhere,) * 7,
        scratch_shapes=[
            pltpu.VMEM((1, count), I32),
            pltpu.VMEM((tok, width), BF16),
            pltpu.VMEM((tok, width), BF16),
            pltpu.VMEM((window, width), BF16),
            pltpu.VMEM((window, width), BF16),
            pltpu.VMEM((tok, width), BF16),
            pltpu.VMEM((1, window), F32),
            pltpu.VMEM((tok, width), F32),
            pltpu.VMEM((2, ROWS, width), BF16),
            pltpu.VMEM((xn, 2, ROWS, width), BF16),
            pltpu.VMEM((2, yn, xn + 1, ROWS, width), BF16),
            pltpu.VMEM((4, count, 2 * yn * (xn + 1) * ROWS), BF16),
            pltpu.VMEM((4, count, width), BF16),
            pltpu.VMEM((tok, span), F32),
            pltpu.VMEM((tok, width), F32),
            pltpu.VMEM((tok, span), F32),
            pltpu.VMEM((tok, width), F32),
            pltpu.VMEM((tok, width), F32),
            pltpu.VMEM((tok, width), F32),
            pltpu.VMEM((tok, width), F32),
            pltpu.VMEM((window, width), F32),
            pltpu.VMEM((window, width), F32),
            pltpu.VMEM((tok, count), F32),
            pltpu.VMEM((tok, count), F32),
            pltpu.VMEM((8, TILE), F32),
            pltpu.VMEM((8, TILE), F32),
            pltpu.VMEM((8, TILE), F32),
            pltpu.VMEM((xn - 1, 8, TILE), F32),
            pltpu.VMEM((8, TILE), F32),
            pltpu.VMEM((yn - 1, 8, TILE), F32),
            pltpu.VMEM((tok, width), F32),
            pltpu.VMEM((tok, width), F32),
            pltpu.VMEM((2, 2 * xn * yn * SLOTS, count), BF16),
            pltpu.VMEM((ROWS, count), F32),
            pltpu.VMEM((tok, TILE), BF16),
            pltpu.VMEM((2, 3 * xn + 1, ROWS, width), BF16),
            pltpu.VMEM((3 * xn + 1, ROWS, width), BF16),
            pltpu.VMEM((xn, 4, ROWS, width), BF16),
            pltpu.VMEM((xn - 1, 4, ROWS, width), BF16),
            pltpu.VMEM((2, 2 * deep * yn + 1, ROWS, width), BF16),
            pltpu.VMEM((2 * deep * yn + 1, ROWS, width), BF16),
            pltpu.VMEM((yn, 2 * deep + 1, ROWS, width), BF16),
            pltpu.VMEM((yn - 1, 2 * deep + 1, ROWS, width), BF16),
            pltpu.VMEM((xn, 4 * ROWS, width), F32),
            pltpu.VMEM((yn, ROWS, width), BF16),
            pltpu.VMEM((yn - 1, ROWS, width), BF16),
            pltpu.VMEM((xn, ROWS, width), BF16),
            pltpu.VMEM((xn - 1, ROWS, width), BF16),
            pltpu.VMEM((2 * ROWS, width), F32),
            pltpu.VMEM((2, 2, HALF, width), BF16),
            pltpu.VMEM((2, 2, HALF, width), BF16),
            pltpu.SemaphoreType.DMA((copies,)),
            pltpu.SemaphoreType.DMA((copies,)),
            pltpu.SemaphoreType.DMA((5,)),
            pltpu.SemaphoreType.DMA((7,)),
        ],
        compiler_params=pltpu.CompilerParams(
            collective_id=0, has_side_effects=True, vmem_limit_bytes=24 << 20
        ),
    )(*[pltpu.with_memory_space_constraint(x, pltpu.HBM) for x in (global_pos.reshape(1, count), *flat)])
    results = pl.pallas_call(
        functools.partial(finish, width**-0.5),
        name="place_global_rows",
        out_shape=(jax.ShapeDtypeStruct((tok, width), BF16),) + (rows_f32,) * 3,
        in_specs=[vmem] * 7,
        out_specs=(vmem,) * 4,
        scratch_shapes=[pltpu.VMEM((TILE, width), F32)],
        compiler_params=pltpu.CompilerParams(vmem_limit_bytes=8 << 20),
    )(*middle)
    return tuple(x.reshape(tok, 1, width) for x in results)


def solution(mesh):
    rows = P("ctx", "head", None)
    return jax.shard_map(
        functools.partial(shards, mesh.shape["ctx"]),
        mesh=mesh,
        in_specs=(rows,) * 4 + (P(),),
        out_specs=(rows,) * 4,
        check_vma=False,
    )
```

```python
import functools

import jax
import jax.numpy as jnp
from jax import lax
from jax.experimental import pallas as pl
from jax.experimental.pallas import tpu as pltpu
from jax.sharding import PartitionSpec as P

MESH = pl.DeviceIdType.MESH
HALF = 512
TILE = 128
SLOTS = 4
ROWS = 16
NEG = -1e30
F32 = jnp.float32
BF16 = jnp.bfloat16
I32 = jnp.int32


def dot_nn(a, b):
    return lax.dot_general(a, b, (((1,), (0,)), ((), ())), preferred_element_type=F32)


def dot_nt(a, b):
    return lax.dot_general(a, b, (((1,), (1,)), ((), ())), preferred_element_type=F32)


def dot_tn(a, b):
    return lax.dot_general(a, b, (((0,), (0,)), ((), ())), preferred_element_type=F32)


def iota(shape, dim):
    return lax.broadcasted_iota(I32, shape, dim)


def one_hot(cond):
    return jnp.where(cond, 1.0, 0.0).astype(BF16)


def kernel(
    sizes,
    pos_hbm,
    q_hbm,
    k_hbm,
    v_hbm,
    do_hbm,
    o_out,
    dq_out,
    dk_out,
    dv_out,
    hot_out,
    flag_out,
    r_out,
    pos_scr,
    qpad,
    dopad,
    kpad,
    vpad,
    lgrad,
    colbias,
    rowflag,
    pack,
    gx,
    gath,
    pick,
    glob,
    p_scr,
    ow_scr,
    d_scr,
    m_scr,
    l_scr,
    o_scr,
    dq_scr,
    sg_scr,
    gw_scr,
    st_own,
    st_sib,
    st_x,
    st_xin,
    st_y,
    st_yin,
    dkown,
    dvown,
    spread,
    spread_over,
    hot_scr,
    z1_own,
    z1_sib,
    t1_own,
    t1_in,
    z2_own,
    z2_sib,
    t2_own,
    t2_in,
    f_scr,
    u_own,
    u_in,
    v_own,
    v_in,
    r_scr,
    near_out,
    near_in,
    send_sem,
    recv_sem,
    load_sem,
    store_sem,
):
    n, yn, xn, tok, count, width = sizes
    seq = n * tok
    scale = width**-0.5
    x_shift = xn.bit_length() - 1
    tok_shift = tok.bit_length() - 1
    window = tok + 2 * HALF
    span = TILE + 2 * HALF
    tiles = tok // TILE
    own = pl.ds(HALF, tok)

    me = lax.axis_index("ctx")
    core = lax.rem(me, 2)
    xx = lax.rem(lax.div(me, 2), xn)
    yy = lax.div(me, 2 * xn)

    def ctx_id(y, x, c):
        return (y * xn + x) * 2 + c

    x_peers = [ctx_id(yy, lax.rem(xx + d, xn), core) for d in range(1, xn)]
    y_peers = [ctx_id(lax.rem(yy + e, yn), xx, core) for e in range(1, yn)]
    sibling = me + 1 - 2 * core
    right = lax.rem(me + 1, n)
    left = lax.rem(me + n - 1, n)
    greeted = x_peers + y_peers + [left, right]
    x_order = sorted(range(1, xn), key=lambda d: -min(d, xn - d))
    y_order = sorted(range(1, yn), key=lambda e: -min(e, yn - e))

    barrier = pltpu.get_barrier_semaphore()
    for peer in greeted:
        pl.semaphore_signal(barrier, inc=1, device_id={"ctx": peer}, device_id_type=MESH)

    loads = [
        pltpu.make_async_copy(src, dst, load_sem.at[i])
        for i, (src, dst) in enumerate(
            (
                (pos_hbm, pos_scr),
                (q_hbm, qpad.at[own]),
                (k_hbm, kpad.at[own]),
                (v_hbm, vpad.at[own]),
                (do_hbm, dopad.at[own]),
            )
        )
    ]
    for load in loads:
        load.start()

    copies = []

    def send(src, dst, peer):
        number = len(copies)
        copy = pltpu.make_async_remote_copy(
            src_ref=src,
            dst_ref=dst,
            send_sem=send_sem.at[number],
            recv_sem=recv_sem.at[number],
            device_id={"ctx": peer},
            device_id_type=MESH,
        )
        copy.start()
        copies.append(copy)
        return copy

    stores = []

    def keep(src, dst):
        copy = pltpu.make_async_copy(src, dst, store_sem.at[len(stores)])
        copy.start()
        stores.append(copy)

    loads[0].wait()
    pos_r = pos_scr[...]
    first, second = iota((count, count), 0), iota((count, count), 1)
    pos_c = jnp.sum(jnp.where(first == second, pos_r.astype(F32), 0.0), axis=1, keepdims=True).astype(I32)
    owner_c, owner_r = pos_c >> tok_shift, pos_r >> tok_shift
    local_c, local_r = pos_c & (tok - 1), pos_r & (tok - 1)
    same = owner_c == owner_r
    rank_c = jnp.sum(jnp.where(same & (second < first), 1.0, 0.0), axis=1, keepdims=True).astype(I32)
    rank_r = jnp.sum(jnp.where(same & (first < second), 1.0, 0.0), axis=0, keepdims=True).astype(I32)

    rho = iota((2 * ROWS, count), 0)
    slot_rank = ((rho >> 4) << 2) + (rho & 3)
    chosen = (owner_r == me) & (rank_r == slot_rank)
    slot_col = jnp.sum(jnp.where(chosen, (local_r + 1).astype(F32), 0.0), axis=1, keepdims=True).astype(I32) - 1
    array_of = (iota((2 * ROWS, tok), 0) >> 2) & 3
    at_slot = iota((2 * ROWS, tok), 1) == slot_col
    picked = jnp.zeros((2 * ROWS, width), F32)
    for load in loads[1:]:
        load.wait()
    for a, rows in enumerate((qpad[own, :], kpad[own, :], vpad[own, :], dopad[own, :])):
        picked = picked + dot_nn(one_hot(at_slot & (array_of == a)), rows)
    pack[...] = picked.astype(BF16).reshape(2, ROWS, width)
    gx[0] = pack[...]

    pl.semaphore_wait(barrier, len(greeted))

    from_x = [send(pack, gx.at[d], x_peers[d - 1]) for d in x_order]
    halos = [
        send(kpad.at[own], kpad.at[pl.ds(0, HALF)], right),
        send(kpad.at[own], kpad.at[pl.ds(HALF + tok, HALF)], left),
        send(vpad.at[own], vpad.at[pl.ds(0, HALF)], right),
        send(vpad.at[own], vpad.at[pl.ds(HALF + tok, HALF)], left),
    ]
    far_halos = [
        send(qpad.at[own], qpad.at[pl.ds(0, HALF)], right),
        send(qpad.at[own], qpad.at[pl.ds(HALF + tok, HALF)], left),
        send(dopad.at[own], dopad.at[pl.ds(0, HALF)], right),
        send(dopad.at[own], dopad.at[pl.ds(HALF + tok, HALF)], left),
    ]

    for part in range(window // 512):
        reach = me * tok - HALF + part * 512 + iota((1, 512), 1)
        bias = jnp.min(jnp.where(pos_c == reach, NEG, 0.0), axis=0, keepdims=True)
        inside = (reach >= 0) & (reach < seq)
        colbias[:, pl.ds(part * 512, 512)] = jnp.where(inside, bias, NEG)
    row_pos = me * tok + iota((tok, 1), 0)
    flag = jnp.max(jnp.where(row_pos == pos_r, 1.0, 0.0), axis=1, keepdims=True)
    rowflag[...] = jnp.broadcast_to(flag, (tok, width))
    lgrad[...] = jnp.where(rowflag[...] > 0.5, 0.0, dopad[own, :].astype(F32)).astype(BF16)

    for copy in from_x:
        copy.wait_recv()
    over = gx[0, 1].astype(F32)
    gath[0, 0, 0] = gx[0, 0]
    for d in range(1, xn):
        gath[0, 0, d] = gx[d, 0]
        over = over + gx[d, 1].astype(F32)
    gath[0, 0, xn] = over.astype(BF16)
    from_y = {e: send(gath.at[0, 0], gath.at[0, e], y_peers[e - 1]) for e in y_order}
    from_sib = [send(gath.at[0, 0], gath.at[1, 0], sibling)]

    core_c, xo_c, yo_c = owner_c & 1, (owner_c >> 1) & (xn - 1), owner_c >> (1 + x_shift)
    half_c = (core_c ^ core) * yn + ((yy - yo_c) & (yn - 1))
    src_c = jnp.where(
        rank_c < SLOTS,
        (half_c * (xn + 1) + ((xx - xo_c) & (xn - 1))) * ROWS + rank_c,
        (half_c * (xn + 1) + xn) * ROWS + rank_c - SLOTS,
    )
    total = 2 * yn * (xn + 1) * ROWS
    for a in range(4):
        pick[a] = one_hot(iota((count, total), 1) == src_c + SLOTS * a)

    core_r, xo_r, yo_r = owner_r & 1, (owner_r >> 1) & (xn - 1), owner_r >> (1 + x_shift)
    place = ((core_r ^ core) * xn + ((xo_r - xx) & (xn - 1))) * yn + ((yo_r - yy) & (yn - 1))
    beyond = 2 * xn * yn * SLOTS
    key_r = jnp.where(rank_r < SLOTS, place * SLOTS + rank_r, beyond + rank_r - SLOTS)
    spread[0] = one_hot(iota((beyond, count), 0) == key_r)
    turned = ((core_r ^ core) * yn + ((yo_r - yy) & (yn - 1))) * xn + ((xo_r - xx) & (xn - 1))
    turned_r = jnp.where(rank_r < SLOTS, turned * SLOTS + rank_r, beyond + rank_r - SLOTS)
    spread[1] = one_hot(iota((beyond, count), 0) == turned_r)
    spread_over[...] = jnp.where(beyond + (iota((ROWS, count), 0) & 3) == key_r, 1.0, 0.0)

    rho_lane = iota((count, TILE), 1)
    lane_rank = ((rho_lane >> 4) << 2) + (rho_lane & 3)
    chosen_c = (owner_c == me) & (rank_c == lane_rank) & (rho_lane < 2 * ROWS)
    slot_row = jnp.sum(jnp.where(chosen_c, (local_c + 1).astype(F32), 0.0), axis=0, keepdims=True).astype(I32) - 1
    hot_scr[...] = one_hot(iota((tok, TILE), 0) == slot_row)
    keep(hot_scr, hot_out)
    keep(rowflag, flag_out)

    for copy in halos:
        copy.wait_recv()

    lane = iota((TILE, TILE), 1)
    sub = iota((TILE, TILE), 0)
    low_bias = jnp.where(lane >= sub, 0.0, NEG)
    high_bias = jnp.where(lane <= sub, 0.0, NEG)

    def before(t, carry):
        start = pl.multiple_of(t * TILE, TILE)
        rows, keys = pl.ds(start, TILE), pl.ds(start, span)
        s = dot_nt(qpad[pl.ds(HALF + start, TILE), :], kpad[keys, :]) * scale + colbias[:, keys]
        s = jnp.concatenate(
            [s[:, :TILE] + low_bias, s[:, TILE : 2 * HALF], s[:, 2 * HALF :] + high_bias], axis=1
        )
        top = jnp.max(s, axis=1, keepdims=True)
        p = jnp.exp(s - top)
        p_scr[rows, :] = p
        ow_scr[rows, :] = dot_nn(p.astype(BF16), vpad[keys, :])
        m_scr[rows, :] = jnp.broadcast_to(top, (TILE, width))
        l_scr[rows, :] = jnp.broadcast_to(jnp.sum(p, axis=1, keepdims=True), (TILE, width))
        d_scr[rows, :] = dot_nt(lgrad[rows, :], vpad[keys, :])
        return carry

    lax.fori_loop(0, tiles, before, 0)

    for e in reversed(y_order):
        from_y[e].wait_recv()
        from_sib.append(send(gath.at[0, e], gath.at[1, e], sibling))
    for copy in from_sib:
        copy.wait_recv()
    everything = gath[...].reshape(total, width)
    for a in range(4):
        glob[a] = dot_nn(pick[a], everything).astype(BF16)

    middle = (jnp.sum(glob[2].astype(F32), axis=0, keepdims=True) * (1.0 / count)).astype(BF16)
    centre = dot_nt(jnp.broadcast_to(middle, (ROWS, width)), glob[3])[0:1, :]
    sg = dot_nt(kpad[own, :], glob[0]) * scale
    gw = dot_nt(vpad[own, :], glob[3]) - centre
    sg_scr[...] = sg
    gw_scr[...] = gw
    top = jnp.max(sg, axis=0, keepdims=True)
    p = jnp.exp(sg - top)
    stat_rows = [top, jnp.sum(p, axis=0, keepdims=True), jnp.sum(p * gw, axis=0, keepdims=True)]
    for r, row in enumerate(stat_rows):
        st_own[2 * r : 2 * r + 1, :] = row[:, :TILE]
        st_own[2 * r + 1 : 2 * r + 2, :] = row[:, TILE:]
    st_own[6:8, :] = jnp.zeros((2, TILE), F32)

    def join(parts):
        joined = functools.reduce(jnp.maximum, [part[0:2, :] for part in parts])
        weigh = [jnp.exp(part[0:2, :] - joined) for part in parts]
        return (
            joined,
            sum(part[2:4, :] * w for part, w in zip(parts, weigh)),
            sum(part[4:6, :] * w for part, w in zip(parts, weigh)),
        )

    def store(ref, stats):
        for r, part in enumerate(stats):
            ref[2 * r : 2 * r + 2, :] = part
        ref[6:8, :] = jnp.zeros((2, TILE), F32)

    def row_of(part):
        return jnp.concatenate([part[0:1], part[1:2]], axis=1)

    stat_sib = send(st_own, st_sib, sibling)

    lg = lgrad[...]
    s = dot_nt(qpad[own, :], glob[1]) * scale
    top_w = m_scr[:, 0:1]
    top = jnp.maximum(top_w, jnp.max(s, axis=1, keepdims=True))
    pg = jnp.exp(s - top)
    down = jnp.exp(top_w - top)
    all_sum = l_scr[:, 0:1] * down + jnp.sum(pg, axis=1, keepdims=True)
    inv = 1.0 / all_sum
    pg = pg * inv
    pg16 = pg.astype(BF16)
    o = ow_scr[...] * (down * inv) + dot_nn(pg16, glob[2])
    o_scr[...] = o
    row_dot = jnp.sum(lg.astype(F32) * o, axis=1, keepdims=True)
    dsg = (pg * (dot_nt(lg, glob[2]) - row_dot)).astype(BF16)
    m_scr[...] = jnp.broadcast_to(down * inv, (tok, width))
    l_scr[...] = jnp.broadcast_to(row_dot, (tok, width))
    dkg = dot_tn(dsg, qpad[own, :])
    dvg = dot_tn(pg16, lg)
    dq_scr[...] = dot_nn(dsg, glob[1])

    row_lse = jnp.where(rowflag[:, 0:1] > 0.5, -NEG, top + jnp.log(all_sum))
    for t in range(tiles):
        for r, column in enumerate((row_lse, row_dot)):
            mine = column[t * TILE : (t + 1) * TILE]
            near_out[r * tiles + t : r * tiles + t + 1, :] = jnp.sum(
                jnp.where(lane == sub, mine, 0.0), axis=0, keepdims=True
            )
    near = [send(near_out, near_in.at[0], right), send(near_out, near_in.at[1], left)]

    def after():
        dk = jnp.zeros((tok, width), F32)
        dv = jnp.zeros((tok, width), F32)
        for t in range(tiles):
            start = t * TILE
            rows, keys = pl.ds(start, TILE), pl.ds(start, span)
            pw = p_scr[rows, :] * m_scr[rows, 0:1]
            dsw = (pw * (d_scr[rows, :] - l_scr[rows, 0:1])).astype(BF16)
            dq_scr[rows, :] = (dq_scr[rows, :] + dot_nn(dsw, kpad[keys, :])) * scale
            first_own = HALF - start
            dk = dk + dot_tn(dsw[:, first_own : first_own + tok], qpad[pl.ds(HALF + start, TILE), :])
            dv = dv + dot_tn(pw[:, first_own : first_own + tok].astype(BF16), lgrad[rows, :])
        dkown[...] = dk
        dvown[...] = dv

    def from_neighbour(side):
        rows = pl.ds(side * (HALF + tok), HALF)
        key_at, query_at = iota((tok, HALF), 0), iota((tok, HALF), 1)
        within = key_at <= query_at if side == 0 else key_at >= query_at
        there = me > 0 if side == 0 else me < n - 1
        outside = jnp.where(there, 0.0, -NEG)
        lse_n = jnp.concatenate([near_in[side, t : t + 1, :] for t in range(tiles)], axis=1)
        dot_n = jnp.concatenate([near_in[side, tiles + t : tiles + t + 1, :] for t in range(tiles)], axis=1)
        s = dot_nt(kpad[own, :], qpad[rows, :]) * scale
        s = jnp.where(within, s, NEG) + jnp.where(rowflag[:, 0:1] > 0.5, NEG, 0.0)
        p = jnp.exp(s - (lse_n + outside))
        ds = (p * (dot_nt(vpad[own, :], dopad[rows, :]) - dot_n)).astype(BF16)
        dkown[...] += dot_nn(ds, qpad[rows, :])
        dvown[...] += dot_nn(p.astype(BF16), dopad[rows, :])

    over_row = iota((ROWS, count), 0)

    def overflow(partial, arrays):
        z_over = jnp.zeros((ROWS, width), F32)
        for a in range(arrays):
            mine = jnp.where((over_row >> 2) == a, spread_over[...], 0.0).astype(BF16)
            z_over = z_over + dot_nn(mine, partial[:, a * width : (a + 1) * width])
        return z_over.astype(BF16)

    def paired(own_ref, sib_ref, groups, arrays, ref):
        over = (own_ref[0, arrays * groups].astype(F32) + sib_ref[arrays * groups].astype(F32)).astype(BF16)
        for d in range(groups):
            tiles_of = pl.ds(d * arrays, arrays)
            ref[d, 0:arrays] = (own_ref[0, tiles_of].astype(F32) + sib_ref[tiles_of].astype(F32)).astype(BF16)
            ref[d, arrays] = over

    deep = xn * SLOTS // ROWS
    partial = jnp.concatenate([dkg, dvg], axis=1).astype(BF16)
    z = dot_nn(spread[1], partial).astype(BF16)
    z_over = overflow(partial, 2)
    for half in range(2):
        for e in range(yn):
            base = (half * yn + e) * deep * ROWS
            for a in range(2):
                mine = z[base : base + deep * ROWS, a * width : (a + 1) * width]
                z2_own[half, (e * 2 + a) * deep : (e * 2 + a + 1) * deep] = mine.reshape(deep, ROWS, width)
        z2_own[half, 2 * deep * yn] = z_over
    z2_copy = send(z2_own.at[1], z2_sib, sibling)

    stat_sib.wait_recv()
    store(st_x, join([st_own[...], st_sib[...]]))
    stat_x = [send(st_x, st_xin.at[d - 1], x_peers[d - 1]) for d in x_order]

    pair_top = st_x[0:2, :]
    w = jnp.exp(sg_scr[...] - row_of(pair_top))
    w16 = w.astype(BF16)
    ds16 = (w * gw_scr[...]).astype(BF16)
    value_key = dot_tn(w16, jnp.concatenate([vpad[own, :], kpad[own, :]], axis=1))
    partial = [value_key[:, :width], dot_tn(ds16, kpad[own, :]), value_key[:, width:]]
    partial = jnp.concatenate(partial, axis=1).astype(BF16)
    z = dot_nn(spread[0], partial).astype(BF16)
    z_over = overflow(partial, 3)
    for half in range(2):
        for d in range(xn):
            base = (half * xn + d) * ROWS
            for a in range(3):
                z1_own[half, d * 3 + a] = z[base : base + ROWS, a * width : (a + 1) * width]
        z1_own[half, 3 * xn] = z_over
    z1_copy = send(z1_own.at[1], z1_sib, sibling)

    z2_copy.wait_recv()
    paired(z2_own, z2_sib, yn, 2 * deep, t2_own)
    t2_copies = [send(t2_own.at[e], t2_in.at[e - 1], y_peers[e - 1]) for e in y_order]
    keep(o_scr, o_out)
    z1_copy.wait_recv()
    paired(z1_own, z1_sib, xn, 3, t1_own)
    t1_copies = [send(t1_own.at[d], t1_in.at[d - 1], x_peers[d - 1]) for d in x_order]

    after()
    keep(dq_scr, dq_out)

    for copy in stat_x:
        copy.wait_recv()
    store(st_y, join([st_x[...]] + [st_xin[d - 1] for d in range(1, xn)]))
    stat_y = [send(st_y, st_yin.at[e - 1], y_peers[e - 1]) for e in y_order]

    def arrange(groups, depth, wanted, overflow_at, places):
        goal, source = iota((groups * ROWS, places), 0), iota((groups * ROWS, places), 1)
        goal_to, goal_array, goal_slot = goal >> 4, (goal >> 2) & 1, goal & 3
        hit = jnp.zeros(goal.shape, F32)
        for array, tile in wanted:
            at = jnp.where(
                (goal & 15) >= 8,
                overflow_at + tile * SLOTS + goal_slot,
                tile * depth * ROWS + goal_to * SLOTS + goal_slot,
            )
            hit = hit + jnp.where((goal_array == array) & (source == at), 1.0, 0.0)
        return hit.astype(BF16)

    arrange_1 = arrange(yn, 1, ((0, 0), (1, 1), (1, 2)), 3 * ROWS, 4 * ROWS)
    arrange_2 = arrange(xn, deep, ((0, 0), (1, 1)), 2 * deep * ROWS, (2 * deep + 1) * ROWS)

    for copy in t2_copies:
        copy.wait_recv()
    column = t2_own[0].astype(F32)
    for e in range(1, yn):
        column = column + t2_in[e - 1].astype(F32)
    v = dot_nn(arrange_2, column.reshape((2 * deep + 1) * ROWS, width).astype(BF16)).astype(BF16)
    v_own[...] = v.reshape(xn, ROWS, width)
    v_copies = [send(v_own.at[d], v_in.at[d - 1], x_peers[d - 1]) for d in x_order]

    for copy in far_halos + near:
        copy.wait_recv()
    from_neighbour(0)
    from_neighbour(1)

    for copy in stat_y:
        copy.wait_recv()
    joined, summed, dotted = join([st_y[...]] + [st_yin[e - 1] for e in range(1, yn)])
    lse = row_of(joined + jnp.log(summed))
    ratio = row_of(dotted / summed)
    line = iota((4 * ROWS, count), 0)
    line_key = jnp.where(line < 3 * ROWS, line & (ROWS - 1), beyond + (line & 3))
    kind = jnp.where(line < 3 * ROWS, line >> 4, (line >> 2) & 3)
    found = jnp.where(line_key == key_r, 1.0, 0.0)
    found = found * jnp.where(kind == 2, -ratio, jnp.where(kind == 3, 0.0, 1.0))
    column = jnp.zeros((4 * ROWS, width), F32)
    for d in range(xn):
        pair = st_x[0:2, :] if d == 0 else st_xin[d - 1, 0:2, :]
        fall = row_of(jnp.exp(pair - joined) / summed)
        factor = jnp.sum(found * fall, axis=1, keepdims=True)
        f_scr[d] = jnp.broadcast_to(factor, (4 * ROWS, width))

    for copy in t1_copies:
        copy.wait_recv()
    for d in range(xn):
        mine = t1_own[0] if d == 0 else t1_in[d - 1]
        column = column + mine.astype(F32).reshape(4 * ROWS, width) * f_scr[d]
    upper = column.astype(BF16)
    lower = (column - upper.astype(F32)).astype(BF16)
    u = (dot_nn(arrange_1, upper) + dot_nn(arrange_1, lower)).astype(BF16)
    u_own[...] = u.reshape(yn, ROWS, width)
    u_copies = [send(u_own.at[e], u_in.at[e - 1], y_peers[e - 1]) for e in y_order]

    w = jnp.exp(sg_scr[...] - lse)
    dvown[...] += dot_nn(w.astype(BF16), glob[3])
    dkown[...] = (dkown[...] + dot_nn((w * (gw_scr[...] - ratio)).astype(BF16), glob[0])) * scale
    keep(dkown, dk_out)
    keep(dvown, dv_out)

    for copy in v_copies:
        copy.wait_recv()
    late = v_own[0].astype(F32)
    for d in range(1, xn):
        late = late + v_in[d - 1].astype(F32)
    for copy in u_copies:
        copy.wait_recv()
    early = u_own[0].astype(F32)
    for e in range(1, yn):
        early = early + u_in[e - 1].astype(F32)
    for part in range(2):
        r_scr[part * ROWS : part * ROWS + 8, :] = early[part * 8 : part * 8 + 8]
        r_scr[part * ROWS + 8 : part * ROWS + 16, :] = late[part * 8 : part * 8 + 8]
    keep(r_scr, r_out)

    for copy in stores:
        copy.wait()
    for copy in copies:
        copy.wait_send()


def finish(scale, o_ref, dq_in, dk_in, dv_in, hot_ref, flag_ref, r_ref, out_ref, dq_ref, dk_ref, dv_ref, total):
    tok = o_ref.shape[0]
    total[...] = jnp.zeros_like(total)
    total[0 : 2 * ROWS, :] = r_ref[...]
    upper = total[...].astype(BF16)
    lower = (total[...] - upper.astype(F32)).astype(BF16)
    hot = hot_ref[...].astype(F32)
    lane_array = (iota((tok, TILE), 1) >> 2) & 3

    def placed(a):
        mine = jnp.where(lane_array == a, hot, 0.0).astype(BF16)
        return dot_nn(mine, upper) + dot_nn(mine, lower)

    out_ref[...] = jnp.where(flag_ref[...] > 0.5, placed(0), o_ref[...]).astype(BF16)
    dq_ref[...] = dq_in[...] + placed(1) * scale
    dk_ref[...] = dk_in[...] + placed(2) * scale
    dv_ref[...] = dv_in[...] + placed(3)


def shards(n, query_rows, key_rows, value_rows, out_grad, global_pos):
    tok, _, width = query_rows.shape
    count = global_pos.shape[0]
    yn = 4
    xn = n // (2 * yn)
    deep = xn * SLOTS // ROWS
    window = tok + 2 * HALF
    span = TILE + 2 * HALF
    copies = 4 * (xn - 1) + 4 * (yn - 1) + 20
    vmem = pl.BlockSpec(memory_space=pltpu.VMEM)
    anywhere = pl.BlockSpec(memory_space=pl.ANY)
    flat = [x.reshape(tok, width) for x in (query_rows, key_rows, value_rows, out_grad)]
    rows_f32 = jax.ShapeDtypeStruct((tok, width), F32)
    middle = pl.pallas_call(
        functools.partial(kernel, (n, yn, xn, tok, count, width)),
        name="sparse_attention",
        out_shape=(rows_f32,) * 4
        + (
            jax.ShapeDtypeStruct((tok, TILE), BF16),
            rows_f32,
            jax.ShapeDtypeStruct((2 * ROWS, width), F32),
        ),
        in_specs=[pl.BlockSpec(memory_space=pltpu.HBM)] * 5,
        out_specs=(anywhere,) * 7,
        scratch_shapes=[
            pltpu.VMEM((1, count), I32),
            pltpu.VMEM((window, width), BF16),
            pltpu.VMEM((window, width), BF16),
            pltpu.VMEM((window, width), BF16),
            pltpu.VMEM((window, width), BF16),
            pltpu.VMEM((tok, width), BF16),
            pltpu.VMEM((1, window), F32),
            pltpu.VMEM((tok, width), F32),
            pltpu.VMEM((2, ROWS, width), BF16),
            pltpu.VMEM((xn, 2, ROWS, width), BF16),
            pltpu.VMEM((2, yn, xn + 1, ROWS, width), BF16),
            pltpu.VMEM((4, count, 2 * yn * (xn + 1) * ROWS), BF16),
            pltpu.VMEM((4, count, width), BF16),
            pltpu.VMEM((tok, span), F32),
            pltpu.VMEM((tok, width), F32),
            pltpu.VMEM((tok, span), F32),
            pltpu.VMEM((tok, width), F32),
            pltpu.VMEM((tok, width), F32),
            pltpu.VMEM((tok, width), F32),
            pltpu.VMEM((tok, width), F32),
            pltpu.VMEM((tok, count), F32),
            pltpu.VMEM((tok, count), F32),
            pltpu.VMEM((8, TILE), F32),
            pltpu.VMEM((8, TILE), F32),
            pltpu.VMEM((8, TILE), F32),
            pltpu.VMEM((xn - 1, 8, TILE), F32),
            pltpu.VMEM((8, TILE), F32),
            pltpu.VMEM((yn - 1, 8, TILE), F32),
            pltpu.VMEM((tok, width), F32),
            pltpu.VMEM((tok, width), F32),
            pltpu.VMEM((2, 2 * xn * yn * SLOTS, count), BF16),
            pltpu.VMEM((ROWS, count), F32),
            pltpu.VMEM((tok, TILE), BF16),
            pltpu.VMEM((2, 3 * xn + 1, ROWS, width), BF16),
            pltpu.VMEM((3 * xn + 1, ROWS, width), BF16),
            pltpu.VMEM((xn, 4, ROWS, width), BF16),
            pltpu.VMEM((xn - 1, 4, ROWS, width), BF16),
            pltpu.VMEM((2, 2 * deep * yn + 1, ROWS, width), BF16),
            pltpu.VMEM((2 * deep * yn + 1, ROWS, width), BF16),
            pltpu.VMEM((yn, 2 * deep + 1, ROWS, width), BF16),
            pltpu.VMEM((yn - 1, 2 * deep + 1, ROWS, width), BF16),
            pltpu.VMEM((xn, 4 * ROWS, width), F32),
            pltpu.VMEM((yn, ROWS, width), BF16),
            pltpu.VMEM((yn - 1, ROWS, width), BF16),
            pltpu.VMEM((xn, ROWS, width), BF16),
            pltpu.VMEM((xn - 1, ROWS, width), BF16),
            pltpu.VMEM((2 * ROWS, width), F32),
            pltpu.VMEM((8, TILE), F32),
            pltpu.VMEM((2, 8, TILE), F32),
            pltpu.SemaphoreType.DMA((copies,)),
            pltpu.SemaphoreType.DMA((copies,)),
            pltpu.SemaphoreType.DMA((5,)),
            pltpu.SemaphoreType.DMA((7,)),
        ],
        compiler_params=pltpu.CompilerParams(
            collective_id=0, has_side_effects=True, vmem_limit_bytes=24 << 20
        ),
    )(*[pltpu.with_memory_space_constraint(x, pltpu.HBM) for x in (global_pos.reshape(1, count), *flat)])
    results = pl.pallas_call(
        functools.partial(finish, width**-0.5),
        name="place_global_rows",
        out_shape=(jax.ShapeDtypeStruct((tok, width), BF16),) + (rows_f32,) * 3,
        in_specs=[vmem] * 7,
        out_specs=(vmem,) * 4,
        scratch_shapes=[pltpu.VMEM((TILE, width), F32)],
        compiler_params=pltpu.CompilerParams(vmem_limit_bytes=8 << 20),
    )(*middle)
    return tuple(x.reshape(tok, 1, width) for x in results)


def solution(mesh):
    rows = P("ctx", "head", None)
    return jax.shard_map(
        functools.partial(shards, mesh.shape["ctx"]),
        mesh=mesh,
        in_specs=(rows,) * 4 + (P(),),
        out_specs=(rows,) * 4,
        check_vma=False,
    )
```

```python
import functools

import jax
import jax.numpy as jnp
from jax import lax
from jax.experimental import pallas as pl
from jax.experimental.pallas import tpu as pltpu
from jax.sharding import PartitionSpec as P

MESH = pl.DeviceIdType.MESH
HALF = 512
TILE = 128
SLOTS = 4
ROWS = 16
NEG = -1e30
F32 = jnp.float32
BF16 = jnp.bfloat16
I32 = jnp.int32


def dot_nn(a, b):
    return lax.dot_general(a, b, (((1,), (0,)), ((), ())), preferred_element_type=F32)


def dot_nt(a, b):
    return lax.dot_general(a, b, (((1,), (1,)), ((), ())), preferred_element_type=F32)


def dot_tn(a, b):
    return lax.dot_general(a, b, (((0,), (0,)), ((), ())), preferred_element_type=F32)


def iota(shape, dim):
    return lax.broadcasted_iota(I32, shape, dim)


def one_hot(cond):
    return jnp.where(cond, 1.0, 0.0).astype(BF16)


def kernel(
    sizes,
    pos_hbm,
    q_hbm,
    k_hbm,
    v_hbm,
    do_hbm,
    o_out,
    dq_out,
    dk_out,
    dv_out,
    hot_out,
    flag_out,
    r_out,
    pos_scr,
    qpad,
    dopad,
    kpad,
    vpad,
    lgrad,
    colbias,
    rowflag,
    pack,
    gx,
    gath,
    pick,
    glob,
    p_scr,
    ow_scr,
    d_scr,
    m_scr,
    l_scr,
    o_scr,
    dq_scr,
    sg_scr,
    gw_scr,
    st_own,
    st_sib,
    st_x,
    st_xin,
    st_y,
    st_yin,
    dkown,
    dvown,
    spread,
    spread_over,
    hot_scr,
    z1_own,
    z1_sib,
    t1_own,
    t1_in,
    z2_own,
    z2_sib,
    t2_own,
    t2_in,
    f_scr,
    u_own,
    u_in,
    v_own,
    v_in,
    r_scr,
    near_out,
    near_in,
    send_sem,
    recv_sem,
    halo_send,
    halo_recv,
    load_sem,
    store_sem,
):
    n, yn, xn, tok, count, width = sizes
    seq = n * tok
    scale = width**-0.5
    x_shift = xn.bit_length() - 1
    tok_shift = tok.bit_length() - 1
    window = tok + 2 * HALF
    span = TILE + 2 * HALF
    tiles = tok // TILE
    own = pl.ds(HALF, tok)

    me = lax.axis_index("ctx")
    core = lax.rem(me, 2)
    xx = lax.rem(lax.div(me, 2), xn)
    yy = lax.div(me, 2 * xn)

    def ctx_id(y, x, c):
        return (y * xn + x) * 2 + c

    x_peers = [ctx_id(yy, lax.rem(xx + d, xn), core) for d in range(1, xn)]
    y_peers = [ctx_id(lax.rem(yy + e, yn), xx, core) for e in range(1, yn)]
    sibling = me + 1 - 2 * core
    right = lax.rem(me + 1, n)
    left = lax.rem(me + n - 1, n)
    greeted = x_peers + y_peers + [left, right]
    x_order = sorted(range(1, xn), key=lambda d: -min(d, xn - d))
    y_order = sorted(range(1, yn), key=lambda e: -min(e, yn - e))

    barrier = pltpu.get_barrier_semaphore()
    for peer in greeted:
        pl.semaphore_signal(barrier, inc=1, device_id={"ctx": peer}, device_id_type=MESH)

    loads = [
        pltpu.make_async_copy(src, dst, load_sem.at[i])
        for i, (src, dst) in enumerate(
            (
                (pos_hbm, pos_scr),
                (q_hbm, qpad.at[own]),
                (k_hbm, kpad.at[own]),
                (v_hbm, vpad.at[own]),
                (do_hbm, dopad.at[own]),
            )
        )
    ]
    for load in loads:
        load.start()

    copies = []

    def send(src, dst, peer):
        number = len(copies)
        copy = pltpu.make_async_remote_copy(
            src_ref=src,
            dst_ref=dst,
            send_sem=send_sem.at[number],
            recv_sem=recv_sem.at[number],
            device_id={"ctx": peer},
            device_id_type=MESH,
        )
        copy.start()
        copies.append(copy)
        return copy

    stores = []

    def keep(src, dst):
        copy = pltpu.make_async_copy(src, dst, store_sem.at[len(stores)])
        copy.start()
        stores.append(copy)

    loads[0].wait()
    pos_r = pos_scr[...]
    first, second = iota((count, count), 0), iota((count, count), 1)
    pos_c = jnp.sum(jnp.where(first == second, pos_r.astype(F32), 0.0), axis=1, keepdims=True).astype(I32)
    owner_c, owner_r = pos_c >> tok_shift, pos_r >> tok_shift
    local_c, local_r = pos_c & (tok - 1), pos_r & (tok - 1)
    same = owner_c == owner_r
    rank_c = jnp.sum(jnp.where(same & (second < first), 1.0, 0.0), axis=1, keepdims=True).astype(I32)
    rank_r = jnp.sum(jnp.where(same & (first < second), 1.0, 0.0), axis=0, keepdims=True).astype(I32)

    rho = iota((2 * ROWS, count), 0)
    slot_rank = ((rho >> 4) << 2) + (rho & 3)
    chosen = (owner_r == me) & (rank_r == slot_rank)
    slot_col = jnp.sum(jnp.where(chosen, (local_r + 1).astype(F32), 0.0), axis=1, keepdims=True).astype(I32) - 1
    array_of = (iota((2 * ROWS, tok), 0) >> 2) & 3
    at_slot = iota((2 * ROWS, tok), 1) == slot_col
    picked = jnp.zeros((2 * ROWS, width), F32)
    for load in loads[1:]:
        load.wait()
    for a, rows in enumerate((qpad[own, :], kpad[own, :], vpad[own, :], dopad[own, :])):
        picked = picked + dot_nn(one_hot(at_slot & (array_of == a)), rows)
    pack[...] = picked.astype(BF16).reshape(2, ROWS, width)
    gx[0] = pack[...]

    pl.semaphore_wait(barrier, len(greeted))

    from_x = [send(pack, gx.at[d], x_peers[d - 1]) for d in x_order]
    to_right, to_left = me < n - 1, me > 0
    below, above = pl.ds(0, HALF), pl.ds(HALF + tok, HALF)

    def exchange(ref):
        pairs = []
        for peer, there, back, dst in ((right, to_right, to_left, below), (left, to_left, to_right, above)):
            number = len(halos)
            copy = pltpu.make_async_remote_copy(
                src_ref=ref.at[own],
                dst_ref=ref.at[dst],
                send_sem=halo_send.at[number],
                recv_sem=halo_recv.at[number],
                device_id={"ctx": peer},
                device_id_type=MESH,
            )
            pl.when(there)(copy.start)
            halos.append((copy, there))
            pairs.append((copy, back))
        return pairs

    halos = []

    def arrived(pairs):
        for copy, there in pairs:
            pl.when(there)(copy.wait_recv)

    @pl.when(me == 0)
    def _():
        for ref in (kpad, vpad, qpad, dopad):
            ref[below, :] = jnp.zeros((HALF, width), BF16)

    @pl.when(me == n - 1)
    def _():
        for ref in (kpad, vpad, qpad, dopad):
            ref[above, :] = jnp.zeros((HALF, width), BF16)

    near_halos = exchange(kpad) + exchange(vpad)

    for part in range(window // 512):
        reach = me * tok - HALF + part * 512 + iota((1, 512), 1)
        bias = jnp.min(jnp.where(pos_c == reach, NEG, 0.0), axis=0, keepdims=True)
        inside = (reach >= 0) & (reach < seq)
        colbias[:, pl.ds(part * 512, 512)] = jnp.where(inside, bias, NEG)
    row_pos = me * tok + iota((tok, 1), 0)
    flag = jnp.max(jnp.where(row_pos == pos_r, 1.0, 0.0), axis=1, keepdims=True)
    rowflag[...] = jnp.broadcast_to(flag, (tok, width))
    lgrad[...] = jnp.where(rowflag[...] > 0.5, 0.0, dopad[own, :].astype(F32)).astype(BF16)

    for copy in from_x:
        copy.wait_recv()
    over = gx[0, 1].astype(F32)
    gath[0, 0, 0] = gx[0, 0]
    for d in range(1, xn):
        gath[0, 0, d] = gx[d, 0]
        over = over + gx[d, 1].astype(F32)
    gath[0, 0, xn] = over.astype(BF16)
    from_y = {e: send(gath.at[0, 0], gath.at[0, e], y_peers[e - 1]) for e in y_order}
    from_sib = [send(gath.at[0, 0], gath.at[1, 0], sibling)]

    core_c, xo_c, yo_c = owner_c & 1, (owner_c >> 1) & (xn - 1), owner_c >> (1 + x_shift)
    half_c = (core_c ^ core) * yn + ((yy - yo_c) & (yn - 1))
    src_c = jnp.where(
        rank_c < SLOTS,
        (half_c * (xn + 1) + ((xx - xo_c) & (xn - 1))) * ROWS + rank_c,
        (half_c * (xn + 1) + xn) * ROWS + rank_c - SLOTS,
    )
    total = 2 * yn * (xn + 1) * ROWS
    for a in range(4):
        pick[a] = one_hot(iota((count, total), 1) == src_c + SLOTS * a)

    core_r, xo_r, yo_r = owner_r & 1, (owner_r >> 1) & (xn - 1), owner_r >> (1 + x_shift)
    place = ((core_r ^ core) * xn + ((xo_r - xx) & (xn - 1))) * yn + ((yo_r - yy) & (yn - 1))
    beyond = 2 * xn * yn * SLOTS
    key_r = jnp.where(rank_r < SLOTS, place * SLOTS + rank_r, beyond + rank_r - SLOTS)
    spread[0] = one_hot(iota((beyond, count), 0) == key_r)
    turned = ((core_r ^ core) * yn + ((yo_r - yy) & (yn - 1))) * xn + ((xo_r - xx) & (xn - 1))
    turned_r = jnp.where(rank_r < SLOTS, turned * SLOTS + rank_r, beyond + rank_r - SLOTS)
    spread[1] = one_hot(iota((beyond, count), 0) == turned_r)
    spread_over[...] = jnp.where(beyond + (iota((ROWS, count), 0) & 3) == key_r, 1.0, 0.0)

    rho_lane = iota((count, TILE), 1)
    lane_rank = ((rho_lane >> 4) << 2) + (rho_lane & 3)
    chosen_c = (owner_c == me) & (rank_c == lane_rank) & (rho_lane < 2 * ROWS)
    slot_row = jnp.sum(jnp.where(chosen_c, (local_c + 1).astype(F32), 0.0), axis=0, keepdims=True).astype(I32) - 1
    hot_scr[...] = one_hot(iota((tok, TILE), 0) == slot_row)
    keep(hot_scr, hot_out)
    keep(rowflag, flag_out)

    arrived(near_halos)

    lane = iota((TILE, TILE), 1)
    sub = iota((TILE, TILE), 0)
    low_bias = jnp.where(lane >= sub, 0.0, NEG)
    high_bias = jnp.where(lane <= sub, 0.0, NEG)

    def before(t, carry):
        start = pl.multiple_of(t * TILE, TILE)
        rows, keys = pl.ds(start, TILE), pl.ds(start, span)
        s = dot_nt(qpad[pl.ds(HALF + start, TILE), :], kpad[keys, :]) * scale + colbias[:, keys]
        s = jnp.concatenate(
            [s[:, :TILE] + low_bias, s[:, TILE : 2 * HALF], s[:, 2 * HALF :] + high_bias], axis=1
        )
        top = jnp.max(s, axis=1, keepdims=True)
        p = jnp.exp(s - top)
        p_scr[rows, :] = p
        ow_scr[rows, :] = dot_nn(p.astype(BF16), vpad[keys, :])
        m_scr[rows, :] = jnp.broadcast_to(top, (TILE, width))
        l_scr[rows, :] = jnp.broadcast_to(jnp.sum(p, axis=1, keepdims=True), (TILE, width))
        d_scr[rows, :] = dot_nt(lgrad[rows, :], vpad[keys, :])
        return carry

    lax.fori_loop(0, tiles, before, 0)

    for e in reversed(y_order):
        from_y[e].wait_recv()
        from_sib.append(send(gath.at[0, e], gath.at[1, e], sibling))
    far_halos = exchange(qpad) + exchange(dopad)
    for copy in from_sib:
        copy.wait_recv()
    everything = gath[...].reshape(total, width)
    for a in range(4):
        glob[a] = dot_nn(pick[a], everything).astype(BF16)

    middle = (jnp.sum(glob[2].astype(F32), axis=0, keepdims=True) * (1.0 / count)).astype(BF16)
    centre = dot_nt(jnp.broadcast_to(middle, (ROWS, width)), glob[3])[0:1, :]
    sg = dot_nt(kpad[own, :], glob[0]) * scale
    gw = dot_nt(vpad[own, :], glob[3]) - centre
    sg_scr[...] = sg
    gw_scr[...] = gw
    top = jnp.max(sg, axis=0, keepdims=True)
    p = jnp.exp(sg - top)
    stat_rows = [top, jnp.sum(p, axis=0, keepdims=True), jnp.sum(p * gw, axis=0, keepdims=True)]
    for r, row in enumerate(stat_rows):
        st_own[2 * r : 2 * r + 1, :] = row[:, :TILE]
        st_own[2 * r + 1 : 2 * r + 2, :] = row[:, TILE:]
    st_own[6:8, :] = jnp.zeros((2, TILE), F32)

    def join(parts):
        joined = functools.reduce(jnp.maximum, [part[0:2, :] for part in parts])
        weigh = [jnp.exp(part[0:2, :] - joined) for part in parts]
        return (
            joined,
            sum(part[2:4, :] * w for part, w in zip(parts, weigh)),
            sum(part[4:6, :] * w for part, w in zip(parts, weigh)),
        )

    def store(ref, stats):
        for r, part in enumerate(stats):
            ref[2 * r : 2 * r + 2, :] = part
        ref[6:8, :] = jnp.zeros((2, TILE), F32)

    def row_of(part):
        return jnp.concatenate([part[0:1], part[1:2]], axis=1)

    stat_sib = send(st_own, st_sib, sibling)

    lg = lgrad[...]
    s = dot_nt(qpad[own, :], glob[1]) * scale
    top_w = m_scr[:, 0:1]
    top = jnp.maximum(top_w, jnp.max(s, axis=1, keepdims=True))
    pg = jnp.exp(s - top)
    down = jnp.exp(top_w - top)
    all_sum = l_scr[:, 0:1] * down + jnp.sum(pg, axis=1, keepdims=True)
    inv = 1.0 / all_sum
    pg = pg * inv
    pg16 = pg.astype(BF16)
    o = ow_scr[...] * (down * inv) + dot_nn(pg16, glob[2])
    o_scr[...] = o
    row_dot = jnp.sum(lg.astype(F32) * o, axis=1, keepdims=True)
    dsg = (pg * (dot_nt(lg, glob[2]) - row_dot)).astype(BF16)
    m_scr[...] = jnp.broadcast_to(down * inv, (tok, width))
    l_scr[...] = jnp.broadcast_to(row_dot, (tok, width))
    dkg = dot_tn(dsg, qpad[own, :])
    dvg = dot_tn(pg16, lg)
    dq_scr[...] = dot_nn(dsg, glob[1])

    row_lse = jnp.where(rowflag[:, 0:1] > 0.5, -NEG, top + jnp.log(all_sum))
    for t in range(tiles):
        for r, column in enumerate((row_lse, row_dot)):
            mine = column[t * TILE : (t + 1) * TILE]
            near_out[r * tiles + t : r * tiles + t + 1, :] = jnp.sum(
                jnp.where(lane == sub, mine, 0.0), axis=0, keepdims=True
            )
    near = [send(near_out, near_in.at[0], right), send(near_out, near_in.at[1], left)]

    def after():
        dk = jnp.zeros((tok, width), F32)
        dv = jnp.zeros((tok, width), F32)
        for t in range(tiles):
            start = t * TILE
            rows, keys = pl.ds(start, TILE), pl.ds(start, span)
            pw = p_scr[rows, :] * m_scr[rows, 0:1]
            dsw = (pw * (d_scr[rows, :] - l_scr[rows, 0:1])).astype(BF16)
            dq_scr[rows, :] = (dq_scr[rows, :] + dot_nn(dsw, kpad[keys, :])) * scale
            first_own = HALF - start
            dk = dk + dot_tn(dsw[:, first_own : first_own + tok], qpad[pl.ds(HALF + start, TILE), :])
            dv = dv + dot_tn(pw[:, first_own : first_own + tok].astype(BF16), lgrad[rows, :])
        dkown[...] = dk
        dvown[...] = dv

    def from_neighbour(side):
        rows = pl.ds(side * (HALF + tok), HALF)
        key_at, query_at = iota((tok, HALF), 0), iota((tok, HALF), 1)
        within = key_at <= query_at if side == 0 else key_at >= query_at
        there = me > 0 if side == 0 else me < n - 1
        outside = jnp.where(there, 0.0, -NEG)
        lse_n = jnp.concatenate([near_in[side, t : t + 1, :] for t in range(tiles)], axis=1)
        dot_n = jnp.concatenate([near_in[side, tiles + t : tiles + t + 1, :] for t in range(tiles)], axis=1)
        s = dot_nt(kpad[own, :], qpad[rows, :]) * scale
        s = jnp.where(within, s, NEG) + jnp.where(rowflag[:, 0:1] > 0.5, NEG, 0.0)
        p = jnp.exp(s - (lse_n + outside))
        ds = (p * (dot_nt(vpad[own, :], dopad[rows, :]) - dot_n)).astype(BF16)
        dkown[...] += dot_nn(ds, qpad[rows, :])
        dvown[...] += dot_nn(p.astype(BF16), dopad[rows, :])

    over_row = iota((ROWS, count), 0)

    def overflow(partial, arrays):
        z_over = jnp.zeros((ROWS, width), F32)
        for a in range(arrays):
            mine = jnp.where((over_row >> 2) == a, spread_over[...], 0.0).astype(BF16)
            z_over = z_over + dot_nn(mine, partial[:, a * width : (a + 1) * width])
        return z_over.astype(BF16)

    def paired(own_ref, sib_ref, groups, arrays, ref):
        over = (own_ref[0, arrays * groups].astype(F32) + sib_ref[arrays * groups].astype(F32)).astype(BF16)
        for d in range(groups):
            tiles_of = pl.ds(d * arrays, arrays)
            ref[d, 0:arrays] = (own_ref[0, tiles_of].astype(F32) + sib_ref[tiles_of].astype(F32)).astype(BF16)
            ref[d, arrays] = over

    deep = xn * SLOTS // ROWS
    partial = jnp.concatenate([dkg, dvg], axis=1).astype(BF16)
    z = dot_nn(spread[1], partial).astype(BF16)
    z_over = overflow(partial, 2)
    for half in range(2):
        for e in range(yn):
            base = (half * yn + e) * deep * ROWS
            for a in range(2):
                mine = z[base : base + deep * ROWS, a * width : (a + 1) * width]
                z2_own[half, (e * 2 + a) * deep : (e * 2 + a + 1) * deep] = mine.reshape(deep, ROWS, width)
        z2_own[half, 2 * deep * yn] = z_over
    z2_copy = send(z2_own.at[1], z2_sib, sibling)

    stat_sib.wait_recv()
    store(st_x, join([st_own[...], st_sib[...]]))
    stat_x = [send(st_x, st_xin.at[d - 1], x_peers[d - 1]) for d in x_order]

    pair_top = st_x[0:2, :]
    w = jnp.exp(sg_scr[...] - row_of(pair_top))
    w16 = w.astype(BF16)
    ds16 = (w * gw_scr[...]).astype(BF16)
    value_key = dot_tn(w16, jnp.concatenate([vpad[own, :], kpad[own, :]], axis=1))
    partial = [value_key[:, :width], dot_tn(ds16, kpad[own, :]), value_key[:, width:]]
    partial = jnp.concatenate(partial, axis=1).astype(BF16)
    z = dot_nn(spread[0], partial).astype(BF16)
    z_over = overflow(partial, 3)
    for half in range(2):
        for d in range(xn):
            base = (half * xn + d) * ROWS
            for a in range(3):
                z1_own[half, d * 3 + a] = z[base : base + ROWS, a * width : (a + 1) * width]
        z1_own[half, 3 * xn] = z_over
    z1_copy = send(z1_own.at[1], z1_sib, sibling)

    z2_copy.wait_recv()
    paired(z2_own, z2_sib, yn, 2 * deep, t2_own)
    t2_copies = [send(t2_own.at[e], t2_in.at[e - 1], y_peers[e - 1]) for e in y_order]
    keep(o_scr, o_out)
    z1_copy.wait_recv()
    paired(z1_own, z1_sib, xn, 3, t1_own)
    t1_copies = [send(t1_own.at[d], t1_in.at[d - 1], x_peers[d - 1]) for d in x_order]

    after()
    keep(dq_scr, dq_out)

    for copy in stat_x:
        copy.wait_recv()
    store(st_y, join([st_x[...]] + [st_xin[d - 1] for d in range(1, xn)]))
    stat_y = [send(st_y, st_yin.at[e - 1], y_peers[e - 1]) for e in y_order]

    def arrange(groups, depth, wanted, overflow_at, places):
        goal, source = iota((groups * ROWS, places), 0), iota((groups * ROWS, places), 1)
        goal_to, goal_array, goal_slot = goal >> 4, (goal >> 2) & 1, goal & 3
        hit = jnp.zeros(goal.shape, F32)
        for array, tile in wanted:
            at = jnp.where(
                (goal & 15) >= 8,
                overflow_at + tile * SLOTS + goal_slot,
                tile * depth * ROWS + goal_to * SLOTS + goal_slot,
            )
            hit = hit + jnp.where((goal_array == array) & (source == at), 1.0, 0.0)
        return hit.astype(BF16)

    arrange_1 = arrange(yn, 1, ((0, 0), (1, 1), (1, 2)), 3 * ROWS, 4 * ROWS)
    arrange_2 = arrange(xn, deep, ((0, 0), (1, 1)), 2 * deep * ROWS, (2 * deep + 1) * ROWS)

    for copy in t2_copies:
        copy.wait_recv()
    column = t2_own[0].astype(F32)
    for e in range(1, yn):
        column = column + t2_in[e - 1].astype(F32)
    v = dot_nn(arrange_2, column.reshape((2 * deep + 1) * ROWS, width).astype(BF16)).astype(BF16)
    v_own[...] = v.reshape(xn, ROWS, width)
    v_copies = [send(v_own.at[d], v_in.at[d - 1], x_peers[d - 1]) for d in x_order]

    arrived(far_halos)
    for copy in near:
        copy.wait_recv()
    from_neighbour(0)
    from_neighbour(1)

    for copy in stat_y:
        copy.wait_recv()
    joined, summed, dotted = join([st_y[...]] + [st_yin[e - 1] for e in range(1, yn)])
    lse = row_of(joined + jnp.log(summed))
    ratio = row_of(dotted / summed)
    line = iota((4 * ROWS, count), 0)
    line_key = jnp.where(line < 3 * ROWS, line & (ROWS - 1), beyond + (line & 3))
    kind = jnp.where(line < 3 * ROWS, line >> 4, (line >> 2) & 3)
    found = jnp.where(line_key == key_r, 1.0, 0.0)
    found = found * jnp.where(kind == 2, -ratio, jnp.where(kind == 3, 0.0, 1.0))
    column = jnp.zeros((4 * ROWS, width), F32)
    for d in range(xn):
        pair = st_x[0:2, :] if d == 0 else st_xin[d - 1, 0:2, :]
        fall = row_of(jnp.exp(pair - joined) / summed)
        factor = jnp.sum(found * fall, axis=1, keepdims=True)
        f_scr[d] = jnp.broadcast_to(factor, (4 * ROWS, width))

    for copy in t1_copies:
        copy.wait_recv()
    for d in range(xn):
        mine = t1_own[0] if d == 0 else t1_in[d - 1]
        column = column + mine.astype(F32).reshape(4 * ROWS, width) * f_scr[d]
    upper = column.astype(BF16)
    lower = (column - upper.astype(F32)).astype(BF16)
    u = (dot_nn(arrange_1, upper) + dot_nn(arrange_1, lower)).astype(BF16)
    u_own[...] = u.reshape(yn, ROWS, width)
    u_copies = [send(u_own.at[e], u_in.at[e - 1], y_peers[e - 1]) for e in y_order]

    w = jnp.exp(sg_scr[...] - lse)
    dvown[...] += dot_nn(w.astype(BF16), glob[3])
    dkown[...] = (dkown[...] + dot_nn((w * (gw_scr[...] - ratio)).astype(BF16), glob[0])) * scale
    keep(dkown, dk_out)
    keep(dvown, dv_out)

    for copy in v_copies:
        copy.wait_recv()
    late = v_own[0].astype(F32)
    for d in range(1, xn):
        late = late + v_in[d - 1].astype(F32)
    for copy in u_copies:
        copy.wait_recv()
    early = u_own[0].astype(F32)
    for e in range(1, yn):
        early = early + u_in[e - 1].astype(F32)
    for part in range(2):
        r_scr[part * ROWS : part * ROWS + 8, :] = early[part * 8 : part * 8 + 8]
        r_scr[part * ROWS + 8 : part * ROWS + 16, :] = late[part * 8 : part * 8 + 8]
    keep(r_scr, r_out)

    for copy in stores:
        copy.wait()
    for copy in copies:
        copy.wait_send()
    for copy, there in halos:
        pl.when(there)(copy.wait_send)


def finish(scale, o_ref, dq_in, dk_in, dv_in, hot_ref, flag_ref, r_ref, out_ref, dq_ref, dk_ref, dv_ref, total):
    tok = o_ref.shape[0]
    total[...] = jnp.zeros_like(total)
    total[0 : 2 * ROWS, :] = r_ref[...]
    upper = total[...].astype(BF16)
    lower = (total[...] - upper.astype(F32)).astype(BF16)
    hot = hot_ref[...].astype(F32)
    lane_array = (iota((tok, TILE), 1) >> 2) & 3

    def placed(a):
        mine = jnp.where(lane_array == a, hot, 0.0).astype(BF16)
        return dot_nn(mine, upper) + dot_nn(mine, lower)

    out_ref[...] = jnp.where(flag_ref[...] > 0.5, placed(0), o_ref[...]).astype(BF16)
    dq_ref[...] = dq_in[...] + placed(1) * scale
    dk_ref[...] = dk_in[...] + placed(2) * scale
    dv_ref[...] = dv_in[...] + placed(3)


def shards(n, query_rows, key_rows, value_rows, out_grad, global_pos):
    tok, _, width = query_rows.shape
    count = global_pos.shape[0]
    yn = 4
    xn = n // (2 * yn)
    deep = xn * SLOTS // ROWS
    window = tok + 2 * HALF
    span = TILE + 2 * HALF
    copies = 4 * (xn - 1) + 4 * (yn - 1) + 20
    vmem = pl.BlockSpec(memory_space=pltpu.VMEM)
    anywhere = pl.BlockSpec(memory_space=pl.ANY)
    flat = [x.reshape(tok, width) for x in (query_rows, key_rows, value_rows, out_grad)]
    rows_f32 = jax.ShapeDtypeStruct((tok, width), F32)
    middle = pl.pallas_call(
        functools.partial(kernel, (n, yn, xn, tok, count, width)),
        name="sparse_attention",
        out_shape=(rows_f32,) * 4
        + (
            jax.ShapeDtypeStruct((tok, TILE), BF16),
            rows_f32,
            jax.ShapeDtypeStruct((2 * ROWS, width), F32),
        ),
        in_specs=[pl.BlockSpec(memory_space=pltpu.HBM)] * 5,
        out_specs=(anywhere,) * 7,
        scratch_shapes=[
            pltpu.VMEM((1, count), I32),
            pltpu.VMEM((window, width), BF16),
            pltpu.VMEM((window, width), BF16),
            pltpu.VMEM((window, width), BF16),
            pltpu.VMEM((window, width), BF16),
            pltpu.VMEM((tok, width), BF16),
            pltpu.VMEM((1, window), F32),
            pltpu.VMEM((tok, width), F32),
            pltpu.VMEM((2, ROWS, width), BF16),
            pltpu.VMEM((xn, 2, ROWS, width), BF16),
            pltpu.VMEM((2, yn, xn + 1, ROWS, width), BF16),
            pltpu.VMEM((4, count, 2 * yn * (xn + 1) * ROWS), BF16),
            pltpu.VMEM((4, count, width), BF16),
            pltpu.VMEM((tok, span), F32),
            pltpu.VMEM((tok, width), F32),
            pltpu.VMEM((tok, span), F32),
            pltpu.VMEM((tok, width), F32),
            pltpu.VMEM((tok, width), F32),
            pltpu.VMEM((tok, width), F32),
            pltpu.VMEM((tok, width), F32),
            pltpu.VMEM((tok, count), F32),
            pltpu.VMEM((tok, count), F32),
            pltpu.VMEM((8, TILE), F32),
            pltpu.VMEM((8, TILE), F32),
            pltpu.VMEM((8, TILE), F32),
            pltpu.VMEM((xn - 1, 8, TILE), F32),
            pltpu.VMEM((8, TILE), F32),
            pltpu.VMEM((yn - 1, 8, TILE), F32),
            pltpu.VMEM((tok, width), F32),
            pltpu.VMEM((tok, width), F32),
            pltpu.VMEM((2, 2 * xn * yn * SLOTS, count), BF16),
            pltpu.VMEM((ROWS, count), F32),
            pltpu.VMEM((tok, TILE), BF16),
            pltpu.VMEM((2, 3 * xn + 1, ROWS, width), BF16),
            pltpu.VMEM((3 * xn + 1, ROWS, width), BF16),
            pltpu.VMEM((xn, 4, ROWS, width), BF16),
            pltpu.VMEM((xn - 1, 4, ROWS, width), BF16),
            pltpu.VMEM((2, 2 * deep * yn + 1, ROWS, width), BF16),
            pltpu.VMEM((2 * deep * yn + 1, ROWS, width), BF16),
            pltpu.VMEM((yn, 2 * deep + 1, ROWS, width), BF16),
            pltpu.VMEM((yn - 1, 2 * deep + 1, ROWS, width), BF16),
            pltpu.VMEM((xn, 4 * ROWS, width), F32),
            pltpu.VMEM((yn, ROWS, width), BF16),
            pltpu.VMEM((yn - 1, ROWS, width), BF16),
            pltpu.VMEM((xn, ROWS, width), BF16),
            pltpu.VMEM((xn - 1, ROWS, width), BF16),
            pltpu.VMEM((2 * ROWS, width), F32),
            pltpu.VMEM((8, TILE), F32),
            pltpu.VMEM((2, 8, TILE), F32),
            pltpu.SemaphoreType.DMA((copies,)),
            pltpu.SemaphoreType.DMA((copies,)),
            pltpu.SemaphoreType.DMA((8,)),
            pltpu.SemaphoreType.DMA((8,)),
            pltpu.SemaphoreType.DMA((5,)),
            pltpu.SemaphoreType.DMA((7,)),
        ],
        compiler_params=pltpu.CompilerParams(
            collective_id=0, has_side_effects=True, vmem_limit_bytes=24 << 20
        ),
    )(*[pltpu.with_memory_space_constraint(x, pltpu.HBM) for x in (global_pos.reshape(1, count), *flat)])
    results = pl.pallas_call(
        functools.partial(finish, width**-0.5),
        name="place_global_rows",
        out_shape=(jax.ShapeDtypeStruct((tok, width), BF16),) + (rows_f32,) * 3,
        in_specs=[vmem] * 7,
        out_specs=(vmem,) * 4,
        scratch_shapes=[pltpu.VMEM((TILE, width), F32)],
        compiler_params=pltpu.CompilerParams(vmem_limit_bytes=8 << 20),
    )(*middle)
    return tuple(x.reshape(tok, 1, width) for x in results)


def solution(mesh):
    rows = P("ctx", "head", None)
    return jax.shard_map(
        functools.partial(shards, mesh.shape["ctx"]),
        mesh=mesh,
        in_specs=(rows,) * 4 + (P(),),
        out_specs=(rows,) * 4,
        check_vma=False,
    )
```

```python
import functools

import jax
import jax.numpy as jnp
from jax import lax
from jax.experimental import pallas as pl
from jax.experimental.pallas import tpu as pltpu
from jax.sharding import PartitionSpec as P

MESH = pl.DeviceIdType.MESH
HALF = 512
TILE = 128
SLOTS = 4
ROWS = 16
NEG = -1e30
F32 = jnp.float32
BF16 = jnp.bfloat16
I32 = jnp.int32


def dot_nn(a, b):
    return lax.dot_general(a, b, (((1,), (0,)), ((), ())), preferred_element_type=F32)


def dot_nt(a, b):
    return lax.dot_general(a, b, (((1,), (1,)), ((), ())), preferred_element_type=F32)


def dot_tn(a, b):
    return lax.dot_general(a, b, (((0,), (0,)), ((), ())), preferred_element_type=F32)


def iota(shape, dim):
    return lax.broadcasted_iota(I32, shape, dim)


def one_hot(cond):
    return jnp.where(cond, 1.0, 0.0).astype(BF16)


def kernel(
    sizes,
    pos_hbm,
    q_hbm,
    k_hbm,
    v_hbm,
    do_hbm,
    o_out,
    dq_out,
    dk_out,
    dv_out,
    hot_out,
    flag_out,
    r_out,
    pos_scr,
    qpad,
    dopad,
    kpad,
    vpad,
    lgrad,
    colbias,
    rowflag,
    pack,
    gx,
    gath,
    pick,
    glob_part,
    glob,
    p_scr,
    ow_scr,
    d_scr,
    m_scr,
    l_scr,
    o_scr,
    dq_scr,
    sg_scr,
    gw_scr,
    st_own,
    st_sib,
    st_x,
    st_xin,
    st_y,
    st_yin,
    dkown,
    dvown,
    spread,
    spread_over,
    hot_scr,
    z1_own,
    z1_sib,
    t1_own,
    t1_in,
    z2_own,
    z2_sib,
    t2_own,
    t2_in,
    f_scr,
    u_own,
    u_in,
    v_own,
    v_in,
    r_scr,
    near_out,
    near_in,
    send_sem,
    recv_sem,
    halo_send,
    halo_recv,
    load_sem,
    store_sem,
):
    n, yn, xn, tok, count, width = sizes
    seq = n * tok
    scale = width**-0.5
    x_shift = xn.bit_length() - 1
    tok_shift = tok.bit_length() - 1
    window = tok + 2 * HALF
    span = TILE + 2 * HALF
    tiles = tok // TILE
    own = pl.ds(HALF, tok)

    me = lax.axis_index("ctx")
    core = lax.rem(me, 2)
    xx = lax.rem(lax.div(me, 2), xn)
    yy = lax.div(me, 2 * xn)

    def ctx_id(y, x, c):
        return (y * xn + x) * 2 + c

    x_peers = [ctx_id(yy, lax.rem(xx + d, xn), core) for d in range(1, xn)]
    y_peers = [ctx_id(lax.rem(yy + e, yn), xx, core) for e in range(1, yn)]
    sibling = me + 1 - 2 * core
    right = lax.rem(me + 1, n)
    left = lax.rem(me + n - 1, n)
    greeted = x_peers + y_peers + [left, right]
    x_order = sorted(range(1, xn), key=lambda d: -min(d, xn - d))
    y_order = sorted(range(1, yn), key=lambda e: -min(e, yn - e))

    barrier = pltpu.get_barrier_semaphore()
    for peer in greeted:
        pl.semaphore_signal(barrier, inc=1, device_id={"ctx": peer}, device_id_type=MESH)

    loads = [
        pltpu.make_async_copy(src, dst, load_sem.at[i])
        for i, (src, dst) in enumerate(
            (
                (pos_hbm, pos_scr),
                (q_hbm, qpad.at[own]),
                (k_hbm, kpad.at[own]),
                (v_hbm, vpad.at[own]),
                (do_hbm, dopad.at[own]),
            )
        )
    ]
    for load in loads:
        load.start()

    copies = []

    def send(src, dst, peer):
        number = len(copies)
        copy = pltpu.make_async_remote_copy(
            src_ref=src,
            dst_ref=dst,
            send_sem=send_sem.at[number],
            recv_sem=recv_sem.at[number],
            device_id={"ctx": peer},
            device_id_type=MESH,
        )
        copy.start()
        copies.append(copy)
        return copy

    stores = []

    def keep(src, dst):
        copy = pltpu.make_async_copy(src, dst, store_sem.at[len(stores)])
        copy.start()
        stores.append(copy)

    loads[0].wait()
    pos_r = pos_scr[...]
    first, second = iota((count, count), 0), iota((count, count), 1)
    pos_c = jnp.sum(jnp.where(first == second, pos_r.astype(F32), 0.0), axis=1, keepdims=True).astype(I32)
    owner_c, owner_r = pos_c >> tok_shift, pos_r >> tok_shift
    local_c, local_r = pos_c & (tok - 1), pos_r & (tok - 1)
    same = owner_c == owner_r
    rank_c = jnp.sum(jnp.where(same & (second < first), 1.0, 0.0), axis=1, keepdims=True).astype(I32)
    rank_r = jnp.sum(jnp.where(same & (first < second), 1.0, 0.0), axis=0, keepdims=True).astype(I32)

    rho = iota((2 * ROWS, count), 0)
    slot_rank = ((rho >> 4) << 2) + (rho & 3)
    chosen = (owner_r == me) & (rank_r == slot_rank)
    slot_col = jnp.sum(jnp.where(chosen, (local_r + 1).astype(F32), 0.0), axis=1, keepdims=True).astype(I32) - 1
    array_of = (iota((2 * ROWS, tok), 0) >> 2) & 3
    at_slot = iota((2 * ROWS, tok), 1) == slot_col
    picked = jnp.zeros((2 * ROWS, width), F32)
    for load in loads[1:]:
        load.wait()
    for a, rows in enumerate((qpad[own, :], kpad[own, :], vpad[own, :], dopad[own, :])):
        picked = picked + dot_nn(one_hot(at_slot & (array_of == a)), rows)
    pack[...] = picked.astype(BF16).reshape(2, ROWS, width)
    gx[0] = pack[...]

    pl.semaphore_wait(barrier, len(greeted))

    from_x = [send(pack, gx.at[d], x_peers[d - 1]) for d in x_order]
    to_right, to_left = me < n - 1, me > 0
    below, above = pl.ds(0, HALF), pl.ds(HALF + tok, HALF)

    def exchange(ref):
        pairs = []
        for peer, there, back, dst in ((right, to_right, to_left, below), (left, to_left, to_right, above)):
            number = len(halos)
            copy = pltpu.make_async_remote_copy(
                src_ref=ref.at[own],
                dst_ref=ref.at[dst],
                send_sem=halo_send.at[number],
                recv_sem=halo_recv.at[number],
                device_id={"ctx": peer},
                device_id_type=MESH,
            )
            pl.when(there)(copy.start)
            halos.append((copy, there))
            pairs.append((copy, back))
        return pairs

    halos = []

    def arrived(pairs):
        for copy, there in pairs:
            pl.when(there)(copy.wait_recv)

    @pl.when(me == 0)
    def _():
        for ref in (kpad, vpad, qpad, dopad):
            ref[below, :] = jnp.zeros((HALF, width), BF16)

    @pl.when(me == n - 1)
    def _():
        for ref in (kpad, vpad, qpad, dopad):
            ref[above, :] = jnp.zeros((HALF, width), BF16)

    near_halos = exchange(kpad) + exchange(vpad)

    for part in range(window // 512):
        reach = me * tok - HALF + part * 512 + iota((1, 512), 1)
        bias = jnp.min(jnp.where(pos_c == reach, NEG, 0.0), axis=0, keepdims=True)
        inside = (reach >= 0) & (reach < seq)
        colbias[:, pl.ds(part * 512, 512)] = jnp.where(inside, bias, NEG)
    row_pos = me * tok + iota((tok, 1), 0)
    flag = jnp.max(jnp.where(row_pos == pos_r, 1.0, 0.0), axis=1, keepdims=True)
    rowflag[...] = jnp.broadcast_to(flag, (tok, width))
    lgrad[...] = jnp.where(rowflag[...] > 0.5, 0.0, dopad[own, :].astype(F32)).astype(BF16)

    for copy in from_x:
        copy.wait_recv()
    over = gx[0, 1].astype(F32)
    gath[0, 0, 0] = gx[0, 0]
    for d in range(1, xn):
        gath[0, 0, d] = gx[d, 0]
        over = over + gx[d, 1].astype(F32)
    gath[0, 0, xn] = over.astype(BF16)
    from_y = {e: send(gath.at[0, 0], gath.at[0, e], y_peers[e - 1]) for e in y_order}
    from_sib = [send(gath.at[0, 0], gath.at[1, 0], sibling)]

    core_c, xo_c, yo_c = owner_c & 1, (owner_c >> 1) & (xn - 1), owner_c >> (1 + x_shift)
    half_total = yn * (xn + 1) * ROWS
    from_row = (yy - yo_c) & (yn - 1)
    src_c = (core_c ^ core) * half_total + jnp.where(
        rank_c < SLOTS,
        (from_row * (xn + 1) + ((xx - xo_c) & (xn - 1))) * ROWS + rank_c,
        (from_row * (xn + 1) + xn) * ROWS + rank_c - SLOTS,
    )
    for half in range(2):
        tile_row = iota((count, half_total), 1) + half * half_total
        for a in range(4):
            pick[half, a] = one_hot(tile_row == src_c + SLOTS * a)

    core_r, xo_r, yo_r = owner_r & 1, (owner_r >> 1) & (xn - 1), owner_r >> (1 + x_shift)
    place = ((core_r ^ core) * xn + ((xo_r - xx) & (xn - 1))) * yn + ((yo_r - yy) & (yn - 1))
    beyond = 2 * xn * yn * SLOTS
    key_r = jnp.where(rank_r < SLOTS, place * SLOTS + rank_r, beyond + rank_r - SLOTS)
    spread[0] = one_hot(iota((beyond, count), 0) == key_r)
    turned = ((core_r ^ core) * yn + ((yo_r - yy) & (yn - 1))) * xn + ((xo_r - xx) & (xn - 1))
    turned_r = jnp.where(rank_r < SLOTS, turned * SLOTS + rank_r, beyond + rank_r - SLOTS)
    spread[1] = one_hot(iota((beyond, count), 0) == turned_r)
    spread_over[...] = jnp.where(beyond + (iota((ROWS, count), 0) & 3) == key_r, 1.0, 0.0)

    rho_lane = iota((count, TILE), 1)
    lane_rank = ((rho_lane >> 4) << 2) + (rho_lane & 3)
    chosen_c = (owner_c == me) & (rank_c == lane_rank) & (rho_lane < 2 * ROWS)
    slot_row = jnp.sum(jnp.where(chosen_c, (local_c + 1).astype(F32), 0.0), axis=0, keepdims=True).astype(I32) - 1
    hot_scr[...] = one_hot(iota((tok, TILE), 0) == slot_row)
    keep(hot_scr, hot_out)
    keep(rowflag, flag_out)

    arrived(near_halos)

    lane = iota((TILE, TILE), 1)
    sub = iota((TILE, TILE), 0)
    low_bias = jnp.where(lane >= sub, 0.0, NEG)
    high_bias = jnp.where(lane <= sub, 0.0, NEG)

    def before(t, carry):
        start = pl.multiple_of(t * TILE, TILE)
        rows, keys = pl.ds(start, TILE), pl.ds(start, span)
        s = dot_nt(qpad[pl.ds(HALF + start, TILE), :], kpad[keys, :]) * scale + colbias[:, keys]
        s = jnp.concatenate(
            [s[:, :TILE] + low_bias, s[:, TILE : 2 * HALF], s[:, 2 * HALF :] + high_bias], axis=1
        )
        top = jnp.max(s, axis=1, keepdims=True)
        p = jnp.exp(s - top)
        p_scr[rows, :] = p
        ow_scr[rows, :] = dot_nn(p.astype(BF16), vpad[keys, :])
        m_scr[rows, :] = jnp.broadcast_to(top, (TILE, width))
        l_scr[rows, :] = jnp.broadcast_to(jnp.sum(p, axis=1, keepdims=True), (TILE, width))
        d_scr[rows, :] = dot_nt(lgrad[rows, :], vpad[keys, :])
        return carry

    lax.fori_loop(0, tiles, before, 0)

    for e in reversed(y_order):
        from_y[e].wait_recv()
        from_sib.append(send(gath.at[0, e], gath.at[1, e], sibling))
    far_halos = exchange(qpad) + exchange(dopad)
    half_tiles = gath[0].reshape(half_total, width)
    for a in range(4):
        glob_part[a] = dot_nn(pick[0, a], half_tiles)
    for copy in from_sib:
        copy.wait_recv()
    half_tiles = gath[1].reshape(half_total, width)
    for a in range(4):
        glob[a] = (glob_part[a] + dot_nn(pick[1, a], half_tiles)).astype(BF16)

    middle = (jnp.sum(glob[2].astype(F32), axis=0, keepdims=True) * (1.0 / count)).astype(BF16)
    centre = dot_nt(jnp.broadcast_to(middle, (ROWS, width)), glob[3])[0:1, :]
    sg = dot_nt(kpad[own, :], glob[0]) * scale
    gw = dot_nt(vpad[own, :], glob[3]) - centre
    sg_scr[...] = sg
    gw_scr[...] = gw
    top = jnp.max(sg, axis=0, keepdims=True)
    p = jnp.exp(sg - top)
    stat_rows = [top, jnp.sum(p, axis=0, keepdims=True), jnp.sum(p * gw, axis=0, keepdims=True)]
    for r, row in enumerate(stat_rows):
        st_own[2 * r : 2 * r + 1, :] = row[:, :TILE]
        st_own[2 * r + 1 : 2 * r + 2, :] = row[:, TILE:]
    st_own[6:8, :] = jnp.zeros((2, TILE), F32)

    def join(parts):
        joined = functools.reduce(jnp.maximum, [part[0:2, :] for part in parts])
        weigh = [jnp.exp(part[0:2, :] - joined) for part in parts]
        return (
            joined,
            sum(part[2:4, :] * w for part, w in zip(parts, weigh)),
            sum(part[4:6, :] * w for part, w in zip(parts, weigh)),
        )

    def store(ref, stats):
        for r, part in enumerate(stats):
            ref[2 * r : 2 * r + 2, :] = part
        ref[6:8, :] = jnp.zeros((2, TILE), F32)

    def row_of(part):
        return jnp.concatenate([part[0:1], part[1:2]], axis=1)

    stat_sib = send(st_own, st_sib, sibling)

    lg = lgrad[...]
    s = dot_nt(qpad[own, :], glob[1]) * scale
    top_w = m_scr[:, 0:1]
    top = jnp.maximum(top_w, jnp.max(s, axis=1, keepdims=True))
    pg = jnp.exp(s - top)
    down = jnp.exp(top_w - top)
    all_sum = l_scr[:, 0:1] * down + jnp.sum(pg, axis=1, keepdims=True)
    inv = 1.0 / all_sum
    pg = pg * inv
    pg16 = pg.astype(BF16)
    o = ow_scr[...] * (down * inv) + dot_nn(pg16, glob[2])
    o_scr[...] = o
    row_dot = jnp.sum(lg.astype(F32) * o, axis=1, keepdims=True)
    dsg = (pg * (dot_nt(lg, glob[2]) - row_dot)).astype(BF16)
    m_scr[...] = jnp.broadcast_to(down * inv, (tok, width))
    l_scr[...] = jnp.broadcast_to(row_dot, (tok, width))
    dkg = dot_tn(dsg, qpad[own, :])
    dvg = dot_tn(pg16, lg)
    dq_scr[...] = dot_nn(dsg, glob[1])

    row_lse = jnp.where(rowflag[:, 0:1] > 0.5, -NEG, top + jnp.log(all_sum))
    for t in range(tiles):
        for r, column in enumerate((row_lse, row_dot)):
            mine = column[t * TILE : (t + 1) * TILE]
            near_out[r * tiles + t : r * tiles + t + 1, :] = jnp.sum(
                jnp.where(lane == sub, mine, 0.0), axis=0, keepdims=True
            )
    near = [send(near_out, near_in.at[0], right), send(near_out, near_in.at[1], left)]

    def after():
        dk = jnp.zeros((tok, width), F32)
        dv = jnp.zeros((tok, width), F32)
        for t in range(tiles):
            start = t * TILE
            rows, keys = pl.ds(start, TILE), pl.ds(start, span)
            pw = p_scr[rows, :] * m_scr[rows, 0:1]
            dsw = (pw * (d_scr[rows, :] - l_scr[rows, 0:1])).astype(BF16)
            dq_scr[rows, :] = (dq_scr[rows, :] + dot_nn(dsw, kpad[keys, :])) * scale
            first_own = HALF - start
            dk = dk + dot_tn(dsw[:, first_own : first_own + tok], qpad[pl.ds(HALF + start, TILE), :])
            dv = dv + dot_tn(pw[:, first_own : first_own + tok].astype(BF16), lgrad[rows, :])
        dkown[...] = dk
        dvown[...] = dv

    def from_neighbour(side):
        rows = pl.ds(side * (HALF + tok), HALF)
        key_at, query_at = iota((tok, HALF), 0), iota((tok, HALF), 1)
        within = key_at <= query_at if side == 0 else key_at >= query_at
        there = me > 0 if side == 0 else me < n - 1
        outside = jnp.where(there, 0.0, -NEG)
        lse_n = jnp.concatenate([near_in[side, t : t + 1, :] for t in range(tiles)], axis=1)
        dot_n = jnp.concatenate([near_in[side, tiles + t : tiles + t + 1, :] for t in range(tiles)], axis=1)
        s = dot_nt(kpad[own, :], qpad[rows, :]) * scale
        s = jnp.where(within, s, NEG) + jnp.where(rowflag[:, 0:1] > 0.5, NEG, 0.0)
        p = jnp.exp(s - (lse_n + outside))
        ds = (p * (dot_nt(vpad[own, :], dopad[rows, :]) - dot_n)).astype(BF16)
        dkown[...] += dot_nn(ds, qpad[rows, :])
        dvown[...] += dot_nn(p.astype(BF16), dopad[rows, :])

    over_row = iota((ROWS, count), 0)

    def overflow(partial, arrays):
        z_over = jnp.zeros((ROWS, width), F32)
        for a in range(arrays):
            mine = jnp.where((over_row >> 2) == a, spread_over[...], 0.0).astype(BF16)
            z_over = z_over + dot_nn(mine, partial[:, a * width : (a + 1) * width])
        return z_over.astype(BF16)

    def paired(own_ref, sib_ref, order, arrays, ref, land, peers):
        groups = len(order) + 1
        over = (own_ref[0, arrays * groups].astype(F32) + sib_ref[arrays * groups].astype(F32)).astype(BF16)
        sent = []
        for d in order + [0]:
            tiles_of = pl.ds(d * arrays, arrays)
            ref[d, 0:arrays] = (own_ref[0, tiles_of].astype(F32) + sib_ref[tiles_of].astype(F32)).astype(BF16)
            ref[d, arrays] = over
            if d > 0:
                sent.append(send(ref.at[d], land.at[d - 1], peers[d - 1]))
        return sent

    deep = xn * SLOTS // ROWS
    partial = jnp.concatenate([dkg, dvg], axis=1).astype(BF16)
    z = dot_nn(spread[1], partial).astype(BF16)
    z_over = overflow(partial, 2)
    for half in range(2):
        for e in range(yn):
            base = (half * yn + e) * deep * ROWS
            for a in range(2):
                mine = z[base : base + deep * ROWS, a * width : (a + 1) * width]
                z2_own[half, (e * 2 + a) * deep : (e * 2 + a + 1) * deep] = mine.reshape(deep, ROWS, width)
        z2_own[half, 2 * deep * yn] = z_over
    z2_copy = send(z2_own.at[1], z2_sib, sibling)

    stat_sib.wait_recv()
    store(st_x, join([st_own[...], st_sib[...]]))
    stat_x = [send(st_x, st_xin.at[d - 1], x_peers[d - 1]) for d in x_order]

    pair_top = st_x[0:2, :]
    w = jnp.exp(sg_scr[...] - row_of(pair_top))
    w16 = w.astype(BF16)
    ds16 = (w * gw_scr[...]).astype(BF16)
    value_key = dot_tn(w16, jnp.concatenate([vpad[own, :], kpad[own, :]], axis=1))
    partial = [value_key[:, :width], dot_tn(ds16, kpad[own, :]), value_key[:, width:]]
    partial = jnp.concatenate(partial, axis=1).astype(BF16)
    z = dot_nn(spread[0], partial).astype(BF16)
    z_over = overflow(partial, 3)
    for half in range(2):
        for d in range(xn):
            base = (half * xn + d) * ROWS
            for a in range(3):
                z1_own[half, d * 3 + a] = z[base : base + ROWS, a * width : (a + 1) * width]
        z1_own[half, 3 * xn] = z_over
    z1_copy = send(z1_own.at[1], z1_sib, sibling)

    z2_copy.wait_recv()
    t2_copies = paired(z2_own, z2_sib, y_order, 2 * deep, t2_own, t2_in, y_peers)
    keep(o_scr, o_out)
    z1_copy.wait_recv()
    t1_copies = paired(z1_own, z1_sib, x_order, 3, t1_own, t1_in, x_peers)

    after()
    keep(dq_scr, dq_out)

    for copy in stat_x:
        copy.wait_recv()
    store(st_y, join([st_x[...]] + [st_xin[d - 1] for d in range(1, xn)]))
    stat_y = [send(st_y, st_yin.at[e - 1], y_peers[e - 1]) for e in y_order]

    def arrange(groups, depth, wanted, overflow_at, places):
        goal, source = iota((groups * ROWS, places), 0), iota((groups * ROWS, places), 1)
        goal_to, goal_array, goal_slot = goal >> 4, (goal >> 2) & 1, goal & 3
        hit = jnp.zeros(goal.shape, F32)
        for array, tile in wanted:
            at = jnp.where(
                (goal & 15) >= 8,
                overflow_at + tile * SLOTS + goal_slot,
                tile * depth * ROWS + goal_to * SLOTS + goal_slot,
            )
            hit = hit + jnp.where((goal_array == array) & (source == at), 1.0, 0.0)
        return hit.astype(BF16)

    arrived(far_halos)
    for copy in near:
        copy.wait_recv()
    from_neighbour(0)
    from_neighbour(1)

    arrange_1 = arrange(yn, 1, ((0, 0), (1, 1), (1, 2)), 3 * ROWS, 4 * ROWS)
    arrange_2 = arrange(xn, deep, ((0, 0), (1, 1)), 2 * deep * ROWS, (2 * deep + 1) * ROWS)

    for copy in t2_copies:
        copy.wait_recv()
    column = t2_own[0].astype(F32)
    for e in range(1, yn):
        column = column + t2_in[e - 1].astype(F32)
    v = dot_nn(arrange_2, column.reshape((2 * deep + 1) * ROWS, width).astype(BF16)).astype(BF16)
    v_own[...] = v.reshape(xn, ROWS, width)
    v_copies = [send(v_own.at[d], v_in.at[d - 1], x_peers[d - 1]) for d in x_order]

    for copy in stat_y:
        copy.wait_recv()
    joined, summed, dotted = join([st_y[...]] + [st_yin[e - 1] for e in range(1, yn)])
    lse = row_of(joined + jnp.log(summed))
    ratio = row_of(dotted / summed)
    line = iota((4 * ROWS, count), 0)
    line_key = jnp.where(line < 3 * ROWS, line & (ROWS - 1), beyond + (line & 3))
    kind = jnp.where(line < 3 * ROWS, line >> 4, (line >> 2) & 3)
    found = jnp.where(line_key == key_r, 1.0, 0.0)
    found = found * jnp.where(kind == 2, -ratio, jnp.where(kind == 3, 0.0, 1.0))
    column = jnp.zeros((4 * ROWS, width), F32)
    for d in range(xn):
        pair = st_x[0:2, :] if d == 0 else st_xin[d - 1, 0:2, :]
        fall = row_of(jnp.exp(pair - joined) / summed)
        factor = jnp.sum(found * fall, axis=1, keepdims=True)
        f_scr[d] = jnp.broadcast_to(factor, (4 * ROWS, width))

    for copy in t1_copies:
        copy.wait_recv()
    for d in range(xn):
        mine = t1_own[0] if d == 0 else t1_in[d - 1]
        column = column + mine.astype(F32).reshape(4 * ROWS, width) * f_scr[d]
    upper = column.astype(BF16)
    lower = (column - upper.astype(F32)).astype(BF16)
    u = (dot_nn(arrange_1, upper) + dot_nn(arrange_1, lower)).astype(BF16)
    u_own[...] = u.reshape(yn, ROWS, width)
    u_copies = [send(u_own.at[e], u_in.at[e - 1], y_peers[e - 1]) for e in y_order]

    w = jnp.exp(sg_scr[...] - lse)
    dvown[...] += dot_nn(w.astype(BF16), glob[3])
    dkown[...] = (dkown[...] + dot_nn((w * (gw_scr[...] - ratio)).astype(BF16), glob[0])) * scale
    keep(dkown, dk_out)
    keep(dvown, dv_out)

    for copy in v_copies:
        copy.wait_recv()
    late = v_own[0].astype(F32)
    for d in range(1, xn):
        late = late + v_in[d - 1].astype(F32)
    for copy in u_copies:
        copy.wait_recv()
    early = u_own[0].astype(F32)
    for e in range(1, yn):
        early = early + u_in[e - 1].astype(F32)
    for part in range(2):
        r_scr[part * ROWS : part * ROWS + 8, :] = early[part * 8 : part * 8 + 8]
        r_scr[part * ROWS + 8 : part * ROWS + 16, :] = late[part * 8 : part * 8 + 8]
    keep(r_scr, r_out)

    for copy in stores:
        copy.wait()
    for copy in copies:
        copy.wait_send()
    for copy, there in halos:
        pl.when(there)(copy.wait_send)


def finish(scale, o_ref, dq_in, dk_in, dv_in, hot_ref, flag_ref, r_ref, out_ref, dq_ref, dk_ref, dv_ref, total):
    tok = o_ref.shape[0]
    total[...] = jnp.zeros_like(total)
    total[0 : 2 * ROWS, :] = r_ref[...]
    upper = total[...].astype(BF16)
    lower = (total[...] - upper.astype(F32)).astype(BF16)
    hot = hot_ref[...].astype(F32)
    lane_array = (iota((tok, TILE), 1) >> 2) & 3

    def placed(a):
        mine = jnp.where(lane_array == a, hot, 0.0).astype(BF16)
        return dot_nn(mine, upper) + dot_nn(mine, lower)

    out_ref[...] = jnp.where(flag_ref[...] > 0.5, placed(0), o_ref[...]).astype(BF16)
    dq_ref[...] = dq_in[...] + placed(1) * scale
    dk_ref[...] = dk_in[...] + placed(2) * scale
    dv_ref[...] = dv_in[...] + placed(3)


def shards(n, query_rows, key_rows, value_rows, out_grad, global_pos):
    tok, _, width = query_rows.shape
    count = global_pos.shape[0]
    yn = 4
    xn = n // (2 * yn)
    deep = xn * SLOTS // ROWS
    window = tok + 2 * HALF
    span = TILE + 2 * HALF
    copies = 4 * (xn - 1) + 4 * (yn - 1) + 20
    vmem = pl.BlockSpec(memory_space=pltpu.VMEM)
    anywhere = pl.BlockSpec(memory_space=pl.ANY)
    flat = [x.reshape(tok, width) for x in (query_rows, key_rows, value_rows, out_grad)]
    rows_f32 = jax.ShapeDtypeStruct((tok, width), F32)
    middle = pl.pallas_call(
        functools.partial(kernel, (n, yn, xn, tok, count, width)),
        name="sparse_attention",
        out_shape=(rows_f32,) * 4
        + (
            jax.ShapeDtypeStruct((tok, TILE), BF16),
            rows_f32,
            jax.ShapeDtypeStruct((2 * ROWS, width), F32),
        ),
        in_specs=[pl.BlockSpec(memory_space=pltpu.HBM)] * 5,
        out_specs=(anywhere,) * 7,
        scratch_shapes=[
            pltpu.VMEM((1, count), I32),
            pltpu.VMEM((window, width), BF16),
            pltpu.VMEM((window, width), BF16),
            pltpu.VMEM((window, width), BF16),
            pltpu.VMEM((window, width), BF16),
            pltpu.VMEM((tok, width), BF16),
            pltpu.VMEM((1, window), F32),
            pltpu.VMEM((tok, width), F32),
            pltpu.VMEM((2, ROWS, width), BF16),
            pltpu.VMEM((xn, 2, ROWS, width), BF16),
            pltpu.VMEM((2, yn, xn + 1, ROWS, width), BF16),
            pltpu.VMEM((2, 4, count, yn * (xn + 1) * ROWS), BF16),
            pltpu.VMEM((4, count, width), F32),
            pltpu.VMEM((4, count, width), BF16),
            pltpu.VMEM((tok, span), F32),
            pltpu.VMEM((tok, width), F32),
            pltpu.VMEM((tok, span), F32),
            pltpu.VMEM((tok, width), F32),
            pltpu.VMEM((tok, width), F32),
            pltpu.VMEM((tok, width), F32),
            pltpu.VMEM((tok, width), F32),
            pltpu.VMEM((tok, count), F32),
            pltpu.VMEM((tok, count), F32),
            pltpu.VMEM((8, TILE), F32),
            pltpu.VMEM((8, TILE), F32),
            pltpu.VMEM((8, TILE), F32),
            pltpu.VMEM((xn - 1, 8, TILE), F32),
            pltpu.VMEM((8, TILE), F32),
            pltpu.VMEM((yn - 1, 8, TILE), F32),
            pltpu.VMEM((tok, width), F32),
            pltpu.VMEM((tok, width), F32),
            pltpu.VMEM((2, 2 * xn * yn * SLOTS, count), BF16),
            pltpu.VMEM((ROWS, count), F32),
            pltpu.VMEM((tok, TILE), BF16),
            pltpu.VMEM((2, 3 * xn + 1, ROWS, width), BF16),
            pltpu.VMEM((3 * xn + 1, ROWS, width), BF16),
            pltpu.VMEM((xn, 4, ROWS, width), BF16),
            pltpu.VMEM((xn - 1, 4, ROWS, width), BF16),
            pltpu.VMEM((2, 2 * deep * yn + 1, ROWS, width), BF16),
            pltpu.VMEM((2 * deep * yn + 1, ROWS, width), BF16),
            pltpu.VMEM((yn, 2 * deep + 1, ROWS, width), BF16),
            pltpu.VMEM((yn - 1, 2 * deep + 1, ROWS, width), BF16),
            pltpu.VMEM((xn, 4 * ROWS, width), F32),
            pltpu.VMEM((yn, ROWS, width), BF16),
            pltpu.VMEM((yn - 1, ROWS, width), BF16),
            pltpu.VMEM((xn, ROWS, width), BF16),
            pltpu.VMEM((xn - 1, ROWS, width), BF16),
            pltpu.VMEM((2 * ROWS, width), F32),
            pltpu.VMEM((8, TILE), F32),
            pltpu.VMEM((2, 8, TILE), F32),
            pltpu.SemaphoreType.DMA((copies,)),
            pltpu.SemaphoreType.DMA((copies,)),
            pltpu.SemaphoreType.DMA((8,)),
            pltpu.SemaphoreType.DMA((8,)),
            pltpu.SemaphoreType.DMA((5,)),
            pltpu.SemaphoreType.DMA((7,)),
        ],
        compiler_params=pltpu.CompilerParams(
            collective_id=0, has_side_effects=True, vmem_limit_bytes=24 << 20
        ),
    )(*[pltpu.with_memory_space_constraint(x, pltpu.HBM) for x in (global_pos.reshape(1, count), *flat)])
    results = pl.pallas_call(
        functools.partial(finish, width**-0.5),
        name="place_global_rows",
        out_shape=(jax.ShapeDtypeStruct((tok, width), BF16),) + (rows_f32,) * 3,
        in_specs=[vmem] * 7,
        out_specs=(vmem,) * 4,
        scratch_shapes=[pltpu.VMEM((TILE, width), F32)],
        compiler_params=pltpu.CompilerParams(vmem_limit_bytes=8 << 20),
    )(*middle)
    return tuple(x.reshape(tok, 1, width) for x in results)


def solution(mesh):
    rows = P("ctx", "head", None)
    return jax.shard_map(
        functools.partial(shards, mesh.shape["ctx"]),
        mesh=mesh,
        in_specs=(rows,) * 4 + (P(),),
        out_specs=(rows,) * 4,
        check_vma=False,
    )
```

```python
import functools

import jax
import jax.numpy as jnp
from jax import lax
from jax.experimental import pallas as pl
from jax.experimental.pallas import tpu as pltpu
from jax.sharding import PartitionSpec as P

MESH = pl.DeviceIdType.MESH
HALF = 512
TILE = 128
SLOTS = 4
ROWS = 16
NEG = -1e30
F32 = jnp.float32
BF16 = jnp.bfloat16
I32 = jnp.int32


def dot_nn(a, b):
    return lax.dot_general(a, b, (((1,), (0,)), ((), ())), preferred_element_type=F32)


def dot_nt(a, b):
    return lax.dot_general(a, b, (((1,), (1,)), ((), ())), preferred_element_type=F32)


def dot_tn(a, b):
    return lax.dot_general(a, b, (((0,), (0,)), ((), ())), preferred_element_type=F32)


def iota(shape, dim):
    return lax.broadcasted_iota(I32, shape, dim)


def one_hot(cond):
    return jnp.where(cond, 1.0, 0.0).astype(BF16)


def kernel(
    sizes,
    pos_hbm,
    q_hbm,
    k_hbm,
    v_hbm,
    do_hbm,
    o_out,
    dq_out,
    dk_out,
    dv_out,
    hot_out,
    flag_out,
    r_out,
    pos_scr,
    qpad,
    dopad,
    kpad,
    vpad,
    lgrad,
    colbias,
    rowflag,
    pack,
    gx,
    gath,
    pick,
    glob_part,
    glob,
    p_scr,
    ow_scr,
    d_scr,
    m_scr,
    l_scr,
    o_scr,
    dq_scr,
    sg_scr,
    gw_scr,
    st_own,
    st_sib,
    st_x,
    st_xin,
    st_y,
    st_yin,
    dkown,
    dvown,
    spread,
    spread_over,
    hot_scr,
    z1_own,
    z1_sib,
    t1_own,
    t1_in,
    z2_own,
    z2_sib,
    t2_own,
    t2_in,
    f_scr,
    u_own,
    u_in,
    v_own,
    v_in,
    r_scr,
    near_out,
    near_in,
    send_sem,
    recv_sem,
    halo_send,
    halo_recv,
    load_sem,
    store_sem,
):
    n, yn, xn, tok, count, width = sizes
    seq = n * tok
    scale = width**-0.5
    x_shift = xn.bit_length() - 1
    tok_shift = tok.bit_length() - 1
    window = tok + 2 * HALF
    span = TILE + 2 * HALF
    tiles = tok // TILE
    own = pl.ds(HALF, tok)

    me = lax.axis_index("ctx")
    core = lax.rem(me, 2)
    xx = lax.rem(lax.div(me, 2), xn)
    yy = lax.div(me, 2 * xn)

    def ctx_id(y, x, c):
        return (y * xn + x) * 2 + c

    x_peers = [ctx_id(yy, lax.rem(xx + d, xn), core) for d in range(1, xn)]
    y_peers = [ctx_id(lax.rem(yy + e, yn), xx, core) for e in range(1, yn)]
    sibling = me + 1 - 2 * core
    right = lax.rem(me + 1, n)
    left = lax.rem(me + n - 1, n)
    x_order = sorted(range(1, xn), key=lambda d: -min(d, xn - d))
    y_order = sorted(range(1, yn), key=lambda e: -min(e, yn - e))
    greeted = [x_peers[d - 1] for d in x_order] + [y_peers[e - 1] for e in y_order] + [left, right]

    barrier = pltpu.get_barrier_semaphore()
    for peer in greeted:
        pl.semaphore_signal(barrier, inc=1, device_id={"ctx": peer}, device_id_type=MESH)

    loads = [
        pltpu.make_async_copy(src, dst, load_sem.at[i])
        for i, (src, dst) in enumerate(
            (
                (pos_hbm, pos_scr),
                (q_hbm, qpad.at[own]),
                (k_hbm, kpad.at[own]),
                (v_hbm, vpad.at[own]),
                (do_hbm, dopad.at[own]),
            )
        )
    ]
    for load in loads:
        load.start()

    copies = []

    def send(src, dst, peer):
        number = len(copies)
        copy = pltpu.make_async_remote_copy(
            src_ref=src,
            dst_ref=dst,
            send_sem=send_sem.at[number],
            recv_sem=recv_sem.at[number],
            device_id={"ctx": peer},
            device_id_type=MESH,
        )
        copy.start()
        copies.append(copy)
        return copy

    stores = []

    def keep(src, dst):
        copy = pltpu.make_async_copy(src, dst, store_sem.at[len(stores)])
        copy.start()
        stores.append(copy)

    loads[0].wait()
    pos_r = pos_scr[...]
    first, second = iota((count, count), 0), iota((count, count), 1)
    pos_c = jnp.sum(jnp.where(first == second, pos_r.astype(F32), 0.0), axis=1, keepdims=True).astype(I32)
    owner_c, owner_r = pos_c >> tok_shift, pos_r >> tok_shift
    local_c, local_r = pos_c & (tok - 1), pos_r & (tok - 1)
    same = owner_c == owner_r
    rank_c = jnp.sum(jnp.where(same & (second < first), 1.0, 0.0), axis=1, keepdims=True).astype(I32)
    rank_r = jnp.sum(jnp.where(same & (first < second), 1.0, 0.0), axis=0, keepdims=True).astype(I32)

    rho = iota((2 * ROWS, count), 0)
    slot_rank = ((rho >> 4) << 2) + (rho & 3)
    chosen = (owner_r == me) & (rank_r == slot_rank)
    slot_col = jnp.sum(jnp.where(chosen, (local_r + 1).astype(F32), 0.0), axis=1, keepdims=True).astype(I32) - 1
    array_of = (iota((2 * ROWS, tok), 0) >> 2) & 3
    at_slot = iota((2 * ROWS, tok), 1) == slot_col
    picked = jnp.zeros((2 * ROWS, width), F32)
    for load in loads[1:]:
        load.wait()
    for a, rows in enumerate((qpad[own, :], kpad[own, :], vpad[own, :], dopad[own, :])):
        picked = picked + dot_nn(one_hot(at_slot & (array_of == a)), rows)
    pack[...] = picked.astype(BF16).reshape(2, ROWS, width)
    gx[0] = pack[...]

    pl.semaphore_wait(barrier, len(greeted))

    from_x = [send(pack, gx.at[d], x_peers[d - 1]) for d in x_order]
    to_right, to_left = me < n - 1, me > 0
    below, above = pl.ds(0, HALF), pl.ds(HALF + tok, HALF)

    def exchange(ref):
        pairs = []
        for peer, there, back, dst in ((right, to_right, to_left, below), (left, to_left, to_right, above)):
            number = len(halos)
            copy = pltpu.make_async_remote_copy(
                src_ref=ref.at[own],
                dst_ref=ref.at[dst],
                send_sem=halo_send.at[number],
                recv_sem=halo_recv.at[number],
                device_id={"ctx": peer},
                device_id_type=MESH,
            )
            pl.when(there)(copy.start)
            halos.append((copy, there))
            pairs.append((copy, back))
        return pairs

    halos = []

    def arrived(pairs):
        for copy, there in pairs:
            pl.when(there)(copy.wait_recv)

    @pl.when(me == 0)
    def _():
        for ref in (kpad, vpad, qpad, dopad):
            ref[below, :] = jnp.zeros((HALF, width), BF16)

    @pl.when(me == n - 1)
    def _():
        for ref in (kpad, vpad, qpad, dopad):
            ref[above, :] = jnp.zeros((HALF, width), BF16)

    near_halos = exchange(kpad) + exchange(vpad)

    for part in range(window // 512):
        reach = me * tok - HALF + part * 512 + iota((1, 512), 1)
        bias = jnp.min(jnp.where(pos_c == reach, NEG, 0.0), axis=0, keepdims=True)
        inside = (reach >= 0) & (reach < seq)
        colbias[:, pl.ds(part * 512, 512)] = jnp.where(inside, bias, NEG)
    row_pos = me * tok + iota((tok, 1), 0)
    flag = jnp.max(jnp.where(row_pos == pos_r, 1.0, 0.0), axis=1, keepdims=True)
    rowflag[...] = jnp.broadcast_to(flag, (tok, width))
    lgrad[...] = jnp.where(rowflag[...] > 0.5, 0.0, dopad[own, :].astype(F32)).astype(BF16)

    for copy in from_x:
        copy.wait_recv()
    over = gx[0, 1].astype(F32)
    gath[0, 0, 0] = gx[0, 0]
    for d in range(1, xn):
        gath[0, 0, d] = gx[d, 0]
        over = over + gx[d, 1].astype(F32)
    gath[0, 0, xn] = over.astype(BF16)
    from_y = {e: send(gath.at[0, 0], gath.at[0, e], y_peers[e - 1]) for e in y_order}
    from_sib = [send(gath.at[0, 0], gath.at[1, 0], sibling)]
    far_halos = exchange(qpad) + exchange(dopad)

    core_c, xo_c, yo_c = owner_c & 1, (owner_c >> 1) & (xn - 1), owner_c >> (1 + x_shift)
    half_total = yn * (xn + 1) * ROWS
    from_row = (yy - yo_c) & (yn - 1)
    src_c = (core_c ^ core) * half_total + jnp.where(
        rank_c < SLOTS,
        (from_row * (xn + 1) + ((xx - xo_c) & (xn - 1))) * ROWS + rank_c,
        (from_row * (xn + 1) + xn) * ROWS + rank_c - SLOTS,
    )
    for half in range(2):
        tile_row = iota((count, half_total), 1) + half * half_total
        for a in range(4):
            pick[half, a] = one_hot(tile_row == src_c + SLOTS * a)

    core_r, xo_r, yo_r = owner_r & 1, (owner_r >> 1) & (xn - 1), owner_r >> (1 + x_shift)
    place = ((core_r ^ core) * xn + ((xo_r - xx) & (xn - 1))) * yn + ((yo_r - yy) & (yn - 1))
    beyond = 2 * xn * yn * SLOTS
    key_r = jnp.where(rank_r < SLOTS, place * SLOTS + rank_r, beyond + rank_r - SLOTS)
    spread[0] = one_hot(iota((beyond, count), 0) == key_r)
    turned = ((core_r ^ core) * yn + ((yo_r - yy) & (yn - 1))) * xn + ((xo_r - xx) & (xn - 1))
    turned_r = jnp.where(rank_r < SLOTS, turned * SLOTS + rank_r, beyond + rank_r - SLOTS)
    spread[1] = one_hot(iota((beyond, count), 0) == turned_r)
    spread_over[...] = jnp.where(beyond + (iota((ROWS, count), 0) & 3) == key_r, 1.0, 0.0)

    rho_lane = iota((count, TILE), 1)
    lane_rank = ((rho_lane >> 4) << 2) + (rho_lane & 3)
    chosen_c = (owner_c == me) & (rank_c == lane_rank) & (rho_lane < 2 * ROWS)
    slot_row = jnp.sum(jnp.where(chosen_c, (local_c + 1).astype(F32), 0.0), axis=0, keepdims=True).astype(I32) - 1
    hot_scr[...] = one_hot(iota((tok, TILE), 0) == slot_row)
    keep(hot_scr, hot_out)
    keep(rowflag, flag_out)

    arrived(near_halos)

    lane = iota((TILE, TILE), 1)
    sub = iota((TILE, TILE), 0)
    low_bias = jnp.where(lane >= sub, 0.0, NEG)
    high_bias = jnp.where(lane <= sub, 0.0, NEG)

    def before(t, carry):
        start = pl.multiple_of(t * TILE, TILE)
        rows, keys = pl.ds(start, TILE), pl.ds(start, span)
        s = dot_nt(qpad[pl.ds(HALF + start, TILE), :], kpad[keys, :]) * scale + colbias[:, keys]
        s = jnp.concatenate(
            [s[:, :TILE] + low_bias, s[:, TILE : 2 * HALF], s[:, 2 * HALF :] + high_bias], axis=1
        )
        top = jnp.max(s, axis=1, keepdims=True)
        p = jnp.exp(s - top)
        p_scr[rows, :] = p
        ow_scr[rows, :] = dot_nn(p.astype(BF16), vpad[keys, :])
        m_scr[rows, :] = jnp.broadcast_to(top, (TILE, width))
        l_scr[rows, :] = jnp.broadcast_to(jnp.sum(p, axis=1, keepdims=True), (TILE, width))
        d_scr[rows, :] = dot_nt(lgrad[rows, :], vpad[keys, :])
        return carry

    lax.fori_loop(0, tiles, before, 0)

    for e in reversed(y_order):
        from_y[e].wait_recv()
        from_sib.append(send(gath.at[0, e], gath.at[1, e], sibling))
    half_tiles = gath[0].reshape(half_total, width)
    for a in range(4):
        glob_part[a] = dot_nn(pick[0, a], half_tiles)
    for copy in from_sib:
        copy.wait_recv()
    half_tiles = gath[1].reshape(half_total, width)
    for a in range(4):
        glob[a] = (glob_part[a] + dot_nn(pick[1, a], half_tiles)).astype(BF16)

    middle = (jnp.sum(glob[2].astype(F32), axis=0, keepdims=True) * (1.0 / count)).astype(BF16)
    centre = dot_nt(jnp.broadcast_to(middle, (ROWS, width)), glob[3])[0:1, :]
    sg = dot_nt(kpad[own, :], glob[0]) * scale
    gw = dot_nt(vpad[own, :], glob[3]) - centre
    sg_scr[...] = sg
    gw_scr[...] = gw
    top = jnp.max(sg, axis=0, keepdims=True)
    p = jnp.exp(sg - top)
    stat_rows = [top, jnp.sum(p, axis=0, keepdims=True), jnp.sum(p * gw, axis=0, keepdims=True)]
    for r, row in enumerate(stat_rows):
        st_own[2 * r : 2 * r + 1, :] = row[:, :TILE]
        st_own[2 * r + 1 : 2 * r + 2, :] = row[:, TILE:]
    st_own[6:8, :] = jnp.zeros((2, TILE), F32)

    def join(parts):
        joined = functools.reduce(jnp.maximum, [part[0:2, :] for part in parts])
        weigh = [jnp.exp(part[0:2, :] - joined) for part in parts]
        return (
            joined,
            sum(part[2:4, :] * w for part, w in zip(parts, weigh)),
            sum(part[4:6, :] * w for part, w in zip(parts, weigh)),
        )

    def store(ref, stats):
        for r, part in enumerate(stats):
            ref[2 * r : 2 * r + 2, :] = part
        ref[6:8, :] = jnp.zeros((2, TILE), F32)

    def row_of(part):
        return jnp.concatenate([part[0:1], part[1:2]], axis=1)

    stat_sib = send(st_own, st_sib, sibling)

    lg = lgrad[...]
    s = dot_nt(qpad[own, :], glob[1]) * scale
    top_w = m_scr[:, 0:1]
    top = jnp.maximum(top_w, jnp.max(s, axis=1, keepdims=True))
    pg = jnp.exp(s - top)
    down = jnp.exp(top_w - top)
    all_sum = l_scr[:, 0:1] * down + jnp.sum(pg, axis=1, keepdims=True)
    inv = 1.0 / all_sum
    pg = pg * inv
    pg16 = pg.astype(BF16)
    o = ow_scr[...] * (down * inv) + dot_nn(pg16, glob[2])
    o_scr[...] = o
    row_dot = jnp.sum(lg.astype(F32) * o, axis=1, keepdims=True)
    dsg = (pg * (dot_nt(lg, glob[2]) - row_dot)).astype(BF16)
    m_scr[...] = jnp.broadcast_to(down * inv, (tok, width))
    l_scr[...] = jnp.broadcast_to(row_dot, (tok, width))
    dkg = dot_tn(dsg, qpad[own, :])
    dvg = dot_tn(pg16, lg)
    dq_scr[...] = dot_nn(dsg, glob[1])

    row_lse = jnp.where(rowflag[:, 0:1] > 0.5, -NEG, top + jnp.log(all_sum))
    for t in range(tiles):
        for r, column in enumerate((row_lse, row_dot)):
            mine = column[t * TILE : (t + 1) * TILE]
            near_out[r * tiles + t : r * tiles + t + 1, :] = jnp.sum(
                jnp.where(lane == sub, mine, 0.0), axis=0, keepdims=True
            )
    near = [send(near_out, near_in.at[0], right), send(near_out, near_in.at[1], left)]

    def after():
        dk = jnp.zeros((tok, width), F32)
        dv = jnp.zeros((tok, width), F32)
        for t in range(tiles):
            start = t * TILE
            rows, keys = pl.ds(start, TILE), pl.ds(start, span)
            pw = p_scr[rows, :] * m_scr[rows, 0:1]
            dsw = (pw * (d_scr[rows, :] - l_scr[rows, 0:1])).astype(BF16)
            dq_scr[rows, :] = (dq_scr[rows, :] + dot_nn(dsw, kpad[keys, :])) * scale
            first_own = HALF - start
            dk = dk + dot_tn(dsw[:, first_own : first_own + tok], qpad[pl.ds(HALF + start, TILE), :])
            dv = dv + dot_tn(pw[:, first_own : first_own + tok].astype(BF16), lgrad[rows, :])
        dkown[...] = dk
        dvown[...] = dv

    def from_neighbour(side):
        rows = pl.ds(side * (HALF + tok), HALF)
        key_at, query_at = iota((tok, HALF), 0), iota((tok, HALF), 1)
        within = key_at <= query_at if side == 0 else key_at >= query_at
        there = me > 0 if side == 0 else me < n - 1
        outside = jnp.where(there, 0.0, -NEG)
        lse_n = jnp.concatenate([near_in[side, t : t + 1, :] for t in range(tiles)], axis=1)
        dot_n = jnp.concatenate([near_in[side, tiles + t : tiles + t + 1, :] for t in range(tiles)], axis=1)
        s = dot_nt(kpad[own, :], qpad[rows, :]) * scale
        s = jnp.where(within, s, NEG) + jnp.where(rowflag[:, 0:1] > 0.5, NEG, 0.0)
        p = jnp.exp(s - (lse_n + outside))
        ds = (p * (dot_nt(vpad[own, :], dopad[rows, :]) - dot_n)).astype(BF16)
        dkown[...] += dot_nn(ds, qpad[rows, :])
        dvown[...] += dot_nn(p.astype(BF16), dopad[rows, :])

    over_row = iota((ROWS, count), 0)

    def overflow(partial, arrays):
        z_over = jnp.zeros((ROWS, width), F32)
        for a in range(arrays):
            mine = jnp.where((over_row >> 2) == a, spread_over[...], 0.0).astype(BF16)
            z_over = z_over + dot_nn(mine, partial[:, a * width : (a + 1) * width])
        return z_over.astype(BF16)

    def paired(own_ref, sib_ref, order, arrays, ref, land, peers):
        groups = len(order) + 1
        over = (own_ref[0, arrays * groups].astype(F32) + sib_ref[arrays * groups].astype(F32)).astype(BF16)
        sent = []
        for d in order + [0]:
            tiles_of = pl.ds(d * arrays, arrays)
            ref[d, 0:arrays] = (own_ref[0, tiles_of].astype(F32) + sib_ref[tiles_of].astype(F32)).astype(BF16)
            ref[d, arrays] = over
            if d > 0:
                sent.append(send(ref.at[d], land.at[d - 1], peers[d - 1]))
        return sent

    deep = xn * SLOTS // ROWS
    partial = jnp.concatenate([dkg, dvg], axis=1).astype(BF16)
    z = dot_nn(spread[1], partial).astype(BF16)
    z_over = overflow(partial, 2)
    for half in range(2):
        for e in range(yn):
            base = (half * yn + e) * deep * ROWS
            for a in range(2):
                mine = z[base : base + deep * ROWS, a * width : (a + 1) * width]
                z2_own[half, (e * 2 + a) * deep : (e * 2 + a + 1) * deep] = mine.reshape(deep, ROWS, width)
        z2_own[half, 2 * deep * yn] = z_over
    z2_copy = send(z2_own.at[1], z2_sib, sibling)

    stat_sib.wait_recv()
    store(st_x, join([st_own[...], st_sib[...]]))
    stat_x = [send(st_x, st_xin.at[d - 1], x_peers[d - 1]) for d in x_order]

    pair_top = st_x[0:2, :]
    w = jnp.exp(sg_scr[...] - row_of(pair_top))
    w16 = w.astype(BF16)
    ds16 = (w * gw_scr[...]).astype(BF16)
    value_key = dot_tn(w16, jnp.concatenate([vpad[own, :], kpad[own, :]], axis=1))
    partial = [value_key[:, :width], dot_tn(ds16, kpad[own, :]), value_key[:, width:]]
    partial = jnp.concatenate(partial, axis=1).astype(BF16)
    z = dot_nn(spread[0], partial).astype(BF16)
    z_over = overflow(partial, 3)
    for half in range(2):
        for d in range(xn):
            base = (half * xn + d) * ROWS
            for a in range(3):
                z1_own[half, d * 3 + a] = z[base : base + ROWS, a * width : (a + 1) * width]
        z1_own[half, 3 * xn] = z_over
    z1_copy = send(z1_own.at[1], z1_sib, sibling)

    z2_copy.wait_recv()
    t2_copies = paired(z2_own, z2_sib, y_order, 2 * deep, t2_own, t2_in, y_peers)
    keep(o_scr, o_out)
    z1_copy.wait_recv()
    t1_copies = paired(z1_own, z1_sib, x_order, 3, t1_own, t1_in, x_peers)

    after()
    keep(dq_scr, dq_out)

    for copy in stat_x:
        copy.wait_recv()
    store(st_y, join([st_x[...]] + [st_xin[d - 1] for d in range(1, xn)]))
    stat_y = [send(st_y, st_yin.at[e - 1], y_peers[e - 1]) for e in y_order]

    def arrange(groups, depth, wanted, overflow_at, places):
        goal, source = iota((groups * ROWS, places), 0), iota((groups * ROWS, places), 1)
        goal_to, goal_array, goal_slot = goal >> 4, (goal >> 2) & 1, goal & 3
        hit = jnp.zeros(goal.shape, F32)
        for array, tile in wanted:
            at = jnp.where(
                (goal & 15) >= 8,
                overflow_at + tile * SLOTS + goal_slot,
                tile * depth * ROWS + goal_to * SLOTS + goal_slot,
            )
            hit = hit + jnp.where((goal_array == array) & (source == at), 1.0, 0.0)
        return hit.astype(BF16)

    arrived(far_halos)
    for copy in near:
        copy.wait_recv()
    from_neighbour(0)
    from_neighbour(1)

    arrange_1 = arrange(yn, 1, ((0, 0), (1, 1), (1, 2)), 3 * ROWS, 4 * ROWS)
    arrange_2 = arrange(xn, deep, ((0, 0), (1, 1)), 2 * deep * ROWS, (2 * deep + 1) * ROWS)

    for copy in t2_copies:
        copy.wait_recv()
    column = t2_own[0].astype(F32)
    for e in range(1, yn):
        column = column + t2_in[e - 1].astype(F32)
    v = dot_nn(arrange_2, column.reshape((2 * deep + 1) * ROWS, width).astype(BF16)).astype(BF16)
    v_own[...] = v.reshape(xn, ROWS, width)
    v_copies = [send(v_own.at[d], v_in.at[d - 1], x_peers[d - 1]) for d in x_order]

    for copy in stat_y:
        copy.wait_recv()
    joined, summed, dotted = join([st_y[...]] + [st_yin[e - 1] for e in range(1, yn)])
    lse = row_of(joined + jnp.log(summed))
    ratio = row_of(dotted / summed)
    line = iota((4 * ROWS, count), 0)
    line_key = jnp.where(line < 3 * ROWS, line & (ROWS - 1), beyond + (line & 3))
    kind = jnp.where(line < 3 * ROWS, line >> 4, (line >> 2) & 3)
    found = jnp.where(line_key == key_r, 1.0, 0.0)
    found = found * jnp.where(kind == 2, -ratio, jnp.where(kind == 3, 0.0, 1.0))
    column = jnp.zeros((4 * ROWS, width), F32)
    for d in range(xn):
        pair = st_x[0:2, :] if d == 0 else st_xin[d - 1, 0:2, :]
        fall = row_of(jnp.exp(pair - joined) / summed)
        factor = jnp.sum(found * fall, axis=1, keepdims=True)
        f_scr[d] = jnp.broadcast_to(factor, (4 * ROWS, width))

    for copy in t1_copies:
        copy.wait_recv()
    for d in range(xn):
        mine = t1_own[0] if d == 0 else t1_in[d - 1]
        column = column + mine.astype(F32).reshape(4 * ROWS, width) * f_scr[d]
    upper = column.astype(BF16)
    lower = (column - upper.astype(F32)).astype(BF16)
    u = (dot_nn(arrange_1, upper) + dot_nn(arrange_1, lower)).astype(BF16)
    u_own[...] = u.reshape(yn, ROWS, width)
    u_copies = [send(u_own.at[e], u_in.at[e - 1], y_peers[e - 1]) for e in y_order]

    w = jnp.exp(sg_scr[...] - lse)
    dvown[...] += dot_nn(w.astype(BF16), glob[3])
    dkown[...] = (dkown[...] + dot_nn((w * (gw_scr[...] - ratio)).astype(BF16), glob[0])) * scale
    keep(dkown, dk_out)
    keep(dvown, dv_out)

    for copy in v_copies:
        copy.wait_recv()
    late = v_own[0].astype(F32)
    for d in range(1, xn):
        late = late + v_in[d - 1].astype(F32)
    for copy in u_copies:
        copy.wait_recv()
    early = u_own[0].astype(F32)
    for e in range(1, yn):
        early = early + u_in[e - 1].astype(F32)
    for part in range(2):
        r_scr[part * ROWS : part * ROWS + 8, :] = early[part * 8 : part * 8 + 8]
        r_scr[part * ROWS + 8 : part * ROWS + 16, :] = late[part * 8 : part * 8 + 8]
    keep(r_scr, r_out)

    for copy in stores:
        copy.wait()
    for copy in copies:
        copy.wait_send()
    for copy, there in halos:
        pl.when(there)(copy.wait_send)


def finish(scale, o_ref, dq_in, dk_in, dv_in, hot_ref, flag_ref, r_ref, out_hbm, dq_hbm, dk_hbm, dv_hbm, total, out_ref, dq_ref, dk_ref, dv_ref, sem):
    tok = o_ref.shape[0]
    total[...] = jnp.zeros_like(total)
    total[0 : 2 * ROWS, :] = r_ref[...]
    upper = total[...].astype(BF16)
    lower = (total[...] - upper.astype(F32)).astype(BF16)
    hot = hot_ref[...].astype(F32)
    lane_array = (iota((tok, TILE), 1) >> 2) & 3

    def placed(a):
        mine = jnp.where(lane_array == a, hot, 0.0).astype(BF16)
        return dot_nn(mine, upper) + dot_nn(mine, lower)

    copies = []

    def put(ref, value, dst):
        ref[...] = value
        copy = pltpu.make_async_copy(ref, dst, sem.at[len(copies)])
        copy.start()
        copies.append(copy)

    put(dq_ref, dq_in[...] + placed(1) * scale, dq_hbm)
    put(dk_ref, dk_in[...] + placed(2) * scale, dk_hbm)
    put(dv_ref, dv_in[...] + placed(3), dv_hbm)
    put(out_ref, jnp.where(flag_ref[...] > 0.5, placed(0), o_ref[...]).astype(BF16), out_hbm)
    for copy in copies:
        copy.wait()


def shards(n, query_rows, key_rows, value_rows, out_grad, global_pos):
    tok, _, width = query_rows.shape
    count = global_pos.shape[0]
    yn = 4
    xn = n // (2 * yn)
    deep = xn * SLOTS // ROWS
    window = tok + 2 * HALF
    span = TILE + 2 * HALF
    copies = 4 * (xn - 1) + 4 * (yn - 1) + 20
    vmem = pl.BlockSpec(memory_space=pltpu.VMEM)
    anywhere = pl.BlockSpec(memory_space=pl.ANY)
    flat = [x.reshape(tok, width) for x in (query_rows, key_rows, value_rows, out_grad)]
    rows_f32 = jax.ShapeDtypeStruct((tok, width), F32)
    middle = pl.pallas_call(
        functools.partial(kernel, (n, yn, xn, tok, count, width)),
        name="sparse_attention",
        out_shape=(rows_f32,) * 4
        + (
            jax.ShapeDtypeStruct((tok, TILE), BF16),
            rows_f32,
            jax.ShapeDtypeStruct((2 * ROWS, width), F32),
        ),
        in_specs=[pl.BlockSpec(memory_space=pltpu.HBM)] * 5,
        out_specs=(anywhere,) * 7,
        scratch_shapes=[
            pltpu.VMEM((1, count), I32),
            pltpu.VMEM((window, width), BF16),
            pltpu.VMEM((window, width), BF16),
            pltpu.VMEM((window, width), BF16),
            pltpu.VMEM((window, width), BF16),
            pltpu.VMEM((tok, width), BF16),
            pltpu.VMEM((1, window), F32),
            pltpu.VMEM((tok, width), F32),
            pltpu.VMEM((2, ROWS, width), BF16),
            pltpu.VMEM((xn, 2, ROWS, width), BF16),
            pltpu.VMEM((2, yn, xn + 1, ROWS, width), BF16),
            pltpu.VMEM((2, 4, count, yn * (xn + 1) * ROWS), BF16),
            pltpu.VMEM((4, count, width), F32),
            pltpu.VMEM((4, count, width), BF16),
            pltpu.VMEM((tok, span), F32),
            pltpu.VMEM((tok, width), F32),
            pltpu.VMEM((tok, span), F32),
            pltpu.VMEM((tok, width), F32),
            pltpu.VMEM((tok, width), F32),
            pltpu.VMEM((tok, width), F32),
            pltpu.VMEM((tok, width), F32),
            pltpu.VMEM((tok, count), F32),
            pltpu.VMEM((tok, count), F32),
            pltpu.VMEM((8, TILE), F32),
            pltpu.VMEM((8, TILE), F32),
            pltpu.VMEM((8, TILE), F32),
            pltpu.VMEM((xn - 1, 8, TILE), F32),
            pltpu.VMEM((8, TILE), F32),
            pltpu.VMEM((yn - 1, 8, TILE), F32),
            pltpu.VMEM((tok, width), F32),
            pltpu.VMEM((tok, width), F32),
            pltpu.VMEM((2, 2 * xn * yn * SLOTS, count), BF16),
            pltpu.VMEM((ROWS, count), F32),
            pltpu.VMEM((tok, TILE), BF16),
            pltpu.VMEM((2, 3 * xn + 1, ROWS, width), BF16),
            pltpu.VMEM((3 * xn + 1, ROWS, width), BF16),
            pltpu.VMEM((xn, 4, ROWS, width), BF16),
            pltpu.VMEM((xn - 1, 4, ROWS, width), BF16),
            pltpu.VMEM((2, 2 * deep * yn + 1, ROWS, width), BF16),
            pltpu.VMEM((2 * deep * yn + 1, ROWS, width), BF16),
            pltpu.VMEM((yn, 2 * deep + 1, ROWS, width), BF16),
            pltpu.VMEM((yn - 1, 2 * deep + 1, ROWS, width), BF16),
            pltpu.VMEM((xn, 4 * ROWS, width), F32),
            pltpu.VMEM((yn, ROWS, width), BF16),
            pltpu.VMEM((yn - 1, ROWS, width), BF16),
            pltpu.VMEM((xn, ROWS, width), BF16),
            pltpu.VMEM((xn - 1, ROWS, width), BF16),
            pltpu.VMEM((2 * ROWS, width), F32),
            pltpu.VMEM((8, TILE), F32),
            pltpu.VMEM((2, 8, TILE), F32),
            pltpu.SemaphoreType.DMA((copies,)),
            pltpu.SemaphoreType.DMA((copies,)),
            pltpu.SemaphoreType.DMA((8,)),
            pltpu.SemaphoreType.DMA((8,)),
            pltpu.SemaphoreType.DMA((5,)),
            pltpu.SemaphoreType.DMA((7,)),
        ],
        compiler_params=pltpu.CompilerParams(
            collective_id=0, has_side_effects=True, vmem_limit_bytes=24 << 20
        ),
    )(*[pltpu.with_memory_space_constraint(x, pltpu.HBM) for x in (global_pos.reshape(1, count), *flat)])
    results = pl.pallas_call(
        functools.partial(finish, width**-0.5),
        name="place_global_rows",
        out_shape=(jax.ShapeDtypeStruct((tok, width), BF16),) + (rows_f32,) * 3,
        in_specs=[vmem] * 7,
        out_specs=(anywhere,) * 4,
        scratch_shapes=[
            pltpu.VMEM((TILE, width), F32),
            pltpu.VMEM((tok, width), BF16),
            pltpu.VMEM((tok, width), F32),
            pltpu.VMEM((tok, width), F32),
            pltpu.VMEM((tok, width), F32),
            pltpu.SemaphoreType.DMA((4,)),
        ],
        compiler_params=pltpu.CompilerParams(vmem_limit_bytes=8 << 20),
    )(*middle)
    return tuple(x.reshape(tok, 1, width) for x in results)


def solution(mesh):
    rows = P("ctx", "head", None)
    return jax.shard_map(
        functools.partial(shards, mesh.shape["ctx"]),
        mesh=mesh,
        in_specs=(rows,) * 4 + (P(),),
        out_specs=(rows,) * 4,
        check_vma=False,
    )
```

```python
import functools

import jax
import jax.numpy as jnp
from jax import lax
from jax.experimental import pallas as pl
from jax.experimental.pallas import tpu as pltpu
from jax.sharding import PartitionSpec as P

MESH = pl.DeviceIdType.MESH
HALF = 512
TILE = 128
SLOTS = 4
ROWS = 16
NEG = -1e30
F32 = jnp.float32
BF16 = jnp.bfloat16
I32 = jnp.int32


def dot_nn(a, b):
    return lax.dot_general(a, b, (((1,), (0,)), ((), ())), preferred_element_type=F32)


def dot_nt(a, b):
    return lax.dot_general(a, b, (((1,), (1,)), ((), ())), preferred_element_type=F32)


def dot_tn(a, b):
    return lax.dot_general(a, b, (((0,), (0,)), ((), ())), preferred_element_type=F32)


def iota(shape, dim):
    return lax.broadcasted_iota(I32, shape, dim)


def one_hot(cond):
    return jnp.where(cond, 1.0, 0.0).astype(BF16)


def kernel(
    sizes,
    pos_hbm,
    q_hbm,
    k_hbm,
    v_hbm,
    do_hbm,
    o_out,
    dq_out,
    dk_out,
    dv_out,
    hot_out,
    flag_out,
    r_out,
    pos_scr,
    qpad,
    dopad,
    kpad,
    vpad,
    lgrad,
    colbias,
    rowflag,
    pack,
    gx,
    gath,
    pick,
    glob_part,
    glob,
    p_scr,
    ow_scr,
    d_scr,
    m_scr,
    l_scr,
    o_scr,
    dq_scr,
    sg_scr,
    gw_scr,
    st_own,
    st_sib,
    st_x,
    st_xin,
    st_y,
    st_yin,
    dkown,
    dvown,
    spread,
    spread_over,
    hot_scr,
    z1_own,
    z1_sib,
    t1_own,
    t1_in,
    z2_own,
    z2_sib,
    t2_own,
    t2_in,
    f_scr,
    u_own,
    u_in,
    v_own,
    v_in,
    r_scr,
    near_out,
    near_in,
    send_sem,
    recv_sem,
    halo_send,
    halo_recv,
    load_sem,
    store_sem,
):
    n, yn, xn, tok, count, width = sizes
    seq = n * tok
    scale = width**-0.5
    x_shift = xn.bit_length() - 1
    tok_shift = tok.bit_length() - 1
    window = tok + 2 * HALF
    span = TILE + 2 * HALF
    tiles = tok // TILE
    own = pl.ds(HALF, tok)

    me = lax.axis_index("ctx")
    core = lax.rem(me, 2)
    xx = lax.rem(lax.div(me, 2), xn)
    yy = lax.div(me, 2 * xn)

    def ctx_id(y, x, c):
        return (y * xn + x) * 2 + c

    x_peers = [ctx_id(yy, lax.rem(xx + d, xn), core) for d in range(1, xn)]
    y_peers = [ctx_id(lax.rem(yy + e, yn), xx, core) for e in range(1, yn)]
    sibling = me + 1 - 2 * core
    right = lax.rem(me + 1, n)
    left = lax.rem(me + n - 1, n)
    greeted = x_peers + y_peers + [left, right]
    x_order = sorted(range(1, xn), key=lambda d: -min(d, xn - d))
    y_order = sorted(range(1, yn), key=lambda e: -min(e, yn - e))

    barrier = pltpu.get_barrier_semaphore()
    for peer in greeted:
        pl.semaphore_signal(barrier, inc=1, device_id={"ctx": peer}, device_id_type=MESH)

    loads = [
        pltpu.make_async_copy(src, dst, load_sem.at[i])
        for i, (src, dst) in enumerate(
            (
                (pos_hbm, pos_scr),
                (q_hbm, qpad.at[own]),
                (k_hbm, kpad.at[own]),
                (v_hbm, vpad.at[own]),
                (do_hbm, dopad.at[own]),
            )
        )
    ]
    for load in loads:
        load.start()

    copies = []

    def send(src, dst, peer):
        number = len(copies)
        copy = pltpu.make_async_remote_copy(
            src_ref=src,
            dst_ref=dst,
            send_sem=send_sem.at[number],
            recv_sem=recv_sem.at[number],
            device_id={"ctx": peer},
            device_id_type=MESH,
        )
        copy.start()
        copies.append(copy)
        return copy

    stores = []

    def keep(src, dst):
        copy = pltpu.make_async_copy(src, dst, store_sem.at[len(stores)])
        copy.start()
        stores.append(copy)

    loads[0].wait()
    pos_r = pos_scr[...]
    first, second = iota((count, count), 0), iota((count, count), 1)
    pos_c = jnp.sum(jnp.where(first == second, pos_r.astype(F32), 0.0), axis=1, keepdims=True).astype(I32)
    owner_c, owner_r = pos_c >> tok_shift, pos_r >> tok_shift
    local_c, local_r = pos_c & (tok - 1), pos_r & (tok - 1)
    same = owner_c == owner_r
    rank_c = jnp.sum(jnp.where(same & (second < first), 1.0, 0.0), axis=1, keepdims=True).astype(I32)
    rank_r = jnp.sum(jnp.where(same & (first < second), 1.0, 0.0), axis=0, keepdims=True).astype(I32)

    rho = iota((2 * ROWS, count), 0)
    slot_rank = ((rho >> 4) << 2) + (rho & 3)
    chosen = (owner_r == me) & (rank_r == slot_rank)
    slot_col = jnp.sum(jnp.where(chosen, (local_r + 1).astype(F32), 0.0), axis=1, keepdims=True).astype(I32) - 1
    array_of = (iota((2 * ROWS, tok), 0) >> 2) & 3
    at_slot = iota((2 * ROWS, tok), 1) == slot_col
    picked = jnp.zeros((2 * ROWS, width), F32)
    for load in loads[1:]:
        load.wait()
    for a, rows in enumerate((qpad[own, :], kpad[own, :], vpad[own, :], dopad[own, :])):
        picked = picked + dot_nn(one_hot(at_slot & (array_of == a)), rows)
    pack[...] = picked.astype(BF16).reshape(2, ROWS, width)
    gx[0] = pack[...]

    pl.semaphore_wait(barrier, len(greeted))

    from_x = [send(pack, gx.at[d], x_peers[d - 1]) for d in x_order]
    to_right, to_left = me < n - 1, me > 0
    below, above = pl.ds(0, HALF), pl.ds(HALF + tok, HALF)

    def exchange(ref):
        pairs = []
        for peer, there, back, dst in ((right, to_right, to_left, below), (left, to_left, to_right, above)):
            number = len(halos)
            copy = pltpu.make_async_remote_copy(
                src_ref=ref.at[own],
                dst_ref=ref.at[dst],
                send_sem=halo_send.at[number],
                recv_sem=halo_recv.at[number],
                device_id={"ctx": peer},
                device_id_type=MESH,
            )
            pl.when(there)(copy.start)
            halos.append((copy, there))
            pairs.append((copy, back))
        return pairs

    halos = []

    def arrived(pairs):
        for copy, there in pairs:
            pl.when(there)(copy.wait_recv)

    @pl.when(me == 0)
    def _():
        for ref in (kpad, vpad, qpad, dopad):
            ref[below, :] = jnp.zeros((HALF, width), BF16)

    @pl.when(me == n - 1)
    def _():
        for ref in (kpad, vpad, qpad, dopad):
            ref[above, :] = jnp.zeros((HALF, width), BF16)

    near_halos = exchange(kpad) + exchange(vpad)

    for part in range(window // 512):
        reach = me * tok - HALF + part * 512 + iota((1, 512), 1)
        bias = jnp.min(jnp.where(pos_c == reach, NEG, 0.0), axis=0, keepdims=True)
        inside = (reach >= 0) & (reach < seq)
        colbias[:, pl.ds(part * 512, 512)] = jnp.where(inside, bias, NEG)
    row_pos = me * tok + iota((tok, 1), 0)
    flag = jnp.max(jnp.where(row_pos == pos_r, 1.0, 0.0), axis=1, keepdims=True)
    rowflag[...] = jnp.broadcast_to(flag, (tok, width))
    lgrad[...] = jnp.where(rowflag[...] > 0.5, 0.0, dopad[own, :].astype(F32)).astype(BF16)

    for copy in from_x:
        copy.wait_recv()
    over = gx[0, 1].astype(F32)
    gath[0, 0, 0] = gx[0, 0]
    for d in range(1, xn):
        gath[0, 0, d] = gx[d, 0]
        over = over + gx[d, 1].astype(F32)
    gath[0, 0, xn] = over.astype(BF16)
    from_y = {e: send(gath.at[0, 0], gath.at[0, e], y_peers[e - 1]) for e in y_order}
    from_sib = [send(gath.at[0, 0], gath.at[1, 0], sibling)]

    core_c, xo_c, yo_c = owner_c & 1, (owner_c >> 1) & (xn - 1), owner_c >> (1 + x_shift)
    half_total = yn * (xn + 1) * ROWS
    from_row = (yy - yo_c) & (yn - 1)
    src_c = (core_c ^ core) * half_total + jnp.where(
        rank_c < SLOTS,
        (from_row * (xn + 1) + ((xx - xo_c) & (xn - 1))) * ROWS + rank_c,
        (from_row * (xn + 1) + xn) * ROWS + rank_c - SLOTS,
    )
    for half in range(2):
        tile_row = iota((count, half_total), 1) + half * half_total
        for a in range(4):
            pick[half, a] = one_hot(tile_row == src_c + SLOTS * a)

    core_r, xo_r, yo_r = owner_r & 1, (owner_r >> 1) & (xn - 1), owner_r >> (1 + x_shift)
    place = ((core_r ^ core) * xn + ((xo_r - xx) & (xn - 1))) * yn + ((yo_r - yy) & (yn - 1))
    beyond = 2 * xn * yn * SLOTS
    key_r = jnp.where(rank_r < SLOTS, place * SLOTS + rank_r, beyond + rank_r - SLOTS)
    spread[0] = one_hot(iota((beyond, count), 0) == key_r)
    turned = ((core_r ^ core) * yn + ((yo_r - yy) & (yn - 1))) * xn + ((xo_r - xx) & (xn - 1))
    turned_r = jnp.where(rank_r < SLOTS, turned * SLOTS + rank_r, beyond + rank_r - SLOTS)
    spread[1] = one_hot(iota((beyond, count), 0) == turned_r)
    spread_over[...] = jnp.where(beyond + (iota((ROWS, count), 0) & 3) == key_r, 1.0, 0.0)

    rho_lane = iota((count, TILE), 1)
    lane_rank = ((rho_lane >> 4) << 2) + (rho_lane & 3)
    chosen_c = (owner_c == me) & (rank_c == lane_rank) & (rho_lane < 2 * ROWS)
    slot_row = jnp.sum(jnp.where(chosen_c, (local_c + 1).astype(F32), 0.0), axis=0, keepdims=True).astype(I32) - 1
    hot_scr[...] = one_hot(iota((tok, TILE), 0) == slot_row)
    keep(hot_scr, hot_out)
    keep(rowflag, flag_out)

    arrived(near_halos)

    lane = iota((TILE, TILE), 1)
    sub = iota((TILE, TILE), 0)
    low_bias = jnp.where(lane >= sub, 0.0, NEG)
    high_bias = jnp.where(lane <= sub, 0.0, NEG)

    def before(t, carry):
        start = pl.multiple_of(t * TILE, TILE)
        rows, keys = pl.ds(start, TILE), pl.ds(start, span)
        s = dot_nt(qpad[pl.ds(HALF + start, TILE), :], kpad[keys, :]) * scale + colbias[:, keys]
        s = jnp.concatenate(
            [s[:, :TILE] + low_bias, s[:, TILE : 2 * HALF], s[:, 2 * HALF :] + high_bias], axis=1
        )
        top = jnp.max(s, axis=1, keepdims=True)
        p = jnp.exp(s - top)
        p_scr[rows, :] = p
        ow_scr[rows, :] = dot_nn(p.astype(BF16), vpad[keys, :])
        m_scr[rows, :] = jnp.broadcast_to(top, (TILE, width))
        l_scr[rows, :] = jnp.broadcast_to(jnp.sum(p, axis=1, keepdims=True), (TILE, width))
        d_scr[rows, :] = dot_nt(lgrad[rows, :], vpad[keys, :])
        return carry

    lax.fori_loop(0, tiles, before, 0)

    for e in reversed(y_order):
        from_y[e].wait_recv()
        from_sib.append(send(gath.at[0, e], gath.at[1, e], sibling))
    half_tiles = gath[0].reshape(half_total, width)
    for a in range(4):
        glob_part[a] = dot_nn(pick[0, a], half_tiles)
    for copy in from_sib:
        copy.wait_recv()
    half_tiles = gath[1].reshape(half_total, width)
    for a in range(4):
        glob[a] = (glob_part[a] + dot_nn(pick[1, a], half_tiles)).astype(BF16)

    middle = (jnp.sum(glob[2].astype(F32), axis=0, keepdims=True) * (1.0 / count)).astype(BF16)
    centre = dot_nt(jnp.broadcast_to(middle, (ROWS, width)), glob[3])[0:1, :]
    sg = dot_nt(kpad[own, :], glob[0]) * scale
    gw = dot_nt(vpad[own, :], glob[3]) - centre
    sg_scr[...] = sg
    gw_scr[...] = gw
    top = jnp.max(sg, axis=0, keepdims=True)
    p = jnp.exp(sg - top)
    stat_rows = [top, jnp.sum(p, axis=0, keepdims=True), jnp.sum(p * gw, axis=0, keepdims=True)]
    for r, row in enumerate(stat_rows):
        st_own[2 * r : 2 * r + 1, :] = row[:, :TILE]
        st_own[2 * r + 1 : 2 * r + 2, :] = row[:, TILE:]
    st_own[6:8, :] = jnp.zeros((2, TILE), F32)

    def join(parts):
        joined = functools.reduce(jnp.maximum, [part[0:2, :] for part in parts])
        weigh = [jnp.exp(part[0:2, :] - joined) for part in parts]
        return (
            joined,
            sum(part[2:4, :] * w for part, w in zip(parts, weigh)),
            sum(part[4:6, :] * w for part, w in zip(parts, weigh)),
        )

    def store(ref, stats):
        for r, part in enumerate(stats):
            ref[2 * r : 2 * r + 2, :] = part
        ref[6:8, :] = jnp.zeros((2, TILE), F32)

    def row_of(part):
        return jnp.concatenate([part[0:1], part[1:2]], axis=1)

    stat_sib = send(st_own, st_sib, sibling)
    far_halos = exchange(qpad) + exchange(dopad)

    lg = lgrad[...]
    s = dot_nt(qpad[own, :], glob[1]) * scale
    top_w = m_scr[:, 0:1]
    top = jnp.maximum(top_w, jnp.max(s, axis=1, keepdims=True))
    pg = jnp.exp(s - top)
    down = jnp.exp(top_w - top)
    all_sum = l_scr[:, 0:1] * down + jnp.sum(pg, axis=1, keepdims=True)
    inv = 1.0 / all_sum
    pg = pg * inv
    pg16 = pg.astype(BF16)
    o = ow_scr[...] * (down * inv) + dot_nn(pg16, glob[2])
    o_scr[...] = o
    row_dot = jnp.sum(lg.astype(F32) * o, axis=1, keepdims=True)
    dsg = (pg * (dot_nt(lg, glob[2]) - row_dot)).astype(BF16)
    m_scr[...] = jnp.broadcast_to(down * inv, (tok, width))
    l_scr[...] = jnp.broadcast_to(row_dot, (tok, width))
    dkg = dot_tn(dsg, qpad[own, :])
    dvg = dot_tn(pg16, lg)
    dq_scr[...] = dot_nn(dsg, glob[1])

    row_lse = jnp.where(rowflag[:, 0:1] > 0.5, -NEG, top + jnp.log(all_sum))
    for t in range(tiles):
        for r, column in enumerate((row_lse, row_dot)):
            mine = column[t * TILE : (t + 1) * TILE]
            near_out[r * tiles + t : r * tiles + t + 1, :] = jnp.sum(
                jnp.where(lane == sub, mine, 0.0), axis=0, keepdims=True
            )
    near = [send(near_out, near_in.at[0], right), send(near_out, near_in.at[1], left)]

    def after():
        dk = jnp.zeros((tok, width), F32)
        dv = jnp.zeros((tok, width), F32)
        for t in range(tiles):
            start = t * TILE
            rows, keys = pl.ds(start, TILE), pl.ds(start, span)
            pw = p_scr[rows, :] * m_scr[rows, 0:1]
            dsw = (pw * (d_scr[rows, :] - l_scr[rows, 0:1])).astype(BF16)
            dq_scr[rows, :] = (dq_scr[rows, :] + dot_nn(dsw, kpad[keys, :])) * scale
            first_own = HALF - start
            dk = dk + dot_tn(dsw[:, first_own : first_own + tok], qpad[pl.ds(HALF + start, TILE), :])
            dv = dv + dot_tn(pw[:, first_own : first_own + tok].astype(BF16), lgrad[rows, :])
        dkown[...] = dk
        dvown[...] = dv

    def from_neighbour(side):
        rows = pl.ds(side * (HALF + tok), HALF)
        key_at, query_at = iota((tok, HALF), 0), iota((tok, HALF), 1)
        within = key_at <= query_at if side == 0 else key_at >= query_at
        there = me > 0 if side == 0 else me < n - 1
        outside = jnp.where(there, 0.0, -NEG)
        lse_n = jnp.concatenate([near_in[side, t : t + 1, :] for t in range(tiles)], axis=1)
        dot_n = jnp.concatenate([near_in[side, tiles + t : tiles + t + 1, :] for t in range(tiles)], axis=1)
        s = dot_nt(kpad[own, :], qpad[rows, :]) * scale
        s = jnp.where(within, s, NEG) + jnp.where(rowflag[:, 0:1] > 0.5, NEG, 0.0)
        p = jnp.exp(s - (lse_n + outside))
        ds = (p * (dot_nt(vpad[own, :], dopad[rows, :]) - dot_n)).astype(BF16)
        dkown[...] += dot_nn(ds, qpad[rows, :])
        dvown[...] += dot_nn(p.astype(BF16), dopad[rows, :])

    over_row = iota((ROWS, count), 0)

    def overflow(partial, arrays):
        z_over = jnp.zeros((ROWS, width), F32)
        for a in range(arrays):
            mine = jnp.where((over_row >> 2) == a, spread_over[...], 0.0).astype(BF16)
            z_over = z_over + dot_nn(mine, partial[:, a * width : (a + 1) * width])
        return z_over.astype(BF16)

    def paired(own_ref, sib_ref, order, arrays, ref, land, peers):
        groups = len(order) + 1
        over = (own_ref[0, arrays * groups].astype(F32) + sib_ref[arrays * groups].astype(F32)).astype(BF16)
        sent = []
        for d in order + [0]:
            tiles_of = pl.ds(d * arrays, arrays)
            ref[d, 0:arrays] = (own_ref[0, tiles_of].astype(F32) + sib_ref[tiles_of].astype(F32)).astype(BF16)
            ref[d, arrays] = over
            if d > 0:
                sent.append(send(ref.at[d], land.at[d - 1], peers[d - 1]))
        return sent

    deep = xn * SLOTS // ROWS
    partial = jnp.concatenate([dkg, dvg], axis=1).astype(BF16)
    z = dot_nn(spread[1], partial).astype(BF16)
    z_over = overflow(partial, 2)
    for half in range(2):
        for e in range(yn):
            base = (half * yn + e) * deep * ROWS
            for a in range(2):
                mine = z[base : base + deep * ROWS, a * width : (a + 1) * width]
                z2_own[half, (e * 2 + a) * deep : (e * 2 + a + 1) * deep] = mine.reshape(deep, ROWS, width)
        z2_own[half, 2 * deep * yn] = z_over
    z2_copy = send(z2_own.at[1], z2_sib, sibling)

    stat_sib.wait_recv()
    store(st_x, join([st_own[...], st_sib[...]]))
    stat_x = [send(st_x, st_xin.at[d - 1], x_peers[d - 1]) for d in x_order]

    pair_top = st_x[0:2, :]
    w = jnp.exp(sg_scr[...] - row_of(pair_top))
    w16 = w.astype(BF16)
    ds16 = (w * gw_scr[...]).astype(BF16)
    value_key = dot_tn(w16, jnp.concatenate([vpad[own, :], kpad[own, :]], axis=1))
    partial = [value_key[:, :width], dot_tn(ds16, kpad[own, :]), value_key[:, width:]]
    partial = jnp.concatenate(partial, axis=1).astype(BF16)
    z = dot_nn(spread[0], partial).astype(BF16)
    z_over = overflow(partial, 3)
    for half in range(2):
        for d in range(xn):
            base = (half * xn + d) * ROWS
            for a in range(3):
                z1_own[half, d * 3 + a] = z[base : base + ROWS, a * width : (a + 1) * width]
        z1_own[half, 3 * xn] = z_over
    z1_copy = send(z1_own.at[1], z1_sib, sibling)

    z2_copy.wait_recv()
    t2_copies = paired(z2_own, z2_sib, y_order, 2 * deep, t2_own, t2_in, y_peers)
    keep(o_scr, o_out)
    z1_copy.wait_recv()
    t1_copies = paired(z1_own, z1_sib, x_order, 3, t1_own, t1_in, x_peers)

    after()
    keep(dq_scr, dq_out)

    for copy in stat_x:
        copy.wait_recv()
    store(st_y, join([st_x[...]] + [st_xin[d - 1] for d in range(1, xn)]))
    stat_y = [send(st_y, st_yin.at[e - 1], y_peers[e - 1]) for e in y_order]

    def arrange(groups, depth, wanted, overflow_at, places):
        goal, source = iota((groups * ROWS, places), 0), iota((groups * ROWS, places), 1)
        goal_to, goal_array, goal_slot = goal >> 4, (goal >> 2) & 1, goal & 3
        hit = jnp.zeros(goal.shape, F32)
        for array, tile in wanted:
            at = jnp.where(
                (goal & 15) >= 8,
                overflow_at + tile * SLOTS + goal_slot,
                tile * depth * ROWS + goal_to * SLOTS + goal_slot,
            )
            hit = hit + jnp.where((goal_array == array) & (source == at), 1.0, 0.0)
        return hit.astype(BF16)

    arrange_1 = arrange(yn, 1, ((0, 0), (1, 1), (1, 2)), 3 * ROWS, 4 * ROWS)
    arrange_2 = arrange(xn, deep, ((0, 0), (1, 1)), 2 * deep * ROWS, (2 * deep + 1) * ROWS)

    for copy in t2_copies:
        copy.wait_recv()
    column = t2_own[0].astype(F32)
    for e in range(1, yn):
        column = column + t2_in[e - 1].astype(F32)
    v = dot_nn(arrange_2, column.reshape((2 * deep + 1) * ROWS, width).astype(BF16)).astype(BF16)
    v_own[...] = v.reshape(xn, ROWS, width)
    v_copies = [send(v_own.at[d], v_in.at[d - 1], x_peers[d - 1]) for d in x_order]

    arrived(far_halos)
    for copy in near:
        copy.wait_recv()
    from_neighbour(0)
    from_neighbour(1)

    for copy in stat_y:
        copy.wait_recv()
    joined, summed, dotted = join([st_y[...]] + [st_yin[e - 1] for e in range(1, yn)])
    lse = row_of(joined + jnp.log(summed))
    ratio = row_of(dotted / summed)
    line = iota((4 * ROWS, count), 0)
    line_key = jnp.where(line < 3 * ROWS, line & (ROWS - 1), beyond + (line & 3))
    kind = jnp.where(line < 3 * ROWS, line >> 4, (line >> 2) & 3)
    found = jnp.where(line_key == key_r, 1.0, 0.0)
    found = found * jnp.where(kind == 2, -ratio, jnp.where(kind == 3, 0.0, 1.0))
    column = jnp.zeros((4 * ROWS, width), F32)
    for d in range(xn):
        pair = st_x[0:2, :] if d == 0 else st_xin[d - 1, 0:2, :]
        fall = row_of(jnp.exp(pair - joined) / summed)
        factor = jnp.sum(found * fall, axis=1, keepdims=True)
        f_scr[d] = jnp.broadcast_to(factor, (4 * ROWS, width))

    for copy in t1_copies:
        copy.wait_recv()
    for d in range(xn):
        mine = t1_own[0] if d == 0 else t1_in[d - 1]
        column = column + mine.astype(F32).reshape(4 * ROWS, width) * f_scr[d]
    upper = column.astype(BF16)
    lower = (column - upper.astype(F32)).astype(BF16)
    u = (dot_nn(arrange_1, upper) + dot_nn(arrange_1, lower)).astype(BF16)
    u_own[...] = u.reshape(yn, ROWS, width)
    u_copies = [send(u_own.at[e], u_in.at[e - 1], y_peers[e - 1]) for e in y_order]

    w = jnp.exp(sg_scr[...] - lse)
    dvown[...] += dot_nn(w.astype(BF16), glob[3])
    dkown[...] = (dkown[...] + dot_nn((w * (gw_scr[...] - ratio)).astype(BF16), glob[0])) * scale
    keep(dkown, dk_out)
    keep(dvown, dv_out)

    for copy in v_copies:
        copy.wait_recv()
    late = v_own[0].astype(F32)
    for d in range(1, xn):
        late = late + v_in[d - 1].astype(F32)
    for copy in u_copies:
        copy.wait_recv()
    early = u_own[0].astype(F32)
    for e in range(1, yn):
        early = early + u_in[e - 1].astype(F32)
    for part in range(2):
        r_scr[part * ROWS : part * ROWS + 8, :] = early[part * 8 : part * 8 + 8]
        r_scr[part * ROWS + 8 : part * ROWS + 16, :] = late[part * 8 : part * 8 + 8]
    keep(r_scr, r_out)

    for copy in stores:
        copy.wait()
    for copy in copies:
        copy.wait_send()
    for copy, there in halos:
        pl.when(there)(copy.wait_send)


def finish(scale, o_ref, dq_in, dk_in, dv_in, hot_ref, flag_ref, r_ref, out_ref, dq_ref, dk_ref, dv_ref, total):
    tok = o_ref.shape[0]
    total[...] = jnp.zeros_like(total)
    total[0 : 2 * ROWS, :] = r_ref[...]
    upper = total[...].astype(BF16)
    lower = (total[...] - upper.astype(F32)).astype(BF16)
    hot = hot_ref[...].astype(F32)
    lane_array = (iota((tok, TILE), 1) >> 2) & 3

    def placed(a):
        mine = jnp.where(lane_array == a, hot, 0.0).astype(BF16)
        return dot_nn(mine, upper) + dot_nn(mine, lower)

    out_ref[...] = jnp.where(flag_ref[...] > 0.5, placed(0), o_ref[...]).astype(BF16)
    dq_ref[...] = dq_in[...] + placed(1) * scale
    dk_ref[...] = dk_in[...] + placed(2) * scale
    dv_ref[...] = dv_in[...] + placed(3)


def shards(n, query_rows, key_rows, value_rows, out_grad, global_pos):
    tok, _, width = query_rows.shape
    count = global_pos.shape[0]
    yn = 4
    xn = n // (2 * yn)
    deep = xn * SLOTS // ROWS
    window = tok + 2 * HALF
    span = TILE + 2 * HALF
    copies = 4 * (xn - 1) + 4 * (yn - 1) + 20
    vmem = pl.BlockSpec(memory_space=pltpu.VMEM)
    anywhere = pl.BlockSpec(memory_space=pl.ANY)
    flat = [x.reshape(tok, width) for x in (query_rows, key_rows, value_rows, out_grad)]
    rows_f32 = jax.ShapeDtypeStruct((tok, width), F32)
    middle = pl.pallas_call(
        functools.partial(kernel, (n, yn, xn, tok, count, width)),
        name="sparse_attention",
        out_shape=(rows_f32,) * 4
        + (
            jax.ShapeDtypeStruct((tok, TILE), BF16),
            rows_f32,
            jax.ShapeDtypeStruct((2 * ROWS, width), F32),
        ),
        in_specs=[pl.BlockSpec(memory_space=pltpu.HBM)] * 5,
        out_specs=(anywhere,) * 7,
        scratch_shapes=[
            pltpu.VMEM((1, count), I32),
            pltpu.VMEM((window, width), BF16),
            pltpu.VMEM((window, width), BF16),
            pltpu.VMEM((window, width), BF16),
            pltpu.VMEM((window, width), BF16),
            pltpu.VMEM((tok, width), BF16),
            pltpu.VMEM((1, window), F32),
            pltpu.VMEM((tok, width), F32),
            pltpu.VMEM((2, ROWS, width), BF16),
            pltpu.VMEM((xn, 2, ROWS, width), BF16),
            pltpu.VMEM((2, yn, xn + 1, ROWS, width), BF16),
            pltpu.VMEM((2, 4, count, yn * (xn + 1) * ROWS), BF16),
            pltpu.VMEM((4, count, width), F32),
            pltpu.VMEM((4, count, width), BF16),
            pltpu.VMEM((tok, span), F32),
            pltpu.VMEM((tok, width), F32),
            pltpu.VMEM((tok, span), F32),
            pltpu.VMEM((tok, width), F32),
            pltpu.VMEM((tok, width), F32),
            pltpu.VMEM((tok, width), F32),
            pltpu.VMEM((tok, width), F32),
            pltpu.VMEM((tok, count), F32),
            pltpu.VMEM((tok, count), F32),
            pltpu.VMEM((8, TILE), F32),
            pltpu.VMEM((8, TILE), F32),
            pltpu.VMEM((8, TILE), F32),
            pltpu.VMEM((xn - 1, 8, TILE), F32),
            pltpu.VMEM((8, TILE), F32),
            pltpu.VMEM((yn - 1, 8, TILE), F32),
            pltpu.VMEM((tok, width), F32),
            pltpu.VMEM((tok, width), F32),
            pltpu.VMEM((2, 2 * xn * yn * SLOTS, count), BF16),
            pltpu.VMEM((ROWS, count), F32),
            pltpu.VMEM((tok, TILE), BF16),
            pltpu.VMEM((2, 3 * xn + 1, ROWS, width), BF16),
            pltpu.VMEM((3 * xn + 1, ROWS, width), BF16),
            pltpu.VMEM((xn, 4, ROWS, width), BF16),
            pltpu.VMEM((xn - 1, 4, ROWS, width), BF16),
            pltpu.VMEM((2, 2 * deep * yn + 1, ROWS, width), BF16),
            pltpu.VMEM((2 * deep * yn + 1, ROWS, width), BF16),
            pltpu.VMEM((yn, 2 * deep + 1, ROWS, width), BF16),
            pltpu.VMEM((yn - 1, 2 * deep + 1, ROWS, width), BF16),
            pltpu.VMEM((xn, 4 * ROWS, width), F32),
            pltpu.VMEM((yn, ROWS, width), BF16),
            pltpu.VMEM((yn - 1, ROWS, width), BF16),
            pltpu.VMEM((xn, ROWS, width), BF16),
            pltpu.VMEM((xn - 1, ROWS, width), BF16),
            pltpu.VMEM((2 * ROWS, width), F32),
            pltpu.VMEM((8, TILE), F32),
            pltpu.VMEM((2, 8, TILE), F32),
            pltpu.SemaphoreType.DMA((copies,)),
            pltpu.SemaphoreType.DMA((copies,)),
            pltpu.SemaphoreType.DMA((8,)),
            pltpu.SemaphoreType.DMA((8,)),
            pltpu.SemaphoreType.DMA((5,)),
            pltpu.SemaphoreType.DMA((7,)),
        ],
        compiler_params=pltpu.CompilerParams(
            collective_id=0, has_side_effects=True, vmem_limit_bytes=24 << 20
        ),
    )(*[pltpu.with_memory_space_constraint(x, pltpu.HBM) for x in (global_pos.reshape(1, count), *flat)])
    results = pl.pallas_call(
        functools.partial(finish, width**-0.5),
        name="place_global_rows",
        out_shape=(jax.ShapeDtypeStruct((tok, width), BF16),) + (rows_f32,) * 3,
        in_specs=[vmem] * 7,
        out_specs=(vmem,) * 4,
        scratch_shapes=[pltpu.VMEM((TILE, width), F32)],
        compiler_params=pltpu.CompilerParams(vmem_limit_bytes=8 << 20),
    )(*middle)
    return tuple(x.reshape(tok, 1, width) for x in results)


def solution(mesh):
    rows = P("ctx", "head", None)
    return jax.shard_map(
        functools.partial(shards, mesh.shape["ctx"]),
        mesh=mesh,
        in_specs=(rows,) * 4 + (P(),),
        out_specs=(rows,) * 4,
        check_vma=False,
    )
```

```python
import functools

import jax
import jax.numpy as jnp
from jax import lax
from jax.experimental import pallas as pl
from jax.experimental.pallas import tpu as pltpu
from jax.sharding import PartitionSpec as P

MESH = pl.DeviceIdType.MESH
HALF = 512
TILE = 128
SLOTS = 4
ROWS = 16
NEG = -1e30
F32 = jnp.float32
BF16 = jnp.bfloat16
I32 = jnp.int32


def dot_nn(a, b):
    return lax.dot_general(a, b, (((1,), (0,)), ((), ())), preferred_element_type=F32)


def dot_nt(a, b):
    return lax.dot_general(a, b, (((1,), (1,)), ((), ())), preferred_element_type=F32)


def dot_tn(a, b):
    return lax.dot_general(a, b, (((0,), (0,)), ((), ())), preferred_element_type=F32)


def iota(shape, dim):
    return lax.broadcasted_iota(I32, shape, dim)


def one_hot(cond):
    return jnp.where(cond, 1.0, 0.0).astype(BF16)


def kernel(
    sizes,
    pos_hbm,
    q_hbm,
    k_hbm,
    v_hbm,
    do_hbm,
    o_out,
    dq_out,
    dk_out,
    dv_out,
    hot_out,
    flag_out,
    r_out,
    pos_scr,
    qpad,
    dopad,
    kpad,
    vpad,
    lgrad,
    colbias,
    rowflag,
    pack,
    gx,
    gath,
    pick,
    glob_part,
    glob,
    p_scr,
    ow_scr,
    d_scr,
    m_scr,
    l_scr,
    o_scr,
    dq_scr,
    sg_scr,
    gw_scr,
    st_own,
    st_sib,
    st_x,
    st_xin,
    st_y,
    st_yin,
    dkown,
    dvown,
    spread,
    spread_over,
    hot_scr,
    z1_own,
    z1_sib,
    t1_own,
    t1_in,
    z2_own,
    z2_sib,
    t2_own,
    t2_in,
    f_scr,
    u_own,
    u_in,
    v_own,
    v_in,
    r_scr,
    near_out,
    near_in,
    send_sem,
    recv_sem,
    halo_send,
    halo_recv,
    load_sem,
    store_sem,
):
    n, yn, xn, tok, count, width = sizes
    seq = n * tok
    scale = width**-0.5
    x_shift = xn.bit_length() - 1
    tok_shift = tok.bit_length() - 1
    window = tok + 2 * HALF
    span = TILE + 2 * HALF
    tiles = tok // TILE
    own = pl.ds(HALF, tok)

    me = lax.axis_index("ctx")
    core = lax.rem(me, 2)
    xx = lax.rem(lax.div(me, 2), xn)
    yy = lax.div(me, 2 * xn)

    def ctx_id(y, x, c):
        return (y * xn + x) * 2 + c

    x_peers = [ctx_id(yy, lax.rem(xx + d, xn), core) for d in range(1, xn)]
    y_peers = [ctx_id(lax.rem(yy + e, yn), xx, core) for e in range(1, yn)]
    sibling = me + 1 - 2 * core
    right = lax.rem(me + 1, n)
    left = lax.rem(me + n - 1, n)
    x_order = sorted(range(1, xn), key=lambda d: -min(d, xn - d))
    y_order = sorted(range(1, yn), key=lambda e: -min(e, yn - e))
    greeted = [x_peers[d - 1] for d in x_order] + [y_peers[e - 1] for e in y_order] + [left, right]

    barrier = pltpu.get_barrier_semaphore()
    for peer in greeted:
        pl.semaphore_signal(barrier, inc=1, device_id={"ctx": peer}, device_id_type=MESH)

    loads = [
        pltpu.make_async_copy(src, dst, load_sem.at[i])
        for i, (src, dst) in enumerate(
            (
                (pos_hbm, pos_scr),
                (q_hbm, qpad.at[own]),
                (k_hbm, kpad.at[own]),
                (v_hbm, vpad.at[own]),
                (do_hbm, dopad.at[own]),
            )
        )
    ]
    for load in loads:
        load.start()

    copies = []

    def send(src, dst, peer):
        number = len(copies)
        copy = pltpu.make_async_remote_copy(
            src_ref=src,
            dst_ref=dst,
            send_sem=send_sem.at[number],
            recv_sem=recv_sem.at[number],
            device_id={"ctx": peer},
            device_id_type=MESH,
        )
        copy.start()
        copies.append(copy)
        return copy

    stores = []

    def keep(src, dst):
        copy = pltpu.make_async_copy(src, dst, store_sem.at[len(stores)])
        copy.start()
        stores.append(copy)

    loads[0].wait()
    pos_r = pos_scr[...]
    first, second = iota((count, count), 0), iota((count, count), 1)
    pos_c = jnp.sum(jnp.where(first == second, pos_r.astype(F32), 0.0), axis=1, keepdims=True).astype(I32)
    owner_c, owner_r = pos_c >> tok_shift, pos_r >> tok_shift
    local_c, local_r = pos_c & (tok - 1), pos_r & (tok - 1)
    same = owner_c == owner_r
    rank_c = jnp.sum(jnp.where(same & (second < first), 1.0, 0.0), axis=1, keepdims=True).astype(I32)
    rank_r = jnp.sum(jnp.where(same & (first < second), 1.0, 0.0), axis=0, keepdims=True).astype(I32)

    rho = iota((2 * ROWS, count), 0)
    slot_rank = ((rho >> 4) << 2) + (rho & 3)
    chosen = (owner_r == me) & (rank_r == slot_rank)
    slot_col = jnp.sum(jnp.where(chosen, (local_r + 1).astype(F32), 0.0), axis=1, keepdims=True).astype(I32) - 1
    array_of = (iota((2 * ROWS, tok), 0) >> 2) & 3
    at_slot = iota((2 * ROWS, tok), 1) == slot_col
    picked = jnp.zeros((2 * ROWS, width), F32)
    for load in loads[1:]:
        load.wait()
    for a, rows in enumerate((qpad[own, :], kpad[own, :], vpad[own, :], dopad[own, :])):
        picked = picked + dot_nn(one_hot(at_slot & (array_of == a)), rows)
    pack[...] = picked.astype(BF16).reshape(2, ROWS, width)
    gx[0] = pack[...]

    pl.semaphore_wait(barrier, len(greeted))

    from_x = [send(pack, gx.at[d], x_peers[d - 1]) for d in x_order]
    to_right, to_left = me < n - 1, me > 0
    below, above = pl.ds(0, HALF), pl.ds(HALF + tok, HALF)

    def exchange(ref):
        pairs = []
        for peer, there, back, dst in ((right, to_right, to_left, below), (left, to_left, to_right, above)):
            number = len(halos)
            copy = pltpu.make_async_remote_copy(
                src_ref=ref.at[own],
                dst_ref=ref.at[dst],
                send_sem=halo_send.at[number],
                recv_sem=halo_recv.at[number],
                device_id={"ctx": peer},
                device_id_type=MESH,
            )
            pl.when(there)(copy.start)
            halos.append((copy, there))
            pairs.append((copy, back))
        return pairs

    halos = []

    def arrived(pairs):
        for copy, there in pairs:
            pl.when(there)(copy.wait_recv)

    @pl.when(me == 0)
    def _():
        for ref in (kpad, vpad, qpad, dopad):
            ref[below, :] = jnp.zeros((HALF, width), BF16)

    @pl.when(me == n - 1)
    def _():
        for ref in (kpad, vpad, qpad, dopad):
            ref[above, :] = jnp.zeros((HALF, width), BF16)

    near_halos = exchange(kpad) + exchange(vpad)

    for part in range(window // 512):
        reach = me * tok - HALF + part * 512 + iota((1, 512), 1)
        bias = jnp.min(jnp.where(pos_c == reach, NEG, 0.0), axis=0, keepdims=True)
        inside = (reach >= 0) & (reach < seq)
        colbias[:, pl.ds(part * 512, 512)] = jnp.where(inside, bias, NEG)
    row_pos = me * tok + iota((tok, 1), 0)
    flag = jnp.max(jnp.where(row_pos == pos_r, 1.0, 0.0), axis=1, keepdims=True)
    rowflag[...] = jnp.broadcast_to(flag, (tok, width))
    lgrad[...] = jnp.where(rowflag[...] > 0.5, 0.0, dopad[own, :].astype(F32)).astype(BF16)

    for copy in from_x:
        copy.wait_recv()
    over = gx[0, 1].astype(F32)
    gath[0, 0, 0] = gx[0, 0]
    for d in range(1, xn):
        gath[0, 0, d] = gx[d, 0]
        over = over + gx[d, 1].astype(F32)
    gath[0, 0, xn] = over.astype(BF16)
    from_y = {e: send(gath.at[0, 0], gath.at[0, e], y_peers[e - 1]) for e in y_order}
    from_sib = [send(gath.at[0, 0], gath.at[1, 0], sibling)]

    core_c, xo_c, yo_c = owner_c & 1, (owner_c >> 1) & (xn - 1), owner_c >> (1 + x_shift)
    half_total = yn * (xn + 1) * ROWS
    from_row = (yy - yo_c) & (yn - 1)
    src_c = (core_c ^ core) * half_total + jnp.where(
        rank_c < SLOTS,
        (from_row * (xn + 1) + ((xx - xo_c) & (xn - 1))) * ROWS + rank_c,
        (from_row * (xn + 1) + xn) * ROWS + rank_c - SLOTS,
    )
    for half in range(2):
        tile_row = iota((count, half_total), 1) + half * half_total
        for a in range(4):
            pick[half, a] = one_hot(tile_row == src_c + SLOTS * a)

    core_r, xo_r, yo_r = owner_r & 1, (owner_r >> 1) & (xn - 1), owner_r >> (1 + x_shift)
    place = ((core_r ^ core) * xn + ((xo_r - xx) & (xn - 1))) * yn + ((yo_r - yy) & (yn - 1))
    beyond = 2 * xn * yn * SLOTS
    key_r = jnp.where(rank_r < SLOTS, place * SLOTS + rank_r, beyond + rank_r - SLOTS)
    spread[0] = one_hot(iota((beyond, count), 0) == key_r)
    turned = ((core_r ^ core) * yn + ((yo_r - yy) & (yn - 1))) * xn + ((xo_r - xx) & (xn - 1))
    turned_r = jnp.where(rank_r < SLOTS, turned * SLOTS + rank_r, beyond + rank_r - SLOTS)
    spread[1] = one_hot(iota((beyond, count), 0) == turned_r)
    spread_over[...] = jnp.where(beyond + (iota((ROWS, count), 0) & 3) == key_r, 1.0, 0.0)

    rho_lane = iota((count, TILE), 1)
    lane_rank = ((rho_lane >> 4) << 2) + (rho_lane & 3)
    chosen_c = (owner_c == me) & (rank_c == lane_rank) & (rho_lane < 2 * ROWS)
    slot_row = jnp.sum(jnp.where(chosen_c, (local_c + 1).astype(F32), 0.0), axis=0, keepdims=True).astype(I32) - 1
    hot_scr[...] = one_hot(iota((tok, TILE), 0) == slot_row)
    keep(hot_scr, hot_out)
    keep(rowflag, flag_out)

    arrived(near_halos)

    lane = iota((TILE, TILE), 1)
    sub = iota((TILE, TILE), 0)
    low_bias = jnp.where(lane >= sub, 0.0, NEG)
    high_bias = jnp.where(lane <= sub, 0.0, NEG)

    def before(t, carry):
        start = pl.multiple_of(t * TILE, TILE)
        rows, keys = pl.ds(start, TILE), pl.ds(start, span)
        s = dot_nt(qpad[pl.ds(HALF + start, TILE), :], kpad[keys, :]) * scale + colbias[:, keys]
        s = jnp.concatenate(
            [s[:, :TILE] + low_bias, s[:, TILE : 2 * HALF], s[:, 2 * HALF :] + high_bias], axis=1
        )
        top = jnp.max(s, axis=1, keepdims=True)
        p = jnp.exp(s - top)
        p_scr[rows, :] = p
        ow_scr[rows, :] = dot_nn(p.astype(BF16), vpad[keys, :])
        m_scr[rows, :] = jnp.broadcast_to(top, (TILE, width))
        l_scr[rows, :] = jnp.broadcast_to(jnp.sum(p, axis=1, keepdims=True), (TILE, width))
        d_scr[rows, :] = dot_nt(lgrad[rows, :], vpad[keys, :])
        return carry

    lax.fori_loop(0, tiles, before, 0)

    for e in reversed(y_order):
        from_y[e].wait_recv()
        from_sib.append(send(gath.at[0, e], gath.at[1, e], sibling))
    far_halos = exchange(qpad) + exchange(dopad)
    half_tiles = gath[0].reshape(half_total, width)
    for a in range(4):
        glob_part[a] = dot_nn(pick[0, a], half_tiles)
    for copy in from_sib:
        copy.wait_recv()
    half_tiles = gath[1].reshape(half_total, width)
    for a in range(4):
        glob[a] = (glob_part[a] + dot_nn(pick[1, a], half_tiles)).astype(BF16)

    middle = (jnp.sum(glob[2].astype(F32), axis=0, keepdims=True) * (1.0 / count)).astype(BF16)
    centre = dot_nt(jnp.broadcast_to(middle, (ROWS, width)), glob[3])[0:1, :]
    sg = dot_nt(kpad[own, :], glob[0]) * scale
    gw = dot_nt(vpad[own, :], glob[3]) - centre
    sg_scr[...] = sg
    gw_scr[...] = gw
    top = jnp.max(sg, axis=0, keepdims=True)
    p = jnp.exp(sg - top)
    stat_rows = [top, jnp.sum(p, axis=0, keepdims=True), jnp.sum(p * gw, axis=0, keepdims=True)]
    for r, row in enumerate(stat_rows):
        st_own[2 * r : 2 * r + 1, :] = row[:, :TILE]
        st_own[2 * r + 1 : 2 * r + 2, :] = row[:, TILE:]
    st_own[6:8, :] = jnp.zeros((2, TILE), F32)

    def join(parts):
        joined = functools.reduce(jnp.maximum, [part[0:2, :] for part in parts])
        weigh = [jnp.exp(part[0:2, :] - joined) for part in parts]
        return (
            joined,
            sum(part[2:4, :] * w for part, w in zip(parts, weigh)),
            sum(part[4:6, :] * w for part, w in zip(parts, weigh)),
        )

    def store(ref, stats):
        for r, part in enumerate(stats):
            ref[2 * r : 2 * r + 2, :] = part
        ref[6:8, :] = jnp.zeros((2, TILE), F32)

    def row_of(part):
        return jnp.concatenate([part[0:1], part[1:2]], axis=1)

    stat_sib = send(st_own, st_sib, sibling)

    lg = lgrad[...]
    s = dot_nt(qpad[own, :], glob[1]) * scale
    top_w = m_scr[:, 0:1]
    top = jnp.maximum(top_w, jnp.max(s, axis=1, keepdims=True))
    pg = jnp.exp(s - top)
    down = jnp.exp(top_w - top)
    all_sum = l_scr[:, 0:1] * down + jnp.sum(pg, axis=1, keepdims=True)
    inv = 1.0 / all_sum
    pg = pg * inv
    pg16 = pg.astype(BF16)
    o = ow_scr[...] * (down * inv) + dot_nn(pg16, glob[2])
    o_scr[...] = o
    row_dot = jnp.sum(lg.astype(F32) * o, axis=1, keepdims=True)
    dsg = (pg * (dot_nt(lg, glob[2]) - row_dot)).astype(BF16)
    m_scr[...] = jnp.broadcast_to(down * inv, (tok, width))
    l_scr[...] = jnp.broadcast_to(row_dot, (tok, width))
    dkg = dot_tn(dsg, qpad[own, :])
    dvg = dot_tn(pg16, lg)
    dq_scr[...] = dot_nn(dsg, glob[1])

    row_lse = jnp.where(rowflag[:, 0:1] > 0.5, -NEG, top + jnp.log(all_sum))
    for t in range(tiles):
        for r, column in enumerate((row_lse, row_dot)):
            mine = column[t * TILE : (t + 1) * TILE]
            near_out[r * tiles + t : r * tiles + t + 1, :] = jnp.sum(
                jnp.where(lane == sub, mine, 0.0), axis=0, keepdims=True
            )
    near = [send(near_out, near_in.at[0], right), send(near_out, near_in.at[1], left)]

    def after():
        dk = jnp.zeros((tok, width), F32)
        dv = jnp.zeros((tok, width), F32)
        for t in range(tiles):
            start = t * TILE
            rows, keys = pl.ds(start, TILE), pl.ds(start, span)
            pw = p_scr[rows, :] * m_scr[rows, 0:1]
            dsw = (pw * (d_scr[rows, :] - l_scr[rows, 0:1])).astype(BF16)
            dq_scr[rows, :] = (dq_scr[rows, :] + dot_nn(dsw, kpad[keys, :])) * scale
            first_own = HALF - start
            dk = dk + dot_tn(dsw[:, first_own : first_own + tok], qpad[pl.ds(HALF + start, TILE), :])
            dv = dv + dot_tn(pw[:, first_own : first_own + tok].astype(BF16), lgrad[rows, :])
        dkown[...] = dk
        dvown[...] = dv

    def from_neighbour(side):
        rows = pl.ds(side * (HALF + tok), HALF)
        key_at, query_at = iota((tok, HALF), 0), iota((tok, HALF), 1)
        within = key_at <= query_at if side == 0 else key_at >= query_at
        there = me > 0 if side == 0 else me < n - 1
        outside = jnp.where(there, 0.0, -NEG)
        lse_n = jnp.concatenate([near_in[side, t : t + 1, :] for t in range(tiles)], axis=1)
        dot_n = jnp.concatenate([near_in[side, tiles + t : tiles + t + 1, :] for t in range(tiles)], axis=1)
        s = dot_nt(kpad[own, :], qpad[rows, :]) * scale
        s = jnp.where(within, s, NEG) + jnp.where(rowflag[:, 0:1] > 0.5, NEG, 0.0)
        p = jnp.exp(s - (lse_n + outside))
        ds = (p * (dot_nt(vpad[own, :], dopad[rows, :]) - dot_n)).astype(BF16)
        dkown[...] += dot_nn(ds, qpad[rows, :])
        dvown[...] += dot_nn(p.astype(BF16), dopad[rows, :])

    over_row = iota((ROWS, count), 0)

    def overflow(partial, arrays):
        z_over = jnp.zeros((ROWS, width), F32)
        for a in range(arrays):
            mine = jnp.where((over_row >> 2) == a, spread_over[...], 0.0).astype(BF16)
            z_over = z_over + dot_nn(mine, partial[:, a * width : (a + 1) * width])
        return z_over.astype(BF16)

    def paired(own_ref, sib_ref, order, arrays, ref, land, peers):
        groups = len(order) + 1
        over = (own_ref[0, arrays * groups].astype(F32) + sib_ref[arrays * groups].astype(F32)).astype(BF16)
        sent = []
        for d in order + [0]:
            tiles_of = pl.ds(d * arrays, arrays)
            ref[d, 0:arrays] = (own_ref[0, tiles_of].astype(F32) + sib_ref[tiles_of].astype(F32)).astype(BF16)
            ref[d, arrays] = over
            if d > 0:
                sent.append(send(ref.at[d], land.at[d - 1], peers[d - 1]))
        return sent

    deep = xn * SLOTS // ROWS
    partial = jnp.concatenate([dkg, dvg], axis=1).astype(BF16)
    z = dot_nn(spread[1], partial).astype(BF16)
    z_over = overflow(partial, 2)
    for half in range(2):
        for e in range(yn):
            base = (half * yn + e) * deep * ROWS
            for a in range(2):
                mine = z[base : base + deep * ROWS, a * width : (a + 1) * width]
                z2_own[half, (e * 2 + a) * deep : (e * 2 + a + 1) * deep] = mine.reshape(deep, ROWS, width)
        z2_own[half, 2 * deep * yn] = z_over
    z2_copy = send(z2_own.at[1], z2_sib, sibling)

    stat_sib.wait_recv()
    store(st_x, join([st_own[...], st_sib[...]]))
    stat_x = [send(st_x, st_xin.at[d - 1], x_peers[d - 1]) for d in x_order]

    pair_top = st_x[0:2, :]
    w = jnp.exp(sg_scr[...] - row_of(pair_top))
    w16 = w.astype(BF16)
    ds16 = (w * gw_scr[...]).astype(BF16)
    value_key = dot_tn(w16, jnp.concatenate([vpad[own, :], kpad[own, :]], axis=1))
    partial = [value_key[:, :width], dot_tn(ds16, kpad[own, :]), value_key[:, width:]]
    partial = jnp.concatenate(partial, axis=1).astype(BF16)
    z = dot_nn(spread[0], partial).astype(BF16)
    z_over = overflow(partial, 3)
    for half in range(2):
        for d in range(xn):
            base = (half * xn + d) * ROWS
            for a in range(3):
                z1_own[half, d * 3 + a] = z[base : base + ROWS, a * width : (a + 1) * width]
        z1_own[half, 3 * xn] = z_over
    z1_copy = send(z1_own.at[1], z1_sib, sibling)

    z2_copy.wait_recv()
    t2_copies = paired(z2_own, z2_sib, y_order, 2 * deep, t2_own, t2_in, y_peers)
    keep(o_scr, o_out)
    z1_copy.wait_recv()
    t1_copies = paired(z1_own, z1_sib, x_order, 3, t1_own, t1_in, x_peers)

    after()
    keep(dq_scr, dq_out)

    for copy in stat_x:
        copy.wait_recv()
    store(st_y, join([st_x[...]] + [st_xin[d - 1] for d in range(1, xn)]))
    stat_y = [send(st_y, st_yin.at[e - 1], y_peers[e - 1]) for e in y_order]

    def arrange(groups, depth, wanted, overflow_at, places):
        goal, source = iota((groups * ROWS, places), 0), iota((groups * ROWS, places), 1)
        goal_to, goal_array, goal_slot = goal >> 4, (goal >> 2) & 1, goal & 3
        hit = jnp.zeros(goal.shape, F32)
        for array, tile in wanted:
            at = jnp.where(
                (goal & 15) >= 8,
                overflow_at + tile * SLOTS + goal_slot,
                tile * depth * ROWS + goal_to * SLOTS + goal_slot,
            )
            hit = hit + jnp.where((goal_array == array) & (source == at), 1.0, 0.0)
        return hit.astype(BF16)

    arrange_1 = arrange(yn, 1, ((0, 0), (1, 1), (1, 2)), 3 * ROWS, 4 * ROWS)
    arrange_2 = arrange(xn, deep, ((0, 0), (1, 1)), 2 * deep * ROWS, (2 * deep + 1) * ROWS)

    for copy in t2_copies:
        copy.wait_recv()
    column = t2_own[0].astype(F32)
    for e in range(1, yn):
        column = column + t2_in[e - 1].astype(F32)
    v = dot_nn(arrange_2, column.reshape((2 * deep + 1) * ROWS, width).astype(BF16)).astype(BF16)
    v_own[...] = v.reshape(xn, ROWS, width)
    v_copies = [send(v_own.at[d], v_in.at[d - 1], x_peers[d - 1]) for d in x_order]

    arrived(far_halos)
    for copy in near:
        copy.wait_recv()
    from_neighbour(0)
    from_neighbour(1)

    for copy in stat_y:
        copy.wait_recv()
    joined, summed, dotted = join([st_y[...]] + [st_yin[e - 1] for e in range(1, yn)])
    lse = row_of(joined + jnp.log(summed))
    ratio = row_of(dotted / summed)
    line = iota((4 * ROWS, count), 0)
    line_key = jnp.where(line < 3 * ROWS, line & (ROWS - 1), beyond + (line & 3))
    kind = jnp.where(line < 3 * ROWS, line >> 4, (line >> 2) & 3)
    found = jnp.where(line_key == key_r, 1.0, 0.0)
    found = found * jnp.where(kind == 2, -ratio, jnp.where(kind == 3, 0.0, 1.0))
    column = jnp.zeros((4 * ROWS, width), F32)
    for d in range(xn):
        pair = st_x[0:2, :] if d == 0 else st_xin[d - 1, 0:2, :]
        fall = row_of(jnp.exp(pair - joined) / summed)
        factor = jnp.sum(found * fall, axis=1, keepdims=True)
        f_scr[d] = jnp.broadcast_to(factor, (4 * ROWS, width))

    for copy in t1_copies:
        copy.wait_recv()
    for d in range(xn):
        mine = t1_own[0] if d == 0 else t1_in[d - 1]
        column = column + mine.astype(F32).reshape(4 * ROWS, width) * f_scr[d]
    upper = column.astype(BF16)
    lower = (column - upper.astype(F32)).astype(BF16)
    u = (dot_nn(arrange_1, upper) + dot_nn(arrange_1, lower)).astype(BF16)
    u_own[...] = u.reshape(yn, ROWS, width)
    u_copies = [send(u_own.at[e], u_in.at[e - 1], y_peers[e - 1]) for e in y_order]

    w = jnp.exp(sg_scr[...] - lse)
    dvown[...] += dot_nn(w.astype(BF16), glob[3])
    dkown[...] = (dkown[...] + dot_nn((w * (gw_scr[...] - ratio)).astype(BF16), glob[0])) * scale
    keep(dkown, dk_out)
    keep(dvown, dv_out)

    for copy in v_copies:
        copy.wait_recv()
    late = v_own[0].astype(F32)
    for d in range(1, xn):
        late = late + v_in[d - 1].astype(F32)
    for copy in u_copies:
        copy.wait_recv()
    early = u_own[0].astype(F32)
    for e in range(1, yn):
        early = early + u_in[e - 1].astype(F32)
    for part in range(2):
        r_scr[part * ROWS : part * ROWS + 8, :] = early[part * 8 : part * 8 + 8]
        r_scr[part * ROWS + 8 : part * ROWS + 16, :] = late[part * 8 : part * 8 + 8]
    keep(r_scr, r_out)

    for copy in stores:
        copy.wait()
    for copy in copies:
        copy.wait_send()
    for copy, there in halos:
        pl.when(there)(copy.wait_send)


def finish(scale, o_ref, dq_in, dk_in, dv_in, hot_ref, flag_ref, r_ref, out_ref, dq_ref, dk_ref, dv_ref, total):
    tok = o_ref.shape[0]
    total[...] = jnp.zeros_like(total)
    total[0 : 2 * ROWS, :] = r_ref[...]
    upper = total[...].astype(BF16)
    lower = (total[...] - upper.astype(F32)).astype(BF16)
    hot = hot_ref[...].astype(F32)
    lane_array = (iota((tok, TILE), 1) >> 2) & 3

    def placed(a):
        mine = jnp.where(lane_array == a, hot, 0.0).astype(BF16)
        return dot_nn(mine, upper) + dot_nn(mine, lower)

    out_ref[...] = jnp.where(flag_ref[...] > 0.5, placed(0), o_ref[...]).astype(BF16)
    dq_ref[...] = dq_in[...] + placed(1) * scale
    dk_ref[...] = dk_in[...] + placed(2) * scale
    dv_ref[...] = dv_in[...] + placed(3)


def shards(n, query_rows, key_rows, value_rows, out_grad, global_pos):
    tok, _, width = query_rows.shape
    count = global_pos.shape[0]
    yn = 4
    xn = n // (2 * yn)
    deep = xn * SLOTS // ROWS
    window = tok + 2 * HALF
    span = TILE + 2 * HALF
    copies = 4 * (xn - 1) + 4 * (yn - 1) + 20
    vmem = pl.BlockSpec(memory_space=pltpu.VMEM)
    anywhere = pl.BlockSpec(memory_space=pl.ANY)
    flat = [x.reshape(tok, width) for x in (query_rows, key_rows, value_rows, out_grad)]
    rows_f32 = jax.ShapeDtypeStruct((tok, width), F32)
    middle = pl.pallas_call(
        functools.partial(kernel, (n, yn, xn, tok, count, width)),
        name="sparse_attention",
        out_shape=(rows_f32,) * 4
        + (
            jax.ShapeDtypeStruct((tok, TILE), BF16),
            rows_f32,
            jax.ShapeDtypeStruct((2 * ROWS, width), F32),
        ),
        in_specs=[pl.BlockSpec(memory_space=pltpu.HBM)] * 5,
        out_specs=(anywhere,) * 7,
        scratch_shapes=[
            pltpu.VMEM((1, count), I32),
            pltpu.VMEM((window, width), BF16),
            pltpu.VMEM((window, width), BF16),
            pltpu.VMEM((window, width), BF16),
            pltpu.VMEM((window, width), BF16),
            pltpu.VMEM((tok, width), BF16),
            pltpu.VMEM((1, window), F32),
            pltpu.VMEM((tok, width), F32),
            pltpu.VMEM((2, ROWS, width), BF16),
            pltpu.VMEM((xn, 2, ROWS, width), BF16),
            pltpu.VMEM((2, yn, xn + 1, ROWS, width), BF16),
            pltpu.VMEM((2, 4, count, yn * (xn + 1) * ROWS), BF16),
            pltpu.VMEM((4, count, width), F32),
            pltpu.VMEM((4, count, width), BF16),
            pltpu.VMEM((tok, span), F32),
            pltpu.VMEM((tok, width), F32),
            pltpu.VMEM((tok, span), F32),
            pltpu.VMEM((tok, width), F32),
            pltpu.VMEM((tok, width), F32),
            pltpu.VMEM((tok, width), F32),
            pltpu.VMEM((tok, width), F32),
            pltpu.VMEM((tok, count), F32),
            pltpu.VMEM((tok, count), F32),
            pltpu.VMEM((8, TILE), F32),
            pltpu.VMEM((8, TILE), F32),
            pltpu.VMEM((8, TILE), F32),
            pltpu.VMEM((xn - 1, 8, TILE), F32),
            pltpu.VMEM((8, TILE), F32),
            pltpu.VMEM((yn - 1, 8, TILE), F32),
            pltpu.VMEM((tok, width), F32),
            pltpu.VMEM((tok, width), F32),
            pltpu.VMEM((2, 2 * xn * yn * SLOTS, count), BF16),
            pltpu.VMEM((ROWS, count), F32),
            pltpu.VMEM((tok, TILE), BF16),
            pltpu.VMEM((2, 3 * xn + 1, ROWS, width), BF16),
            pltpu.VMEM((3 * xn + 1, ROWS, width), BF16),
            pltpu.VMEM((xn, 4, ROWS, width), BF16),
            pltpu.VMEM((xn - 1, 4, ROWS, width), BF16),
            pltpu.VMEM((2, 2 * deep * yn + 1, ROWS, width), BF16),
            pltpu.VMEM((2 * deep * yn + 1, ROWS, width), BF16),
            pltpu.VMEM((yn, 2 * deep + 1, ROWS, width), BF16),
            pltpu.VMEM((yn - 1, 2 * deep + 1, ROWS, width), BF16),
            pltpu.VMEM((xn, 4 * ROWS, width), F32),
            pltpu.VMEM((yn, ROWS, width), BF16),
            pltpu.VMEM((yn - 1, ROWS, width), BF16),
            pltpu.VMEM((xn, ROWS, width), BF16),
            pltpu.VMEM((xn - 1, ROWS, width), BF16),
            pltpu.VMEM((2 * ROWS, width), F32),
            pltpu.VMEM((8, TILE), F32),
            pltpu.VMEM((2, 8, TILE), F32),
            pltpu.SemaphoreType.DMA((copies,)),
            pltpu.SemaphoreType.DMA((copies,)),
            pltpu.SemaphoreType.DMA((8,)),
            pltpu.SemaphoreType.DMA((8,)),
            pltpu.SemaphoreType.DMA((5,)),
            pltpu.SemaphoreType.DMA((7,)),
        ],
        compiler_params=pltpu.CompilerParams(
            collective_id=0, has_side_effects=True, vmem_limit_bytes=24 << 20
        ),
    )(*[pltpu.with_memory_space_constraint(x, pltpu.HBM) for x in (global_pos.reshape(1, count), *flat)])
    results = pl.pallas_call(
        functools.partial(finish, width**-0.5),
        name="place_global_rows",
        out_shape=(jax.ShapeDtypeStruct((tok, width), BF16),) + (rows_f32,) * 3,
        in_specs=[vmem] * 7,
        out_specs=(vmem,) * 4,
        scratch_shapes=[pltpu.VMEM((TILE, width), F32)],
        compiler_params=pltpu.CompilerParams(vmem_limit_bytes=8 << 20),
    )(*middle)
    return tuple(x.reshape(tok, 1, width) for x in results)


def solution(mesh):
    rows = P("ctx", "head", None)
    return jax.shard_map(
        functools.partial(shards, mesh.shape["ctx"]),
        mesh=mesh,
        in_specs=(rows,) * 4 + (P(),),
        out_specs=(rows,) * 4,
        check_vma=False,
    )
```
